256 devices in a mesh: spec: 4 (over x), wave: 64 (over y, z, core).
Axes of the slice: x: 4, y: 4, z: 8, core: 2. Of those that a mesh axis runs over, the one named last changes fastest.
Arguments:
- pixels: float32 [8, 8, 3200, 500], P(None, 'spec', 'wave')
- ivar: float32 [8, 8, 3200, 500], P(None, 'spec', 'wave'), may hold values from 0.25 to 4
- mask: int32 [8, 8, 3200, 500], P(None, 'spec', 'wave'), may hold values 0 or 1
- psf_left: float32 [8, 8, 3200, 500], P(None, 'spec', 'wave'), may hold values from 0.1 to 0.45
- psf_right: float32 [8, 8, 3200, 500], P(None, 'spec', 'wave'), may hold values from 0.1 to 0.45
- sky_index: int32 [8, 40], P('spec'), may hold values from 0 to 499, as said below
Outputs:
- cleaned: float32 [8, 8, 3200, 500], P(None, 'spec', 'wave')
- sky_model: float32 [8, 3200], P(None, 'wave')
The draws below stay inside these ranges and needn't reach their ends.
Inputs may be any that keep to these rules, and one draw needn't show every extreme that they name: `sky_index`: each row names 40 different fibres.
All inputs are finite; a program needn't handle non-finite values. No bound on the sum of `mask` on one device may be relied on, other than what follows from the above.
Results may differ from the reference program's by a relative error of at most 0.0002.
Values sent between devices are 32-bit elements; how exact they have to be, the bound alone decides.
A program may use at most 128 MiB of HBM per device.

```python
import math
import jax
import jax.numpy as jnp
from jax import lax

F = 500
PW = 50
NSKY = 40
EXPO = 8
SPECS = 8
NW = 3200


def draw_pixels(key, part):
    key_sky, key_thru, key_tilt, key_noise = jax.random.split(key, 4)
    sky_level = jnp.exp(jax.random.uniform(key_sky, (EXPO, 1, NW, 1), jnp.float32, jnp.log(0.5), jnp.log(4.0)))
    through = 1.0 + 0.3 * jax.random.normal(key_thru, (EXPO, SPECS, 1, F), jnp.float32)
    tilt = 0.2 * jax.random.normal(key_tilt, (EXPO, SPECS, 1, F), jnp.float32)
    position = 2.0 * jnp.arange(NW).astype(jnp.float32) / max(NW - 1, 1) - 1.0
    noise = jax.random.normal(key_noise, (EXPO, SPECS, NW, F), jnp.float32)
    return sky_level * (through + tilt * position[None, None, :, None]) + noise


def draw_sky_index(key, part):
    keys = jax.random.split(jax.random.fold_in(key, 7), SPECS)
    chosen = jax.vmap(lambda single: jax.random.permutation(single, F)[:NSKY])(keys)
    return chosen.astype(jnp.int32)


def with_ends(entries, own_key, smallest, largest):
    longest = entries.shape.index(max(entries.shape))
    spots = []
    for shift in (0, 1):
        where = [jax.random.randint(jax.random.fold_in(own_key, axis), (), 0, length) for axis, length in enumerate(entries.shape)]
        where[longest] = (where[longest] + shift) % entries.shape[longest]
        spots.append(tuple(where))
    return entries.at[spots[0]].set(smallest).at[spots[1]].set(largest)


def block_scale(rng, dims, cuts, smallest, largest):
    def one(dim, parts):
        heights = jax.random.uniform(jax.random.fold_in(jax.random.fold_in(rng, 6), dim), (parts,), jnp.float32, smallest / len(cuts), largest / len(cuts))
        return jnp.repeat(jnp.exp(heights), dims[dim] // parts).reshape((-1,) + (1,) * (len(dims) - dim - 1))

    level = one(*cuts[0])
    for cut in cuts[1:]:
        level = level * one(*cut)
    return level


def setup_inputs(seed: int = 0) -> dict:
    key_of = jax.random.split(jax.random.key(seed), 7)
    pixels = draw_pixels(jax.random.fold_in(key_of[6], 71), 0)
    ivar = jnp.clip(jnp.exp(math.log(4.0) - 2.7725887 * jax.random.uniform(key_of[1], (EXPO, SPECS, NW, F), jnp.float32) ** block_scale(key_of[1], (EXPO, SPECS, NW, F), ((1, 4), (2, 64)), -0.2, 0.2)), 0.25, 4.0)
    mask = with_ends((jax.random.randint(key_of[2], (EXPO, SPECS, NW, F), 0, 16) < 1).astype(jnp.int32), jax.random.fold_in(key_of[2], 1), 0, 1)
    psf_left = jnp.clip(0.1 + 0.35 * jax.random.uniform(key_of[3], (EXPO, SPECS, NW, F), jnp.float32) ** block_scale(key_of[3], (EXPO, SPECS, NW, F), ((1, 4), (2, 64)), -0.2, 0.2), 0.1, 0.45)
    psf_right = jnp.clip(0.1 + 0.35 * jax.random.uniform(key_of[4], (EXPO, SPECS, NW, F), jnp.float32) ** block_scale(key_of[4], (EXPO, SPECS, NW, F), ((1, 4), (2, 64)), -0.2, 0.2), 0.1, 0.45)
    sky_index = draw_sky_index(jax.random.fold_in(key_of[6], 71), 0)
    return {"pixels": pixels, "ivar": ivar, "mask": mask, "psf_left": psf_left, "psf_right": psf_right, "sky_index": sky_index}


REG = 0.05
RIDGE = 1.0

def shift_up(values):
    return jnp.concatenate([values[1:], jnp.zeros_like(values[:1])], axis=0)

def shift_down(values):
    return jnp.concatenate([jnp.zeros_like(values[:1]), values[:-1]], axis=0)

def band_solve(pixel_rows, weight, left, right):
    diag_main = weight + shift_up(weight * left * left) + shift_down(weight * right * right) + REG
    first_off = weight * right + shift_up(weight * left)
    second_off = shift_up(weight * left * right)
    rhs_rows = weight * pixel_rows + shift_up(weight * left * pixel_rows) + shift_down(weight * right * pixel_rows)
    prev_one = shift_down(first_off)
    prev_two = shift_down(shift_down(second_off))
    length = diag_main.shape[0]
    unit_fill = jnp.ones_like(diag_main[0])
    zero_fill = jnp.zeros_like(diag_main[0])
    pivots, lowers, farther, forward = ([], [], [], [])
    pivot_last, pivot_before = (unit_fill, unit_fill)
    lower_last, forward_last, forward_before = (zero_fill, zero_fill, zero_fill)
    for step_row in range(length):
        far_term = prev_two[step_row] / pivot_before
        lower_term = (prev_one[step_row] - far_term * lower_last) / pivot_last
        pivot_now = jnp.sqrt(diag_main[step_row] - lower_term * lower_term - far_term * far_term)
        forward_now = (rhs_rows[step_row] - lower_term * forward_last - far_term * forward_before) / pivot_now
        pivots.append(pivot_now)
        lowers.append(lower_term)
        farther.append(far_term)
        forward.append(forward_now)
        pivot_before, pivot_last = (pivot_last, pivot_now)
        lower_last = lower_term
        forward_before, forward_last = (forward_last, forward_now)
    solved = [None] * length
    next_one, next_two = (zero_fill, zero_fill)
    for step_row in reversed(range(length)):
        lower_next = lowers[step_row + 1] if step_row + 1 < length else zero_fill
        far_next = farther[step_row + 2] if step_row + 2 < length else zero_fill
        result_now = (forward[step_row] - lower_next * next_one - far_next * next_two) / pivots[step_row]
        solved[step_row] = result_now
        next_two, next_one = (next_one, result_now)
    return (jnp.stack(solved), diag_main)

def extract_rows(extended, patch_count):
    span = PW + 8
    pieces = [extended[..., start * PW:start * PW + span, :] for start in range(patch_count)]
    picked = jnp.moveaxis(jnp.stack(pieces), -2, 0)
    solved, diag_main = band_solve(picked[:, :, 0], picked[:, :, 1], picked[:, :, 2], picked[:, :, 3])
    outputs = []
    for field in (solved, diag_main):
        kept = field[4:4 + PW]
        kept = jnp.moveaxis(jnp.moveaxis(kept, 0, -2), 0, -3)
        outputs.append(kept.reshape(kept.shape[:-3] + (patch_count * PW, kept.shape[-1])))
    return (outputs[0], outputs[1])

def reference(pixels, ivar, mask, psf_left, psf_right, sky_index):
    weight = ivar * (1.0 - mask.astype(jnp.float32))
    stacked = jnp.stack([pixels, weight, psf_left, psf_right])
    padded = jnp.pad(stacked, ((0, 0), (0, 0), (0, 0), (4, 4), (0, 0)))
    padded = jnp.moveaxis(padded, 1, 0)
    patch_count = NW // PW
    flux, precision = lax.map(lambda single: extract_rows(single, patch_count), padded)
    is_sky = lax.optimization_barrier(jnp.sum((sky_index[:, :, None] == jnp.arange(F)[None, None, :]).astype(jnp.float32), axis=1))
    numer = jnp.einsum('eswf,sf->ew', precision * flux, is_sky, precision=lax.Precision.HIGHEST)
    denom = jnp.einsum('eswf,sf->ew', precision, is_sky, precision=lax.Precision.HIGHEST)
    sky_model = numer / denom
    position = 2.0 * jnp.arange(NW).astype(jnp.float32) / (NW - 1) - 1.0
    square = sky_model * sky_model
    moment_zero = lax.optimization_barrier(jnp.sum(square, axis=1))
    moment_one = lax.optimization_barrier(jnp.sum(square * position, axis=1))
    moment_two = lax.optimization_barrier(jnp.sum(square * position * position, axis=1))
    first_sum = jnp.einsum('eswf,ew->esf', flux, sky_model, precision=lax.Precision.HIGHEST)
    second_sum = jnp.einsum('eswf,ew->esf', flux, sky_model * position, precision=lax.Precision.HIGHEST)
    upper_left = (moment_zero + RIDGE)[:, None, None]
    lower_right = (moment_two + RIDGE)[:, None, None]
    cross = moment_one[:, None, None]
    determinant = upper_left * lower_right - cross * cross
    slope_a = (lower_right * first_sum - cross * second_sum) / determinant
    slope_b = (upper_left * second_sum - cross * first_sum) / determinant
    fitted = (slope_a[:, :, None, :] + slope_b[:, :, None, :] * position[None, None, :, None]) * sky_model[:, None, :, None]
    cleaned = flux - fitted
    return (cleaned, sky_model)
```

```python
import jax
import jax.numpy as jnp
from jax import lax
from jax.experimental import pallas as pl
from jax.experimental.pallas import tpu as pltpu
from jax.sharding import PartitionSpec as P

F = 500
PADDED = 512
EXPO = 8


REG = 0.05
RIDGE = 1.0


def extended_2(cells, sides, width):
    for axis, dim in sides:
        count = lax.axis_size(axis)
        ends = count - 1
        head = lax.slice_in_dim(cells, 0, width, axis=dim)
        tail = lax.slice_in_dim(cells, cells.shape[dim] - width, cells.shape[dim], axis=dim)
        cells = jnp.concatenate(
            [
                lax.ppermute(tail, axis, [(i, (i + 1) % count) for i in range(ends)]),
                cells,
                lax.ppermute(head, axis, [((i + 1) % count, i) for i in range(ends)]),
            ],
            axis=dim,
        )
    return cells


MESH = pl.DeviceIdType.MESH
ROWS = 4
COLS = 8
CORES = 2
PLANE = ROWS * CORES


def spec_kernel(mine, total, inbox, send_sem, recv_sem):
    me = lax.axis_index("spec")
    count = lax.axis_size("spec")
    barrier = pltpu.get_barrier_semaphore()
    peers = [lax.rem(me + d, count) for d in range(1, count)]
    for peer in peers:
        pl.semaphore_signal(barrier, inc=1, device_id={"spec": peer}, device_id_type=MESH)
    pl.semaphore_wait(barrier, count - 1)
    copies = []
    for d, peer in enumerate(peers, 1):
        copies.append(
            pltpu.make_async_remote_copy(
                src_ref=mine,
                dst_ref=inbox.at[count - 1 - d],
                send_sem=send_sem.at[d - 1],
                recv_sem=recv_sem.at[count - 1 - d],
                device_id={"spec": peer},
                device_id_type=MESH,
            )
        )
        copies[-1].start()
    for copy in copies:
        copy.wait()
    total[...] = mine[...] + inbox[0] + inbox[1] + inbox[2]


def spec_sum(mine):
    count = lax.axis_size("spec")
    return pl.pallas_call(
        spec_kernel,
        out_shape=jax.ShapeDtypeStruct(mine.shape, mine.dtype),
        in_specs=[pl.BlockSpec(memory_space=pltpu.VMEM)],
        out_specs=pl.BlockSpec(memory_space=pltpu.VMEM),
        scratch_shapes=[
            pltpu.VMEM((count - 1,) + mine.shape, mine.dtype),
            pltpu.SemaphoreType.DMA((count - 1,)),
            pltpu.SemaphoreType.DMA((count - 1,)),
        ],
        compiler_params=pltpu.CompilerParams(collective_id=1, has_side_effects=True),
        name="spec_sum",
    )(mine)


def wave_kernel(mine, total, box_a, box_b, part, whole, send_a, send_b, send_c, recv_a, recv_b, recv_c):
    me = lax.axis_index("wave")
    core = lax.rem(me, CORES)
    col = lax.rem(lax.div(me, CORES), COLS)
    row = lax.div(me, CORES * COLS)
    mem = row * CORES + core
    wide = mine.shape[0] // PLANE

    def plane_peer(d):
        other = lax.rem(mem + d, PLANE)
        return other, (lax.div(other, CORES) * COLS + col) * CORES + lax.rem(other, CORES)

    def line_peer(d):
        return (row * COLS + lax.rem(col + d, COLS)) * CORES + core

    barrier = pltpu.get_barrier_semaphore()
    for d in range(1, PLANE):
        pl.semaphore_signal(barrier, inc=1, device_id={"wave": plane_peer(d)[1]}, device_id_type=MESH)
    for d in range(1, COLS):
        pl.semaphore_signal(barrier, inc=1, device_id={"wave": line_peer(d)}, device_id_type=MESH)
    pl.semaphore_wait(barrier, PLANE - 1 + COLS - 1)

    first, second, third = [], [], []
    for d in range(1, PLANE):
        other, where = plane_peer(d)
        first.append(
            pltpu.make_async_remote_copy(
                src_ref=mine.at[pl.ds(other * wide, wide)],
                dst_ref=box_a.at[PLANE - 1 - d],
                send_sem=send_a.at[d - 1],
                recv_sem=recv_a.at[PLANE - 1 - d],
                device_id={"wave": where},
                device_id_type=MESH,
            )
        )
        first[-1].start()
    for copy in first:
        copy.wait_recv()
    acc = mine[pl.ds(mem * wide, wide)]
    for d in range(PLANE - 1):
        acc = acc + box_a[d]
    part[...] = acc
    for d in range(1, COLS):
        second.append(
            pltpu.make_async_remote_copy(
                src_ref=part,
                dst_ref=box_b.at[COLS - 1 - d],
                send_sem=send_b.at[d - 1],
                recv_sem=recv_b.at[COLS - 1 - d],
                device_id={"wave": line_peer(d)},
                device_id_type=MESH,
            )
        )
        second[-1].start()
    for copy in second:
        copy.wait_recv()
    acc = part[...]
    for d in range(COLS - 1):
        acc = acc + box_b[d]
    whole[...] = acc
    total[pl.ds(mem * wide, wide)] = acc
    for d in range(1, PLANE):
        third.append(
            pltpu.make_async_remote_copy(
                src_ref=whole,
                dst_ref=total.at[pl.ds(mem * wide, wide)],
                send_sem=send_c.at[d - 1],
                recv_sem=recv_c.at[PLANE - 1 - d],
                device_id={"wave": plane_peer(d)[1]},
                device_id_type=MESH,
            )
        )
        third[-1].start()
    for copy in third:
        copy.wait_recv()
    for copy in first + second + third:
        copy.wait_send()


def wave_sum(mine):
    wide = mine.shape[0] // PLANE
    piece = (wide,) + mine.shape[1:]
    sems = [pltpu.SemaphoreType.DMA((PLANE - 1,)), pltpu.SemaphoreType.DMA((COLS - 1,)), pltpu.SemaphoreType.DMA((PLANE - 1,))]
    return pl.pallas_call(
        wave_kernel,
        out_shape=jax.ShapeDtypeStruct(mine.shape, mine.dtype),
        in_specs=[pl.BlockSpec(memory_space=pltpu.VMEM)],
        out_specs=pl.BlockSpec(memory_space=pltpu.VMEM),
        scratch_shapes=[
            pltpu.VMEM((PLANE - 1,) + piece, mine.dtype),
            pltpu.VMEM((COLS - 1,) + piece, mine.dtype),
            pltpu.VMEM(piece, mine.dtype),
            pltpu.VMEM(piece, mine.dtype),
        ]
        + sems
        + sems,
        compiler_params=pltpu.CompilerParams(collective_id=2, has_side_effects=True),
        name="wave_sum",
    )(mine)


def shift_up(values):
    return jnp.concatenate([values[1:], jnp.zeros_like(values[:1])], axis=0)


def shift_down(values):
    return jnp.concatenate([jnp.zeros_like(values[:1]), values[:-1]], axis=0)


def band_terms(pixel_rows, weight, left, right):
    diag_main = weight + shift_up(weight * left * left) + shift_down(weight * right * right) + REG
    first_off = weight * right + shift_up(weight * left)
    second_off = shift_up(weight * left * right)
    rhs_rows = (
        weight * pixel_rows
        + shift_up(weight * left * pixel_rows)
        + shift_down(weight * right * pixel_rows)
    )
    return (diag_main, first_off, second_off, rhs_rows)


def band_factor(diag_main, first_off, second_off):
    length = diag_main.shape[0]
    unit_fill = jnp.ones_like(diag_main[0])
    zero_fill = jnp.zeros_like(diag_main[0])
    pivots, lowers, farther = ([], [], [])
    pivot_last, pivot_before, lower_last = (unit_fill, unit_fill, zero_fill)
    for step_row in range(length):
        prev_one = first_off[step_row - 1] if step_row >= 1 else zero_fill
        prev_two = second_off[step_row - 2] if step_row >= 2 else zero_fill
        far_term = prev_two / pivot_before
        lower_term = (prev_one - far_term * lower_last) / pivot_last
        pivot_now = jnp.sqrt(diag_main[step_row] - lower_term * lower_term - far_term * far_term)
        pivots.append(pivot_now)
        lowers.append(lower_term)
        farther.append(far_term)
        pivot_before, pivot_last = (pivot_last, pivot_now)
        lower_last = lower_term
    return (pivots, lowers, farther)


def band_substitute(factors, rhs_rows):
    pivots, lowers, farther = factors
    length = len(pivots)
    zero_fill = jnp.zeros_like(rhs_rows[0])
    forward = []
    forward_last, forward_before = (zero_fill, zero_fill)
    for step_row in range(length):
        forward_now = (
            rhs_rows[step_row]
            - lowers[step_row] * forward_last
            - farther[step_row] * forward_before
        ) / pivots[step_row]
        forward.append(forward_now)
        forward_before, forward_last = (forward_last, forward_now)
    solved = [None] * length
    next_one, next_two = (zero_fill, zero_fill)
    for step_row in reversed(range(length)):
        result_now = forward[step_row]
        if step_row + 1 < length:
            result_now = result_now - lowers[step_row + 1] * next_one
        if step_row + 2 < length:
            result_now = result_now - farther[step_row + 2] * next_two
        result_now = result_now / pivots[step_row]
        solved[step_row] = result_now
        next_two, next_one = (next_one, result_now)
    return jnp.stack(solved)


def band_solve(pixel_rows, weight, left, right):
    diag_main, first_off, second_off, rhs_rows = band_terms(pixel_rows, weight, left, right)
    factors = band_factor(diag_main, first_off, second_off)
    return (band_substitute(factors, rhs_rows), diag_main)


def local(pixels, ivar, mask, psf_left, psf_right, sky_index):
    weight = ivar * (1.0 - mask.astype(jnp.float32))
    stacked = jnp.stack([pixels, weight, psf_left, psf_right])
    rows_here = pixels.shape[2]
    extended = extended_2(stacked, (("wave", 3),), 4)
    full_rows = jnp.moveaxis(extended, 3, 1)
    solved_all, diag_main = band_solve(full_rows[0], full_rows[1], full_rows[2], full_rows[3])
    solved = solved_all[4 : 4 + rows_here]
    diag_kept = diag_main[4 : 4 + rows_here]
    flux = jnp.moveaxis(solved, 0, 2)
    precision = jnp.moveaxis(diag_kept, 0, 2)
    is_sky = jnp.sum(
        (sky_index[:, :, None] == jnp.arange(F)[None, None, :]).astype(jnp.float32), axis=1
    )
    numer = jnp.einsum("eswf,sf->ew", precision * flux, is_sky, precision=lax.Precision.HIGHEST)
    denom = jnp.einsum("eswf,sf->ew", precision, is_sky, precision=lax.Precision.HIGHEST)
    both = spec_sum(jnp.stack([numer, denom]))
    numer, denom = both[0], both[1]
    sky_model = numer / denom
    total_rows = rows_here * lax.axis_size("wave")
    offsets = lax.axis_index("wave") * rows_here + jnp.arange(rows_here)
    position = 2.0 * offsets.astype(jnp.float32) / (total_rows - 1) - 1.0
    square = sky_model * sky_model
    moments = jnp.stack(
        [
            jnp.sum(square, axis=1),
            jnp.sum(square * position, axis=1),
            jnp.sum(square * position * position, axis=1),
        ],
        axis=1,
    )
    first_sum = jnp.einsum("eswf,ew->esf", flux, sky_model, precision=lax.Precision.HIGHEST)
    second_sum = jnp.einsum(
        "eswf,ew->esf", flux, sky_model * position, precision=lax.Precision.HIGHEST
    )
    fibre_sums = jnp.stack([first_sum, second_sum])
    tail = jnp.zeros((2, EXPO, 2, PADDED - F), jnp.float32).at[0, :, 0, :3].set(moments)
    packed = jnp.concatenate([fibre_sums, tail], axis=3)
    packed = wave_sum(packed.reshape(2 * EXPO, 2, PADDED)).reshape(2, EXPO, 2, PADDED)
    moments, fibre_sums = packed[0, :, 0, F : F + 3], packed[..., :F]
    upper_left = (moments[:, 0] + RIDGE)[:, None, None]
    lower_right = (moments[:, 2] + RIDGE)[:, None, None]
    cross = moments[:, 1][:, None, None]
    determinant = upper_left * lower_right - cross * cross
    slope_a = (lower_right * fibre_sums[0] - cross * fibre_sums[1]) / determinant
    slope_b = (upper_left * fibre_sums[1] - cross * fibre_sums[0]) / determinant
    fitted = (
        slope_a[:, :, None, :] + slope_b[:, :, None, :] * position[None, None, :, None]
    ) * sky_model[:, None, :, None]
    cleaned = flux - fitted
    return (cleaned, sky_model)


def solution(mesh):
    in_specs = (
        P(None, "spec", "wave", None),
        P(None, "spec", "wave", None),
        P(None, "spec", "wave", None),
        P(None, "spec", "wave", None),
        P(None, "spec", "wave", None),
        P("spec", None),
    )
    out_specs = (P(None, "spec", "wave", None), P(None, "wave"))
    return jax.shard_map(local, mesh=mesh, in_specs=in_specs, out_specs=out_specs, check_vma=False)
```

```python
import jax
import jax.numpy as jnp
from jax import lax
from jax.experimental import pallas as pl
from jax.experimental.pallas import tpu as pltpu
from jax.sharding import PartitionSpec as P

F = 500
WIDE = 512
EXPO = 8
PAIR = 2
ROWS = 50
EDGE = 4
REG = 0.05
RIDGE = 1.0
MESH = pl.DeviceIdType.MESH

LINE = 8
CORES = 2
PLANE = 8
GROUP = 4
PARTS = 6
LOAD = 2 * WIDE + 128
FAR_FIRST = (4, 3, 5, 2, 6, 1, 7)

f32 = jnp.float32


def absorb(front, weight, outer, inner, pixel):
    a, b, d, ra, rb = front
    w_outer, w_inner, w_pixel = weight * outer, weight * inner, weight * pixel
    outer_square, inner_square = w_outer * outer, w_inner * inner
    a = a + outer_square + REG
    b = b + w_outer
    far = w_outer * inner
    d = d + weight
    ra = ra + outer * w_pixel
    rb = rb + w_pixel
    inverse = 1.0 / a
    near_factor, far_factor, start = b * inverse, far * inverse, ra * inverse
    front = (
        d - near_factor * b,
        w_inner - near_factor * far,
        inner_square - far_factor * far,
        rb - b * start,
        inner * w_pixel - far * start,
    )
    return front, (near_factor, far_factor, start), outer_square, inner_square


def main_kernel(
    px_hbm, iv_hbm, mk_hbm, lf_hbm, rt_hbm, sky_ref,
    flux, slope_ref, model_ref,
    px, iv, mk, lf, rt, near, far, start, prec,
    out_edge, in_edge, sums, boxes, model_s, load, box_a, part, box_b, piece,
    load_sem, edge_send, edge_recv, spec_send, spec_recv, smem_sem,
    a_send, a_recv, b_send, b_recv, c_send, c_recv,
):
    me = lax.axis_index("wave")
    count = lax.axis_size("wave")
    spec = lax.axis_index("spec")
    specs = lax.axis_size("spec")
    core = lax.rem(me, CORES)
    col = lax.rem(lax.div(me, CORES), LINE)
    row = lax.div(me, CORES * LINE)
    mem = row * CORES + core

    def plane_peer(d):
        other = lax.rem(mem + d, PLANE)
        return other, (lax.div(other, CORES) * LINE + col) * CORES + lax.rem(other, CORES)

    def line_peer(d):
        return (row * LINE + lax.rem(col + d, LINE)) * CORES + core

    following = lax.rem(me + 1, count)
    preceding = lax.rem(me + count - 1, count)

    def send(src, dst, send_sem, recv_sem, where):
        return pltpu.make_async_remote_copy(
            src_ref=src, dst_ref=dst, send_sem=send_sem, recv_sem=recv_sem, device_id=where, device_id_type=MESH
        )

    hbm = (iv_hbm, mk_hbm, lf_hbm, rt_hbm, px_hbm)
    vmem = (iv, mk, lf, rt, px)
    spans = (pl.ds(ROWS - EDGE, EDGE), pl.ds(0, EDGE), pl.ds(EDGE, ROWS - 2 * EDGE))
    loads = [
        [pltpu.make_async_copy(h.at[:, span], v.at[:, span], load_sem.at[i, j]) for j, (h, v) in enumerate(zip(hbm, vmem))]
        for i, span in enumerate(spans)
    ]
    for group in loads:
        for copy in group:
            copy.start()

    barrier = pltpu.get_barrier_semaphore()
    peers = [{"wave": following}, {"wave": preceding}]
    peers += [{"spec": lax.rem(spec + d, specs)} for d in range(1, specs)]
    peers += [{"wave": line_peer(d)} for d in FAR_FIRST]
    peers += [{"wave": plane_peer(d)[1]} for d in FAR_FIRST]
    for peer in peers:
        pl.semaphore_signal(barrier, inc=1, device_id=peer, device_id_type=MESH)

    def weight_of(es, n):
        return iv[es, n] * (1.0 - mk[es, n].astype(f32))

    def reduce_edge(side, rows, outer, inner):
        for g in range(EXPO // GROUP):
            es = pl.ds(g * GROUP, GROUP)
            first = rows[0]
            weight = weight_of(es, first)
            w_inner, w_pixel = weight * inner[es, first], weight * px[es, first]
            front = (weight, w_inner, w_inner * inner[es, first], w_pixel, inner[es, first] * w_pixel)
            inner_square = None
            for n in rows[1:]:
                front, _, _, inner_square = absorb(front, weight_of(es, n), outer[es, n], inner[es, n], px[es, n])
            for i, value in enumerate(front + (inner_square,)):
                out_edge[side, g, i] = value

    for copy in loads[0]:
        copy.wait()
    reduce_edge(0, tuple(range(ROWS - EDGE, ROWS)), lf, rt)
    for copy in loads[1]:
        copy.wait()
    reduce_edge(1, tuple(range(EDGE - 1, -1, -1)), rt, lf)

    pl.semaphore_wait(barrier, len(peers))
    edges = []
    for g in range(EXPO // GROUP):
        for side, where in ((0, following), (1, preceding)):
            copy = send(
                out_edge.at[side, g], in_edge.at[side, g], edge_send.at[side, g], edge_recv.at[side, g], {"wave": where}
            )
            copy.start()
            edges.append(copy)
    for copy in loads[2]:
        copy.wait()

    no_before = me == 0
    no_after = me == count - 1
    for g in range(EXPO // GROUP):
        es = pl.ds(g * GROUP, GROUP)
        edges[2 * g].wait_recv()
        a, b, d, ra, rb, last_square = (jnp.where(no_before, 0.0, in_edge[0, g, i]) for i in range(PARTS))

        def forward(n, carry, es=es):
            front, partial, last_square = carry
            weight = weight_of(es, n)
            front, factors, outer_square, inner_square = absorb(front, weight, lf[es, n], rt[es, n], px[es, n])
            prec[es, n] = partial + outer_square
            near[es, n], far[es, n], start[es, n] = factors
            return front, weight + last_square + REG, inner_square

        front, partial, _ = lax.fori_loop(
            0, ROWS, forward, ((a, b, d, ra, rb), jnp.zeros_like(a), last_square), unroll=5
        )
        edges[2 * g + 1].wait_recv()
        a2, b2, d2, ra2, rb2, next_square = (jnp.where(no_after, 0.0, in_edge[1, g, i]) for i in range(PARTS))
        a, b, d, ra, rb = front
        prec[es, ROWS] = partial + next_square
        b = b + b2
        inverse = 1.0 / (a + d2 + REG)
        factor, base = b * inverse, (ra + rb2) * inverse
        beyond = (rb + ra2 - b * base) / (d + a2 + REG - factor * b)
        edge_flux = base - factor * beyond
        flux[es, ROWS - 1] = edge_flux

        def backward(i, carry, es=es):
            next_one, next_two = carry
            n = ROWS - 1 - i
            value = start[es, n] - near[es, n] * next_one - far[es, n] * next_two
            flux[es, n - 1] = value
            return value, next_one

        lax.fori_loop(0, ROWS - 1, backward, (edge_flux, beyond), unroll=7)

    is_sky = sky_ref[...][None]
    lane16 = lax.broadcasted_iota(jnp.int32, (EXPO * PAIR, 128), 1)

    def fold(value):
        return jnp.sum(value.reshape(EXPO * PAIR, F), axis=1, keepdims=True)

    def sky_row(n, carry):
        top, bottom = carry
        share = prec[:, n + 1] * is_sky
        scaled = share * flux[:, n]
        return jnp.where(lane16 == n, fold(scaled), top), jnp.where(lane16 == n, fold(share), bottom)

    zero16 = jnp.zeros((EXPO * PAIR, 128), f32)
    top, bottom = lax.fori_loop(0, ROWS, sky_row, (zero16, zero16), unroll=10)
    sums[0] = top.reshape(EXPO, PAIR, 128).sum(1)
    sums[1] = bottom.reshape(EXPO, PAIR, 128).sum(1)
    sky_copies = []
    for d in range(1, specs):
        copy = send(
            sums, boxes.at[specs - 1 - d], spec_send.at[d - 1], spec_recv.at[specs - 1 - d], {"spec": lax.rem(spec + d, specs)}
        )
        copy.start()
        sky_copies.append(copy)
    for copy in sky_copies:
        copy.wait_recv()
    held = [sums[...]] + [boxes[k] for k in range(specs - 1)]
    total = None
    for s in range(specs):
        place = lax.rem(s - spec + specs, specs)
        term = held[0]
        for k in range(1, specs):
            term = jnp.where(place == k, held[k], term)
        total = term if total is None else total + term
    lane = lax.broadcasted_iota(jnp.int32, (EXPO, 128), 1)
    used = lane < ROWS
    model_ref[...] = jnp.where(used, total[0], 0.0) / jnp.where(used, total[1], 1.0)
    to_scalar = pltpu.make_async_copy(model_ref, model_s, smem_sem)
    to_scalar.start()
    to_scalar.wait()

    scale = 2.0 / (count * ROWS - 1)
    base_row = me * ROWS
    lane2 = lax.broadcasted_iota(jnp.int32, (PAIR, 128), 1)

    def regress(n, carry):
        first, second, moment = carry
        place = (base_row + n).astype(f32) * scale - 1.0
        powers = jnp.where(lane2 == 0, 1.0, jnp.where(lane2 == 1, place, place * place))
        first, second, moment = list(first), list(second), list(moment)
        for e in range(EXPO):
            sky = model_s[e, n]
            term = flux[e, n] * sky
            first[e] = first[e] + term
            second[e] = second[e] + term * place
            moment[e] = moment[e] + powers * (sky * sky)
        return tuple(first), tuple(second), tuple(moment)

    zero = jnp.zeros((PAIR, F), f32)
    first, second, moment = lax.fori_loop(
        0, ROWS, regress, ((zero,) * EXPO, (zero,) * EXPO, (jnp.zeros((PAIR, 128), f32),) * EXPO), unroll=2
    )
    for e in range(EXPO):
        load[e, :, 0:F] = first[e]
        load[e, :, WIDE : WIDE + F] = second[e]
        load[e, :, 2 * WIDE : LOAD] = moment[e]

    for d in FAR_FIRST:
        other, where = plane_peer(d)
        send(load.at[other], box_a.at[PLANE - 1 - d], a_send, a_recv, {"wave": where}).start()
    whole_a = send(box_a, box_a, a_send, a_recv, {"wave": following})
    whole_a.wait_recv()
    acc = load[mem]
    for k in range(PLANE - 1):
        acc = acc + box_a[k]
    part[...] = acc
    for d in FAR_FIRST:
        send(part, box_b.at[LINE - 1 - d], b_send, b_recv, {"wave": line_peer(d)}).start()
    whole_b = send(box_b, box_b, b_send, b_recv, {"wave": following})
    whole_b.wait_recv()
    for k in range(LINE - 1):
        acc = acc + box_b[k]
    first_sum, second_sum, powers_sum = acc[:, :WIDE], acc[:, WIDE : 2 * WIDE], acc[:, 2 * WIDE : LOAD]

    def pick(i):
        return jnp.sum(jnp.where(lane2 == i, powers_sum, 0.0), axis=1, keepdims=True)

    upper, cross, lower = pick(0) + RIDGE, pick(1), pick(2) + RIDGE
    inverse = 1.0 / (upper * lower - cross * cross)
    piece[0] = (lower * first_sum - cross * second_sum) * inverse
    piece[1] = (upper * second_sum - cross * first_sum) * inverse
    slope_ref[mem] = piece[...]
    for d in FAR_FIRST:
        send(piece, slope_ref.at[mem], c_send, c_recv, {"wave": plane_peer(d)[1]}).start()
    whole_c = send(slope_ref.at[pl.ds(0, PLANE - 1)], slope_ref.at[pl.ds(0, PLANE - 1)], c_send, c_recv, {"wave": following})
    whole_c.wait_recv()
    for copy in edges + sky_copies:
        copy.wait_send()
    whole_a.wait_send()
    whole_b.wait_send()
    whole_c.wait_send()


def local(pixels, ivar, mask, psf_left, psf_right, sky_index):
    is_sky = jnp.sum((sky_index[:, :, None] == jnp.arange(F)[None, None, :]).astype(f32), axis=1)
    turned = [jnp.transpose(v, (0, 2, 1, 3)) for v in (pixels, ivar, mask, psf_left, psf_right)]
    field = (EXPO, ROWS, PAIR, F)
    specs = lax.axis_size("spec")
    hbm, vmem = pl.BlockSpec(memory_space=pltpu.HBM), pl.BlockSpec(memory_space=pltpu.VMEM)
    dma = pltpu.SemaphoreType.DMA
    groups = EXPO // GROUP
    edge = (2, groups, PARTS, GROUP, PAIR, F)
    flux, slopes, model = pl.pallas_call(
        main_kernel,
        out_shape=(
            jax.ShapeDtypeStruct(field, f32),
            jax.ShapeDtypeStruct((EXPO, 2, PAIR, WIDE), f32),
            jax.ShapeDtypeStruct((EXPO, 128), f32),
        ),
        in_specs=[hbm] * 5 + [vmem],
        out_specs=(vmem, vmem, vmem),
        scratch_shapes=[
            pltpu.VMEM(field, f32),
            pltpu.VMEM(field, f32),
            pltpu.VMEM(field, jnp.int32),
            pltpu.VMEM(field, f32),
            pltpu.VMEM(field, f32),
            pltpu.VMEM(field, f32),
            pltpu.VMEM(field, f32),
            pltpu.VMEM(field, f32),
            pltpu.VMEM((EXPO, ROWS + 1, PAIR, F), f32),
            pltpu.VMEM(edge, f32),
            pltpu.VMEM(edge, f32),
            pltpu.VMEM((2, EXPO, 128), f32),
            pltpu.VMEM((specs - 1, 2, EXPO, 128), f32),
            pltpu.SMEM((EXPO, 128), f32),
            pltpu.VMEM((EXPO, PAIR, LOAD), f32),
            pltpu.VMEM((PLANE - 1, PAIR, LOAD), f32),
            pltpu.VMEM((PAIR, LOAD), f32),
            pltpu.VMEM((LINE - 1, PAIR, LOAD), f32),
            pltpu.VMEM((2, PAIR, WIDE), f32),
            dma((3, 5)),
            dma((2, groups)),
            dma((2, groups)),
            dma((specs - 1,)),
            dma((specs - 1,)),
            dma,
            dma,
            dma,
            dma,
            dma,
            dma,
            dma,
        ],
        compiler_params=pltpu.CompilerParams(
            collective_id=0, has_side_effects=True, vmem_limit_bytes=40 * 1024 * 1024
        ),
        name="deconvolve",
    )(*turned, is_sky)
    model = model[:, :ROWS]
    total_rows = ROWS * lax.axis_size("wave")
    offsets = lax.axis_index("wave") * ROWS + jnp.arange(ROWS)
    position = 2.0 * offsets.astype(f32) / (total_rows - 1) - 1.0
    slope_a, slope_b = slopes[:, None, 0, :, :F], slopes[:, None, 1, :, :F]
    fitted = (slope_a + slope_b * position[None, :, None, None]) * model[:, :, None, None]
    return (jnp.transpose(flux - fitted, (0, 2, 1, 3)), model)


def solution(mesh):
    in_specs = (
        P(None, "spec", "wave", None),
        P(None, "spec", "wave", None),
        P(None, "spec", "wave", None),
        P(None, "spec", "wave", None),
        P(None, "spec", "wave", None),
        P("spec", None),
    )
    out_specs = (P(None, "spec", "wave", None), P(None, "wave"))
    return jax.shard_map(local, mesh=mesh, in_specs=in_specs, out_specs=out_specs, check_vma=False)
```

```python
import jax
import jax.numpy as jnp
from jax import lax
from jax.experimental import pallas as pl
from jax.experimental.pallas import tpu as pltpu
from jax.sharding import PartitionSpec as P

F = 500
WIDE = 512
EXPO = 8
PAIR = 2
ROWS = 50
EDGE = 4
REG = 0.05
RIDGE = 1.0
MESH = pl.DeviceIdType.MESH

LINE = 8
CORES = 2
PLANE = 8
GROUP = 4
PARTS = 6
LOAD = 2 * WIDE + 128
FAR_FIRST = (4, 3, 5, 2, 6, 1, 7)

f32 = jnp.float32


def absorb(front, weight, outer, inner, pixel):
    a, b, d, ra, rb = front
    w_outer, w_inner, w_pixel = weight * outer, weight * inner, weight * pixel
    outer_square, inner_square = w_outer * outer, w_inner * inner
    a = a + outer_square + REG
    b = b + w_outer
    far = w_outer * inner
    d = d + weight
    ra = ra + outer * w_pixel
    rb = rb + w_pixel
    inverse = 1.0 / a
    near_factor, far_factor, start = b * inverse, far * inverse, ra * inverse
    front = (
        d - near_factor * b,
        w_inner - near_factor * far,
        inner_square - far_factor * far,
        rb - b * start,
        inner * w_pixel - far * start,
    )
    return front, (near_factor, far_factor, start), outer_square, inner_square


def main_kernel(
    px_hbm, iv_hbm, mk_hbm, lf_hbm, rt_hbm, index_hbm,
    flux, model_ref,
    px, iv, mk, lf, rt, index, near, far, start, prec,
    out_edge, in_edge, sums, boxes, model_s, load, box_a, part, box_b, piece, slope_ref,
    load_sem, index_sem, edge_send, edge_recv, spec_send, spec_recv, smem_sem,
    a_send, a_recv, b_send, b_recv, c_send, c_recv,
):
    me = lax.axis_index("wave")
    count = lax.axis_size("wave")
    spec = lax.axis_index("spec")
    specs = lax.axis_size("spec")
    core = lax.rem(me, CORES)
    col = lax.rem(lax.div(me, CORES), LINE)
    row = lax.div(me, CORES * LINE)
    mem = row * CORES + core

    def plane_peer(d):
        other = lax.rem(mem + d, PLANE)
        return other, (lax.div(other, CORES) * LINE + col) * CORES + lax.rem(other, CORES)

    def line_peer(d):
        return (row * LINE + lax.rem(col + d, LINE)) * CORES + core

    following = lax.rem(me + 1, count)
    preceding = lax.rem(me + count - 1, count)

    def send(src, dst, send_sem, recv_sem, where):
        return pltpu.make_async_remote_copy(
            src_ref=src, dst_ref=dst, send_sem=send_sem, recv_sem=recv_sem, device_id=where, device_id_type=MESH
        )

    hbm = (iv_hbm, mk_hbm, lf_hbm, rt_hbm, px_hbm)
    vmem = (iv, mk, lf, rt, px)
    spans = (pl.ds(ROWS - EDGE, EDGE), pl.ds(0, EDGE), pl.ds(EDGE, ROWS - 2 * EDGE))
    loads = [
        [pltpu.make_async_copy(h.at[:, span], v.at[:, span], load_sem.at[i, j]) for j, (h, v) in enumerate(zip(hbm, vmem))]
        for i, span in enumerate(spans)
    ]
    for group in loads:
        for copy in group:
            copy.start()

    index_copy = pltpu.make_async_copy(index_hbm, index, index_sem)
    index_copy.start()

    barrier = pltpu.get_barrier_semaphore()
    peers = [{"wave": following}, {"wave": preceding}]
    peers += [{"spec": lax.rem(spec + d, specs)} for d in range(1, specs)]
    peers += [{"wave": line_peer(d)} for d in FAR_FIRST]
    peers += [{"wave": plane_peer(d)[1]} for d in FAR_FIRST]
    for peer in peers:
        pl.semaphore_signal(barrier, inc=1, device_id=peer, device_id_type=MESH)

    def weight_of(es, n):
        return iv[es, n] * (1.0 - mk[es, n].astype(f32))

    def reduce_edge(side, rows, outer, inner):
        for g in range(EXPO // GROUP):
            es = pl.ds(g * GROUP, GROUP)
            first = rows[0]
            weight = weight_of(es, first)
            w_inner, w_pixel = weight * inner[es, first], weight * px[es, first]
            front = (weight, w_inner, w_inner * inner[es, first], w_pixel, inner[es, first] * w_pixel)
            inner_square = None
            for n in rows[1:]:
                front, _, _, inner_square = absorb(front, weight_of(es, n), outer[es, n], inner[es, n], px[es, n])
            for i, value in enumerate(front + (inner_square,)):
                out_edge[side, g, i] = value

    for copy in loads[0]:
        copy.wait()
    reduce_edge(0, tuple(range(ROWS - EDGE, ROWS)), lf, rt)
    for copy in loads[1]:
        copy.wait()
    reduce_edge(1, tuple(range(EDGE - 1, -1, -1)), rt, lf)

    pl.semaphore_wait(barrier, len(peers))
    edges = []
    for g in range(EXPO // GROUP):
        for side, where in ((0, following), (1, preceding)):
            copy = send(
                out_edge.at[side, g], in_edge.at[side, g], edge_send.at[side, g], edge_recv.at[side, g], {"wave": where}
            )
            copy.start()
            edges.append(copy)
    fibre = lax.broadcasted_iota(jnp.int32, (PAIR, F), 1)
    index_copy.wait()
    listed = index[...]
    is_sky = jnp.zeros((PAIR, F), f32)
    for j in range(listed.shape[1]):
        is_sky = is_sky + jnp.where(listed[:, j : j + 1] == fibre, 1.0, 0.0)
    is_sky = is_sky[None]
    for copy in loads[2]:
        copy.wait()

    no_before = me == 0
    no_after = me == count - 1
    for g in range(EXPO // GROUP):
        es = pl.ds(g * GROUP, GROUP)
        edges[2 * g].wait_recv()
        a, b, d, ra, rb, last_square = (jnp.where(no_before, 0.0, in_edge[0, g, i]) for i in range(PARTS))

        def forward(n, carry, es=es):
            front, partial, last_square = carry
            weight = weight_of(es, n)
            front, factors, outer_square, inner_square = absorb(front, weight, lf[es, n], rt[es, n], px[es, n])
            prec[es, n] = partial + outer_square
            near[es, n], far[es, n], start[es, n] = factors
            return front, weight + last_square + REG, inner_square

        front, partial, _ = lax.fori_loop(
            0, ROWS, forward, ((a, b, d, ra, rb), jnp.zeros_like(a), last_square), unroll=5
        )
        edges[2 * g + 1].wait_recv()
        a2, b2, d2, ra2, rb2, next_square = (jnp.where(no_after, 0.0, in_edge[1, g, i]) for i in range(PARTS))
        a, b, d, ra, rb = front
        prec[es, ROWS] = partial + next_square
        b = b + b2
        inverse = 1.0 / (a + d2 + REG)
        factor, base = b * inverse, (ra + rb2) * inverse
        beyond = (rb + ra2 - b * base) / (d + a2 + REG - factor * b)
        edge_flux = base - factor * beyond
        flux[es, ROWS - 1] = edge_flux

        def backward(i, carry, es=es):
            next_one, next_two = carry
            n = ROWS - 1 - i
            value = start[es, n] - near[es, n] * next_one - far[es, n] * next_two
            flux[es, n - 1] = value
            return value, next_one

        lax.fori_loop(0, ROWS - 1, backward, (edge_flux, beyond), unroll=7)

    lane16 = lax.broadcasted_iota(jnp.int32, (EXPO * PAIR, 128), 1)

    def fold(value):
        return jnp.sum(value.reshape(EXPO * PAIR, F), axis=1, keepdims=True)

    def sky_row(n, carry):
        top, bottom = carry
        share = prec[:, n + 1] * is_sky
        scaled = share * flux[:, n]
        return jnp.where(lane16 == n, fold(scaled), top), jnp.where(lane16 == n, fold(share), bottom)

    zero16 = jnp.zeros((EXPO * PAIR, 128), f32)
    top, bottom = lax.fori_loop(0, ROWS, sky_row, (zero16, zero16), unroll=10)
    sums[0] = top.reshape(EXPO, PAIR, 128).sum(1)
    sums[1] = bottom.reshape(EXPO, PAIR, 128).sum(1)
    sky_copies = []
    for d in range(1, specs):
        copy = send(
            sums, boxes.at[specs - 1 - d], spec_send.at[d - 1], spec_recv.at[specs - 1 - d], {"spec": lax.rem(spec + d, specs)}
        )
        copy.start()
        sky_copies.append(copy)
    for copy in sky_copies:
        copy.wait_recv()
    held = [sums[...]] + [boxes[k] for k in range(specs - 1)]
    total = None
    for s in range(specs):
        place = lax.rem(s - spec + specs, specs)
        term = held[0]
        for k in range(1, specs):
            term = jnp.where(place == k, held[k], term)
        total = term if total is None else total + term
    lane = lax.broadcasted_iota(jnp.int32, (EXPO, 128), 1)
    used = lane < ROWS
    model_ref[...] = jnp.where(used, total[0], 0.0) / jnp.where(used, total[1], 1.0)
    to_scalar = pltpu.make_async_copy(model_ref, model_s, smem_sem)
    to_scalar.start()
    to_scalar.wait()

    scale = 2.0 / (count * ROWS - 1)
    base_row = me * ROWS
    lane2 = lax.broadcasted_iota(jnp.int32, (PAIR, 128), 1)

    def regress(n, carry):
        first, second, moment = carry
        place = (base_row + n).astype(f32) * scale - 1.0
        powers = jnp.where(lane2 == 0, 1.0, jnp.where(lane2 == 1, place, place * place))
        first, second, moment = list(first), list(second), list(moment)
        for e in range(EXPO):
            sky = model_s[e, n]
            term = flux[e, n] * sky
            first[e] = first[e] + term
            second[e] = second[e] + term * place
            moment[e] = moment[e] + powers * (sky * sky)
        return tuple(first), tuple(second), tuple(moment)

    zero = jnp.zeros((PAIR, F), f32)
    first, second, moment = lax.fori_loop(
        0, ROWS, regress, ((zero,) * EXPO, (zero,) * EXPO, (jnp.zeros((PAIR, 128), f32),) * EXPO), unroll=2
    )
    for e in range(EXPO):
        load[e, :, 0:F] = first[e]
        load[e, :, WIDE : WIDE + F] = second[e]
        load[e, :, 2 * WIDE : LOAD] = moment[e]

    for d in FAR_FIRST:
        other, where = plane_peer(d)
        send(load.at[other], box_a.at[PLANE - 1 - d], a_send, a_recv, {"wave": where}).start()
    whole_a = send(box_a, box_a, a_send, a_recv, {"wave": following})
    whole_a.wait_recv()
    acc = load[mem]
    for k in range(PLANE - 1):
        acc = acc + box_a[k]
    part[...] = acc
    for d in FAR_FIRST:
        send(part, box_b.at[LINE - 1 - d], b_send, b_recv, {"wave": line_peer(d)}).start()
    whole_b = send(box_b, box_b, b_send, b_recv, {"wave": following})
    whole_b.wait_recv()
    for k in range(LINE - 1):
        acc = acc + box_b[k]
    first_sum, second_sum, powers_sum = acc[:, :WIDE], acc[:, WIDE : 2 * WIDE], acc[:, 2 * WIDE : LOAD]

    def pick(i):
        return jnp.sum(jnp.where(lane2 == i, powers_sum, 0.0), axis=1, keepdims=True)

    upper, cross, lower = pick(0) + RIDGE, pick(1), pick(2) + RIDGE
    inverse = 1.0 / (upper * lower - cross * cross)
    piece[0] = (lower * first_sum - cross * second_sum) * inverse
    piece[1] = (upper * second_sum - cross * first_sum) * inverse
    slope_ref[mem] = piece[...]
    for d in FAR_FIRST:
        send(piece, slope_ref.at[mem], c_send, c_recv, {"wave": plane_peer(d)[1]}).start()
    whole_c = send(slope_ref.at[pl.ds(0, PLANE - 1)], slope_ref.at[pl.ds(0, PLANE - 1)], c_send, c_recv, {"wave": following})
    whole_c.wait_recv()

    def clean(n, carry):
        place = (base_row + n).astype(f32) * scale - 1.0
        for e in range(EXPO):
            fitted = slope_ref[e, 0, :, 0:F] + slope_ref[e, 1, :, 0:F] * place
            flux[e, n] = flux[e, n] - fitted * model_s[e, n]
        return carry

    lax.fori_loop(0, ROWS, clean, 0, unroll=2)
    for copy in edges + sky_copies:
        copy.wait_send()
    whole_a.wait_send()
    whole_b.wait_send()
    whole_c.wait_send()


def store_kernel(cleaned, model, cleaned_out, model_out, model_rows, sems):
    main = pltpu.make_async_copy(cleaned, cleaned_out, sems.at[0])
    main.start()
    model_rows[...] = model[:, 0:ROWS]
    small = pltpu.make_async_copy(model_rows, model_out, sems.at[1])
    small.start()
    small.wait()
    main.wait()


def local(pixels, ivar, mask, psf_left, psf_right, sky_index):
    turned = [jnp.transpose(v, (0, 2, 1, 3)) for v in (pixels, ivar, mask, psf_left, psf_right)]
    field = (EXPO, ROWS, PAIR, F)
    specs = lax.axis_size("spec")
    hbm, vmem = pl.BlockSpec(memory_space=pltpu.HBM), pl.BlockSpec(memory_space=pltpu.VMEM)
    dma = pltpu.SemaphoreType.DMA
    groups = EXPO // GROUP
    edge = (2, groups, PARTS, GROUP, PAIR, F)
    cleaned, model = pl.pallas_call(
        main_kernel,
        out_shape=(
            jax.ShapeDtypeStruct(field, f32),
            jax.ShapeDtypeStruct((EXPO, 128), f32),
        ),
        in_specs=[hbm] * 6,
        out_specs=(vmem, vmem),
        scratch_shapes=[
            pltpu.VMEM(field, f32),
            pltpu.VMEM(field, f32),
            pltpu.VMEM(field, jnp.int32),
            pltpu.VMEM(field, f32),
            pltpu.VMEM(field, f32),
            pltpu.VMEM(sky_index.shape, jnp.int32),
            pltpu.VMEM(field, f32),
            pltpu.VMEM(field, f32),
            pltpu.VMEM(field, f32),
            pltpu.VMEM((EXPO, ROWS + 1, PAIR, F), f32),
            pltpu.VMEM(edge, f32),
            pltpu.VMEM(edge, f32),
            pltpu.VMEM((2, EXPO, 128), f32),
            pltpu.VMEM((specs - 1, 2, EXPO, 128), f32),
            pltpu.SMEM((EXPO, 128), f32),
            pltpu.VMEM((EXPO, PAIR, LOAD), f32),
            pltpu.VMEM((PLANE - 1, PAIR, LOAD), f32),
            pltpu.VMEM((PAIR, LOAD), f32),
            pltpu.VMEM((LINE - 1, PAIR, LOAD), f32),
            pltpu.VMEM((2, PAIR, WIDE), f32),
            pltpu.VMEM((EXPO, 2, PAIR, WIDE), f32),
            dma((3, 5)),
            dma,
            dma((2, groups)),
            dma((2, groups)),
            dma((specs - 1,)),
            dma((specs - 1,)),
            dma,
            dma,
            dma,
            dma,
            dma,
            dma,
            dma,
        ],
        compiler_params=pltpu.CompilerParams(
            collective_id=0, has_side_effects=True, vmem_limit_bytes=54_000_000
        ),
        name="deconvolve",
    )(*turned, sky_index)
    cleaned, model = pl.pallas_call(
        store_kernel,
        out_shape=(jax.ShapeDtypeStruct(field, f32), jax.ShapeDtypeStruct((EXPO, ROWS), f32)),
        in_specs=[vmem, vmem],
        out_specs=(hbm, hbm),
        scratch_shapes=[pltpu.VMEM((EXPO, ROWS), f32), dma((2,))],
        compiler_params=pltpu.CompilerParams(vmem_limit_bytes=54_000_000),
        name="store",
    )(cleaned, model)
    return (jnp.transpose(cleaned, (0, 2, 1, 3)), model)


def solution(mesh):
    in_specs = (
        P(None, "spec", "wave", None),
        P(None, "spec", "wave", None),
        P(None, "spec", "wave", None),
        P(None, "spec", "wave", None),
        P(None, "spec", "wave", None),
        P("spec", None),
    )
    out_specs = (P(None, "spec", "wave", None), P(None, "wave"))
    return jax.shard_map(local, mesh=mesh, in_specs=in_specs, out_specs=out_specs, check_vma=False)
```

```python
import jax
import jax.numpy as jnp
from jax import lax
from jax.experimental import pallas as pl
from jax.experimental.pallas import tpu as pltpu
from jax.sharding import PartitionSpec as P

F = 500
WIDE = 512
EXPO = 8
PAIR = 2
ROWS = 50
EDGE = 4
REG = 0.05
RIDGE = 1.0
MESH = pl.DeviceIdType.MESH

LINE = 8
CORES = 2
PLANE = 8
GROUP = 4
PARTS = 6
LOAD = 2 * WIDE + 128
FAR_FIRST = (4, 3, 5, 2, 6, 1, 7)

f32 = jnp.float32


def absorb(front, weight, outer, inner, pixel):
    a, b, d, ra, rb = front
    w_outer, w_inner, w_pixel = weight * outer, weight * inner, weight * pixel
    outer_square, inner_square = w_outer * outer, w_inner * inner
    a = a + outer_square + REG
    b = b + w_outer
    far = w_outer * inner
    d = d + weight
    ra = ra + outer * w_pixel
    rb = rb + w_pixel
    inverse = 1.0 / a
    near_factor, far_factor, start = b * inverse, far * inverse, ra * inverse
    front = (
        d - near_factor * b,
        w_inner - near_factor * far,
        inner_square - far_factor * far,
        rb - b * start,
        inner * w_pixel - far * start,
    )
    return front, (near_factor, far_factor, start), outer_square, inner_square


def main_kernel(
    px_hbm, iv_hbm, mk_hbm, lf_hbm, rt_hbm, index,
    flux, model_ref,
    px, iv, mk, lf, rt, near, far, start, prec,
    out_edge, in_edge, sums, boxes, model_v, model_s, load, box_a, part, box_b, piece, slope_ref,
    load_sem, edge_send, edge_recv, spec_send, spec_recv, smem_sem,
    a_send, a_recv, b_send, b_recv, c_send, c_recv,
):
    me = lax.axis_index("wave")
    count = lax.axis_size("wave")
    spec = lax.axis_index("spec")
    specs = lax.axis_size("spec")
    core = lax.rem(me, CORES)
    col = lax.rem(lax.div(me, CORES), LINE)
    row = lax.div(me, CORES * LINE)
    mem = row * CORES + core

    def plane_peer(d):
        other = lax.rem(mem + d, PLANE)
        return other, (lax.div(other, CORES) * LINE + col) * CORES + lax.rem(other, CORES)

    def line_peer(d):
        return (row * LINE + lax.rem(col + d, LINE)) * CORES + core

    following = lax.rem(me + 1, count)
    preceding = lax.rem(me + count - 1, count)

    def send(src, dst, send_sem, recv_sem, where):
        return pltpu.make_async_remote_copy(
            src_ref=src, dst_ref=dst, send_sem=send_sem, recv_sem=recv_sem, device_id=where, device_id_type=MESH
        )

    hbm = (iv_hbm, mk_hbm, lf_hbm, rt_hbm, px_hbm)
    vmem = (iv, mk, lf, rt, px)
    spans = (pl.ds(ROWS - EDGE, EDGE), pl.ds(0, EDGE), pl.ds(EDGE, ROWS - 2 * EDGE))
    loads = [
        [pltpu.make_async_copy(h.at[:, span], v.at[:, span], load_sem.at[i, j]) for j, (h, v) in enumerate(zip(hbm, vmem))]
        for i, span in enumerate(spans)
    ]
    barrier = pltpu.get_barrier_semaphore()

    def greet(peers):
        for peer in peers:
            pl.semaphore_signal(barrier, inc=1, device_id=peer, device_id_type=MESH)
        return len(peers)

    greeted = greet([{"wave": line_peer(d)} for d in FAR_FIRST])
    for group in loads[:2]:
        for copy in group:
            copy.start()
    greeted += greet([{"wave": plane_peer(d)[1]} for d in FAR_FIRST])
    greeted += greet([{"spec": lax.rem(spec + d, specs)} for d in range(1, specs)])
    greeted += greet([{"wave": following}, {"wave": preceding}])

    def weight_of(es, n):
        return iv[es, n] * (1.0 - mk[es, n].astype(f32))

    def reduce_edge(side, rows, outer, inner):
        for g in range(EXPO // GROUP):
            es = pl.ds(g * GROUP, GROUP)
            first = rows[0]
            weight = weight_of(es, first)
            w_inner, w_pixel = weight * inner[es, first], weight * px[es, first]
            front = (weight, w_inner, w_inner * inner[es, first], w_pixel, inner[es, first] * w_pixel)
            inner_square = None
            for n in rows[1:]:
                front, _, _, inner_square = absorb(front, weight_of(es, n), outer[es, n], inner[es, n], px[es, n])
            for i, value in enumerate(front + (inner_square,)):
                out_edge[side, g, i] = value

    for copy in loads[0]:
        copy.wait()
    reduce_edge(0, tuple(range(ROWS - EDGE, ROWS)), lf, rt)
    for copy in loads[1]:
        copy.wait()
    reduce_edge(1, tuple(range(EDGE - 1, -1, -1)), rt, lf)

    pl.semaphore_wait(barrier, greeted)
    edges = []
    for g in range(EXPO // GROUP):
        for side, where in ((0, following), (1, preceding)):
            copy = send(
                out_edge.at[side, g], in_edge.at[side, g], edge_send.at[side, g], edge_recv.at[side, g], {"wave": where}
            )
            copy.start()
            edges.append(copy)
    for copy in loads[2]:
        copy.start()
    fibre = lax.broadcasted_iota(jnp.int32, (PAIR, F), 1)
    second_row = lax.broadcasted_iota(jnp.int32, (PAIR, F), 0) == 1
    is_sky = jnp.zeros((PAIR, F), f32)
    for j in range(index.shape[1]):
        is_sky = is_sky + jnp.where(fibre == jnp.where(second_row, index[1, j], index[0, j]), 1.0, 0.0)
    is_sky = is_sky[None]
    for copy in loads[2]:
        copy.wait()

    no_before = me == 0
    no_after = me == count - 1
    lane8 = lax.broadcasted_iota(jnp.int32, (GROUP * PAIR, 128), 1)
    zero8 = jnp.zeros((GROUP * PAIR, 128), f32)

    def fold(value):
        return jnp.sum(value.reshape(GROUP * PAIR, F), axis=1, keepdims=True)

    sky_copies = []
    for g in range(EXPO // GROUP):
        es = pl.ds(g * GROUP, GROUP)
        edges[2 * g].wait_recv()
        a, b, d, ra, rb, last_square = (jnp.where(no_before, 0.0, in_edge[0, g, i]) for i in range(PARTS))

        def forward(n, carry, es=es):
            front, partial, last_square = carry
            weight = weight_of(es, n)
            front, factors, outer_square, inner_square = absorb(front, weight, lf[es, n], rt[es, n], px[es, n])
            prec[es, n] = partial + outer_square
            near[es, n], far[es, n], start[es, n] = factors
            return front, weight + last_square + REG, inner_square

        front, partial, _ = lax.fori_loop(
            0, ROWS, forward, ((a, b, d, ra, rb), jnp.zeros_like(a), last_square), unroll=5
        )
        edges[2 * g + 1].wait_recv()
        a2, b2, d2, ra2, rb2, next_square = (jnp.where(no_after, 0.0, in_edge[1, g, i]) for i in range(PARTS))
        a, b, d, ra, rb = front
        prec[es, ROWS] = partial + next_square
        b = b + b2
        inverse = 1.0 / (a + d2 + REG)
        factor, base = b * inverse, (ra + rb2) * inverse
        beyond = (rb + ra2 - b * base) / (d + a2 + REG - factor * b)
        edge_flux = base - factor * beyond
        flux[es, ROWS - 1] = edge_flux

        def backward(i, carry, es=es):
            next_one, next_two = carry
            n = ROWS - 1 - i
            value = start[es, n] - near[es, n] * next_one - far[es, n] * next_two
            flux[es, n - 1] = value
            return value, next_one

        lax.fori_loop(0, ROWS - 1, backward, (edge_flux, beyond), unroll=7)

        def sky_row(n, carry, es=es):
            top, bottom = carry
            share = prec[es, n + 1] * is_sky
            scaled = share * flux[es, n]
            return jnp.where(lane8 == n, fold(scaled), top), jnp.where(lane8 == n, fold(share), bottom)

        sums[g, 0], sums[g, 1] = lax.fori_loop(0, ROWS, sky_row, (zero8, zero8), unroll=10)
        sky_copies.append(
            [
                send(
                    sums.at[g], boxes.at[g, specs - 1 - d], spec_send.at[g, d - 1], spec_recv.at[g, specs - 1 - d],
                    {"spec": lax.rem(spec + d, specs)},
                )
                for d in range(1, specs)
            ]
        )
        for copy in sky_copies[g]:
            copy.start()

    scale = 2.0 / (count * ROWS - 1)
    base_row = me * ROWS
    lane2 = lax.broadcasted_iota(jnp.int32, (PAIR, 128), 1)
    used = lax.broadcasted_iota(jnp.int32, (GROUP, 128), 1) < ROWS
    zero = jnp.zeros((PAIR, F), f32)
    zero_moment = jnp.zeros((PAIR, 128), f32)
    for g in range(EXPO // GROUP):
        for copy in sky_copies[g]:
            copy.wait_recv()
        held = [sums[g]] + [boxes[g, k] for k in range(specs - 1)]
        total = None
        for s in range(specs):
            place = lax.rem(s - spec + specs, specs)
            term = held[0]
            for k in range(1, specs):
                term = jnp.where(place == k, held[k], term)
            total = term if total is None else total + term
        total = total.reshape(2, GROUP, PAIR, 128).sum(2)
        model = jnp.where(used, total[0], 0.0) / jnp.where(used, total[1], 1.0)
        model_v[g] = model
        to_scalar = pltpu.make_async_copy(model_v.at[g], model_s.at[g], smem_sem)
        to_scalar.start()
        model_ref[g * GROUP : (g + 1) * GROUP] = model
        to_scalar.wait()

        def regress(n, carry, g=g):
            first, second, moment = (list(v) for v in carry)
            place = (base_row + n).astype(f32) * scale - 1.0
            powers = jnp.where(lane2 == 0, 1.0, jnp.where(lane2 == 1, place, place * place))
            for i in range(GROUP):
                sky = model_s[g, i, n]
                term = flux[g * GROUP + i, n] * sky
                first[i] = first[i] + term
                second[i] = second[i] + term * place
                moment[i] = moment[i] + powers * (sky * sky)
            return tuple(first), tuple(second), tuple(moment)

        first, second, moment = lax.fori_loop(
            0, ROWS, regress, ((zero,) * GROUP, (zero,) * GROUP, (zero_moment,) * GROUP), unroll=5
        )
        for i in range(GROUP):
            e = g * GROUP + i
            load[e, :, 0:F] = first[i]
            load[e, :, WIDE : WIDE + F] = second[i]
            load[e, :, 2 * WIDE : LOAD] = moment[i]
        for i in range(GROUP):
            e = g * GROUP + i
            where = ((e // CORES) * LINE + col) * CORES + e % CORES
            slot = lax.rem(mem - e + PLANE, PLANE) - 1

            @pl.when(mem != e)
            def _(e=e, where=where, slot=slot):
                send(load.at[e], box_a.at[slot], a_send, a_recv, {"wave": where}).start()

    whole_a = send(box_a, box_a, a_send, a_recv, {"wave": following})
    whole_a.wait_recv()
    acc = load[mem]
    for k in range(PLANE - 1):
        acc = acc + box_a[k]
    part[...] = acc
    for d in FAR_FIRST:
        send(part, box_b.at[LINE - 1 - d], b_send, b_recv, {"wave": line_peer(d)}).start()
    whole_b = send(box_b, box_b, b_send, b_recv, {"wave": following})
    whole_b.wait_recv()
    for k in range(LINE - 1):
        acc = acc + box_b[k]
    first_sum, second_sum, powers_sum = acc[:, :WIDE], acc[:, WIDE : 2 * WIDE], acc[:, 2 * WIDE : LOAD]

    def pick(i):
        return jnp.sum(jnp.where(lane2 == i, powers_sum, 0.0), axis=1, keepdims=True)

    upper, cross, lower = pick(0) + RIDGE, pick(1), pick(2) + RIDGE
    inverse = 1.0 / (upper * lower - cross * cross)
    piece[0] = (lower * first_sum - cross * second_sum) * inverse
    piece[1] = (upper * second_sum - cross * first_sum) * inverse
    slope_ref[mem] = piece[...]
    for d in FAR_FIRST:
        send(piece, slope_ref.at[mem], c_send, c_recv, {"wave": plane_peer(d)[1]}).start()
    whole_c = send(slope_ref.at[pl.ds(0, PLANE - 1)], slope_ref.at[pl.ds(0, PLANE - 1)], c_send, c_recv, {"wave": following})
    whole_c.wait_recv()

    slope_a = [slope_ref[e, 0, :, 0:F] for e in range(EXPO)]
    slope_b = [slope_ref[e, 1, :, 0:F] for e in range(EXPO)]

    def clean(n, carry):
        place = (base_row + n).astype(f32) * scale - 1.0
        for e in range(EXPO):
            fitted = slope_a[e] + slope_b[e] * place
            flux[e, n] = flux[e, n] - fitted * model_s[e // GROUP, e % GROUP, n]
        return carry

    lax.fori_loop(0, ROWS, clean, 0, unroll=5)
    for copy in edges + sky_copies[0] + sky_copies[1]:
        copy.wait_send()
    whole_a.wait_send()
    whole_b.wait_send()
    whole_c.wait_send()


def store_kernel(cleaned, model, cleaned_out, model_out, model_rows, sems):
    copies = [pltpu.make_async_copy(cleaned.at[e], cleaned_out.at[e], sems.at[e]) for e in range(EXPO)]
    for copy in copies:
        copy.start()
    model_rows[...] = model[:, 0:ROWS]
    copies.append(pltpu.make_async_copy(model_rows, model_out, sems.at[EXPO]))
    copies[-1].start()
    for copy in copies:
        copy.wait()


def local(pixels, ivar, mask, psf_left, psf_right, sky_index):
    turned = [jnp.transpose(v, (0, 2, 1, 3)) for v in (pixels, ivar, mask, psf_left, psf_right)]
    field = (EXPO, ROWS, PAIR, F)
    specs = lax.axis_size("spec")
    hbm, vmem = pl.BlockSpec(memory_space=pltpu.HBM), pl.BlockSpec(memory_space=pltpu.VMEM)
    dma = pltpu.SemaphoreType.DMA
    groups = EXPO // GROUP
    edge = (2, groups, PARTS, GROUP, PAIR, F)
    cleaned, model = pl.pallas_call(
        main_kernel,
        out_shape=(
            jax.ShapeDtypeStruct(field, f32),
            jax.ShapeDtypeStruct((EXPO, 128), f32),
        ),
        in_specs=[hbm] * 5 + [pl.BlockSpec(memory_space=pltpu.SMEM)],
        out_specs=(vmem, vmem),
        scratch_shapes=[
            pltpu.VMEM(field, f32),
            pltpu.VMEM(field, f32),
            pltpu.VMEM(field, jnp.int32),
            pltpu.VMEM(field, f32),
            pltpu.VMEM(field, f32),
            pltpu.VMEM(field, f32),
            pltpu.VMEM(field, f32),
            pltpu.VMEM(field, f32),
            pltpu.VMEM((EXPO, ROWS + 1, PAIR, F), f32),
            pltpu.VMEM(edge, f32),
            pltpu.VMEM(edge, f32),
            pltpu.VMEM((groups, 2, GROUP * PAIR, 128), f32),
            pltpu.VMEM((groups, specs - 1, 2, GROUP * PAIR, 128), f32),
            pltpu.VMEM((groups, GROUP, 128), f32),
            pltpu.SMEM((groups, GROUP, 128), f32),
            pltpu.VMEM((EXPO, PAIR, LOAD), f32),
            pltpu.VMEM((PLANE - 1, PAIR, LOAD), f32),
            pltpu.VMEM((PAIR, LOAD), f32),
            pltpu.VMEM((LINE - 1, PAIR, LOAD), f32),
            pltpu.VMEM((2, PAIR, WIDE), f32),
            pltpu.VMEM((EXPO, 2, PAIR, WIDE), f32),
            dma((3, 5)),
            dma((2, groups)),
            dma((2, groups)),
            dma((groups, specs - 1)),
            dma((groups, specs - 1)),
            dma,
            dma,
            dma,
            dma,
            dma,
            dma,
            dma,
        ],
        compiler_params=pltpu.CompilerParams(
            collective_id=0, has_side_effects=True, vmem_limit_bytes=54_000_000
        ),
        name="deconvolve",
    )(*turned, sky_index)
    cleaned, model = pl.pallas_call(
        store_kernel,
        out_shape=(jax.ShapeDtypeStruct(field, f32), jax.ShapeDtypeStruct((EXPO, ROWS), f32)),
        in_specs=[vmem, vmem],
        out_specs=(hbm, hbm),
        scratch_shapes=[pltpu.VMEM((EXPO, ROWS), f32), dma((EXPO + 1,))],
        compiler_params=pltpu.CompilerParams(vmem_limit_bytes=54_000_000),
        name="store",
    )(cleaned, model)
    return (jnp.transpose(cleaned, (0, 2, 1, 3)), model)


def solution(mesh):
    in_specs = (
        P(None, "spec", "wave", None),
        P(None, "spec", "wave", None),
        P(None, "spec", "wave", None),
        P(None, "spec", "wave", None),
        P(None, "spec", "wave", None),
        P("spec", None),
    )
    out_specs = (P(None, "spec", "wave", None), P(None, "wave"))
    return jax.shard_map(local, mesh=mesh, in_specs=in_specs, out_specs=out_specs, check_vma=False)
```

```python
import jax
import jax.numpy as jnp
from jax import lax
from jax.experimental import pallas as pl
from jax.experimental.pallas import tpu as pltpu
from jax.sharding import PartitionSpec as P

F = 500
WIDE = 512
EXPO = 8
PAIR = 2
ROWS = 50
EDGE = 4
REG = 0.05
RIDGE = 1.0
MESH = pl.DeviceIdType.MESH

LINE = 8
CORES = 2
PLANE = 8
GROUP = 4
PARTS = 6
LOAD = 2 * WIDE + 128
FAR_FIRST = (4, 3, 5, 2, 6, 1, 7)

f32 = jnp.float32


def absorb(front, weight, outer, inner, pixel):
    a, b, d, ra, rb = front
    w_outer, w_inner, w_pixel = weight * outer, weight * inner, weight * pixel
    outer_square, inner_square = w_outer * outer, w_inner * inner
    a = a + outer_square + REG
    b = b + w_outer
    far = w_outer * inner
    d = d + weight
    ra = ra + outer * w_pixel
    rb = rb + w_pixel
    inverse = 1.0 / a
    near_factor, far_factor, start = b * inverse, far * inverse, ra * inverse
    front = (
        d - near_factor * b,
        w_inner - near_factor * far,
        inner_square - far_factor * far,
        rb - b * start,
        inner * w_pixel - far * start,
    )
    return front, (near_factor, far_factor, start), outer_square, inner_square


def main_kernel(
    px_hbm, iv_hbm, mk_hbm, lf_hbm, rt_hbm, index,
    flux, model_ref,
    px, iv, mk, lr, near, far, start, prec,
    out_edge, in_edge, sums, boxes, model_v, model_s, load, box_a, part, box_b, piece, slope_ref,
    load_sem, edge_send, edge_recv, spec_send, spec_recv, smem_sem,
    a_send, a_recv, b_send, b_recv, c_send, c_recv,
):
    me = lax.axis_index("wave")
    count = lax.axis_size("wave")
    spec = lax.axis_index("spec")
    specs = lax.axis_size("spec")
    core = lax.rem(me, CORES)
    col = lax.rem(lax.div(me, CORES), LINE)
    row = lax.div(me, CORES * LINE)
    mem = row * CORES + core

    def plane_peer(d):
        other = lax.rem(mem + d, PLANE)
        return other, (lax.div(other, CORES) * LINE + col) * CORES + lax.rem(other, CORES)

    def line_peer(d):
        return (row * LINE + lax.rem(col + d, LINE)) * CORES + core

    partner = me + 1 - 2 * core
    outside = lax.rem(me + 2 * core - 1 + count, count)

    def send(src, dst, send_sem, recv_sem, where):
        return pltpu.make_async_remote_copy(
            src_ref=src, dst_ref=dst, send_sem=send_sem, recv_sem=recv_sem, device_id=where, device_id_type=MESH
        )

    hbm = (iv_hbm, mk_hbm, lf_hbm, rt_hbm, px_hbm)
    vmem = (iv, mk, lr.at[0], lr.at[1], px)
    spans = (pl.ds(ROWS - EDGE, EDGE), pl.ds(0, EDGE), pl.ds(EDGE, ROWS - 2 * EDGE))
    loads = [
        [pltpu.make_async_copy(h.at[:, span], v.at[:, span], load_sem.at[i, j]) for j, (h, v) in enumerate(zip(hbm, vmem))]
        for i, span in enumerate(spans)
    ]
    barrier = pltpu.get_barrier_semaphore()

    def greet(peers):
        for peer in peers:
            pl.semaphore_signal(barrier, inc=1, device_id=peer, device_id_type=MESH)
        return len(peers)

    greeted = greet([{"wave": line_peer(d)} for d in FAR_FIRST])
    for group in loads[:2]:
        for copy in group:
            copy.start()
    greeted += greet([{"wave": plane_peer(d)[1]} for d in FAR_FIRST])
    greeted += greet([{"spec": lax.rem(spec + d, specs)} for d in range(1, specs)])
    greeted += greet([{"wave": outside}, {"wave": partner}])

    def weight_of(es, n):
        return iv[es, n] * (1.0 - mk[es, n].astype(f32))

    sides = ((46 - 43 * core, 1 - 2 * core, core, partner), (3 + 43 * core, 2 * core - 1, 1 - core, outside))

    def reduce_edge(side, g):
        base, step, outer, _ = sides[side]
        es = pl.ds(g * GROUP, GROUP)
        weight, inner = weight_of(es, base), lr[1 - outer, es, base]
        w_inner, w_pixel = weight * inner, weight * px[es, base]
        front = (weight, w_inner, w_inner * inner, w_pixel, inner * w_pixel)
        for i in range(1, EDGE):
            n = base + step * i
            front, _, _, inner_square = absorb(front, weight_of(es, n), lr[outer, es, n], lr[1 - outer, es, n], px[es, n])
        for i, value in enumerate(front + (inner_square,)):
            out_edge[side, g, i] = value

    for group in loads[:2]:
        for copy in group:
            copy.wait()
    for copy in loads[2]:
        copy.start()
    for g in range(EXPO // GROUP):
        for side in (1, 0):
            reduce_edge(side, g)

    pl.semaphore_wait(barrier, greeted)
    edges = {}
    for g in range(EXPO // GROUP):
        for side in (1, 0):
            copy = send(
                out_edge.at[side, g], in_edge.at[side, g], edge_send.at[side, g], edge_recv.at[side, g],
                {"wave": sides[side][3]},
            )
            copy.start()
            edges[side, g] = copy
    fibre = lax.broadcasted_iota(jnp.int32, (PAIR, F), 1)
    second_row = lax.broadcasted_iota(jnp.int32, (PAIR, F), 0) == 1
    is_sky = jnp.zeros((PAIR, F), f32)
    for j in range(index.shape[1]):
        is_sky = is_sky + jnp.where(fibre == jnp.where(second_row, index[1, j], index[0, j]), 1.0, 0.0)
    is_sky = is_sky[None]
    for copy in loads[2]:
        copy.wait()

    lane8 = lax.broadcasted_iota(jnp.int32, (GROUP * PAIR, 128), 1)
    zero8 = jnp.zeros((GROUP * PAIR, 128), f32)

    def fold(value):
        return jnp.sum(value.reshape(GROUP * PAIR, F), axis=1, keepdims=True)

    first_row, row_step = (ROWS - 1) * (1 - core), 2 * core - 1
    fronts = []
    for g in range(EXPO // GROUP):
        es = pl.ds(g * GROUP, GROUP)
        edges[0, g].wait_recv()
        a, b, d, ra, rb, last_square = (in_edge[0, g, i] for i in range(PARTS))

        def forward(k, carry, es=es):
            front, partial, last_square = carry
            n = first_row + row_step * k
            weight = weight_of(es, n)
            front, factors, outer_square, inner_square = absorb(
                front, weight, lr[1 - core, es, n], lr[core, es, n], px[es, n]
            )
            prec[es, k] = partial + outer_square
            near[es, k], far[es, k], start[es, k] = factors
            return front, weight + last_square + REG, inner_square

        front, partial, _ = lax.fori_loop(
            0, ROWS, forward, ((a, b, d, ra, rb), jnp.zeros_like(a), last_square), unroll=5
        )
        fronts.append((front, partial))

    alone = (me == 0) | (me == count - 1)
    sky_copies = []
    for g in range(EXPO // GROUP):
        es = pl.ds(g * GROUP, GROUP)
        edges[1, g].wait_recv()
        a2, b2, d2, ra2, rb2, next_square = (jnp.where(alone, 0.0, in_edge[1, g, i]) for i in range(PARTS))
        (a, b, d, ra, rb), partial = fronts[g]
        prec[es, ROWS] = partial + next_square
        b = b + b2
        inverse = 1.0 / (a + d2 + REG)
        factor, base = b * inverse, (ra + rb2) * inverse
        beyond = (rb + ra2 - b * base) / (d + a2 + REG - factor * b)
        edge_flux = base - factor * beyond
        flux[es, first_row + row_step * (ROWS - 1)] = edge_flux

        def backward(i, carry, es=es):
            next_one, next_two = carry
            k = ROWS - 1 - i
            value = start[es, k] - near[es, k] * next_one - far[es, k] * next_two
            flux[es, first_row + row_step * (k - 1)] = value
            return value, next_one

        lax.fori_loop(0, ROWS - 1, backward, (edge_flux, beyond), unroll=7)

        def sky_row(k, carry, es=es):
            top, bottom = carry
            n = first_row + row_step * k
            share = prec[es, k + 1] * is_sky
            scaled = share * flux[es, n]
            return jnp.where(lane8 == n, fold(scaled), top), jnp.where(lane8 == n, fold(share), bottom)

        sums[g, 0], sums[g, 1] = lax.fori_loop(0, ROWS, sky_row, (zero8, zero8), unroll=10)
        sky_copies.append(
            [
                send(
                    sums.at[g], boxes.at[g, specs - 1 - d], spec_send.at[g, d - 1], spec_recv.at[g, specs - 1 - d],
                    {"spec": lax.rem(spec + d, specs)},
                )
                for d in range(1, specs)
            ]
        )
        for copy in sky_copies[g]:
            copy.start()

    scale = 2.0 / (count * ROWS - 1)
    base_row = me * ROWS
    lane2 = lax.broadcasted_iota(jnp.int32, (PAIR, 128), 1)
    used = lax.broadcasted_iota(jnp.int32, (GROUP, 128), 1) < ROWS
    zero = jnp.zeros((PAIR, F), f32)
    zero_moment = jnp.zeros((PAIR, 128), f32)
    for g in range(EXPO // GROUP):
        for copy in sky_copies[g]:
            copy.wait_recv()
        held = [sums[g]] + [boxes[g, k] for k in range(specs - 1)]
        total = None
        for s in range(specs):
            place = lax.rem(s - spec + specs, specs)
            term = held[0]
            for k in range(1, specs):
                term = jnp.where(place == k, held[k], term)
            total = term if total is None else total + term
        total = total.reshape(2, GROUP, PAIR, 128).sum(2)
        model = jnp.where(used, total[0], 0.0) / jnp.where(used, total[1], 1.0)
        model_v[g] = model
        to_scalar = pltpu.make_async_copy(model_v.at[g], model_s.at[g], smem_sem)
        to_scalar.start()
        model_ref[g * GROUP : (g + 1) * GROUP] = model
        to_scalar.wait()

        def regress(n, carry, g=g):
            first, second, moment = (list(v) for v in carry)
            place = (base_row + n).astype(f32) * scale - 1.0
            powers = jnp.where(lane2 == 0, 1.0, jnp.where(lane2 == 1, place, place * place))
            for i in range(GROUP):
                sky = model_s[g, i, n]
                term = flux[g * GROUP + i, n] * sky
                first[i] = first[i] + term
                second[i] = second[i] + term * place
                moment[i] = moment[i] + powers * (sky * sky)
            return tuple(first), tuple(second), tuple(moment)

        first, second, moment = lax.fori_loop(
            0, ROWS, regress, ((zero,) * GROUP, (zero,) * GROUP, (zero_moment,) * GROUP), unroll=5
        )
        for i in range(GROUP):
            e = g * GROUP + i
            load[e, :, 0:F] = first[i]
            load[e, :, WIDE : WIDE + F] = second[i]
            load[e, :, 2 * WIDE : LOAD] = moment[i]
        for i in range(GROUP):
            e = g * GROUP + i
            where = ((e // CORES) * LINE + col) * CORES + e % CORES
            slot = lax.rem(mem - e + PLANE, PLANE) - 1

            @pl.when(mem != e)
            def _(e=e, where=where, slot=slot):
                send(load.at[e], box_a.at[slot], a_send, a_recv, {"wave": where}).start()

    whole_a = send(box_a, box_a, a_send, a_recv, {"wave": partner})
    whole_a.wait_recv()
    acc = load[mem]
    for k in range(PLANE - 1):
        acc = acc + box_a[k]
    part[...] = acc
    for d in FAR_FIRST:
        send(part, box_b.at[LINE - 1 - d], b_send, b_recv, {"wave": line_peer(d)}).start()
    whole_b = send(box_b, box_b, b_send, b_recv, {"wave": partner})
    whole_b.wait_recv()
    for k in range(LINE - 1):
        acc = acc + box_b[k]
    first_sum, second_sum, powers_sum = acc[:, :WIDE], acc[:, WIDE : 2 * WIDE], acc[:, 2 * WIDE : LOAD]

    def pick(i):
        return jnp.sum(jnp.where(lane2 == i, powers_sum, 0.0), axis=1, keepdims=True)

    upper, cross, lower = pick(0) + RIDGE, pick(1), pick(2) + RIDGE
    inverse = 1.0 / (upper * lower - cross * cross)
    piece[0] = (lower * first_sum - cross * second_sum) * inverse
    piece[1] = (upper * second_sum - cross * first_sum) * inverse
    slope_ref[mem] = piece[...]
    for d in FAR_FIRST:
        send(piece, slope_ref.at[mem], c_send, c_recv, {"wave": plane_peer(d)[1]}).start()
    whole_c = send(slope_ref.at[pl.ds(0, PLANE - 1)], slope_ref.at[pl.ds(0, PLANE - 1)], c_send, c_recv, {"wave": partner})
    whole_c.wait_recv()

    slope_a = [slope_ref[e, 0, :, 0:F] for e in range(EXPO)]
    slope_b = [slope_ref[e, 1, :, 0:F] for e in range(EXPO)]

    def clean(n, carry):
        place = (base_row + n).astype(f32) * scale - 1.0
        for e in range(EXPO):
            fitted = slope_a[e] + slope_b[e] * place
            flux[e, n] = flux[e, n] - fitted * model_s[e // GROUP, e % GROUP, n]
        return carry

    lax.fori_loop(0, ROWS, clean, 0, unroll=5)
    for copy in list(edges.values()) + sky_copies[0] + sky_copies[1]:
        copy.wait_send()
    whole_a.wait_send()
    whole_b.wait_send()
    whole_c.wait_send()


def store_kernel(cleaned, model, cleaned_out, model_out, model_rows, sems):
    copies = [pltpu.make_async_copy(cleaned.at[e], cleaned_out.at[e], sems.at[e]) for e in range(EXPO)]
    for copy in copies:
        copy.start()
    model_rows[...] = model[:, 0:ROWS]
    copies.append(pltpu.make_async_copy(model_rows, model_out, sems.at[EXPO]))
    copies[-1].start()
    for copy in copies:
        copy.wait()


def local(pixels, ivar, mask, psf_left, psf_right, sky_index):
    turned = [jnp.transpose(v, (0, 2, 1, 3)) for v in (pixels, ivar, mask, psf_left, psf_right)]
    field = (EXPO, ROWS, PAIR, F)
    specs = lax.axis_size("spec")
    hbm, vmem = pl.BlockSpec(memory_space=pltpu.HBM), pl.BlockSpec(memory_space=pltpu.VMEM)
    dma = pltpu.SemaphoreType.DMA
    groups = EXPO // GROUP
    edge = (2, groups, PARTS, GROUP, PAIR, F)
    cleaned, model = pl.pallas_call(
        main_kernel,
        out_shape=(
            jax.ShapeDtypeStruct(field, f32),
            jax.ShapeDtypeStruct((EXPO, 128), f32),
        ),
        in_specs=[hbm] * 5 + [pl.BlockSpec(memory_space=pltpu.SMEM)],
        out_specs=(vmem, vmem),
        scratch_shapes=[
            pltpu.VMEM(field, f32),
            pltpu.VMEM(field, f32),
            pltpu.VMEM(field, jnp.int32),
            pltpu.VMEM((2,) + field, f32),
            pltpu.VMEM(field, f32),
            pltpu.VMEM(field, f32),
            pltpu.VMEM(field, f32),
            pltpu.VMEM((EXPO, ROWS + 1, PAIR, F), f32),
            pltpu.VMEM(edge, f32),
            pltpu.VMEM(edge, f32),
            pltpu.VMEM((groups, 2, GROUP * PAIR, 128), f32),
            pltpu.VMEM((groups, specs - 1, 2, GROUP * PAIR, 128), f32),
            pltpu.VMEM((groups, GROUP, 128), f32),
            pltpu.SMEM((groups, GROUP, 128), f32),
            pltpu.VMEM((EXPO, PAIR, LOAD), f32),
            pltpu.VMEM((PLANE - 1, PAIR, LOAD), f32),
            pltpu.VMEM((PAIR, LOAD), f32),
            pltpu.VMEM((LINE - 1, PAIR, LOAD), f32),
            pltpu.VMEM((2, PAIR, WIDE), f32),
            pltpu.VMEM((EXPO, 2, PAIR, WIDE), f32),
            dma((3, 5)),
            dma((2, groups)),
            dma((2, groups)),
            dma((groups, specs - 1)),
            dma((groups, specs - 1)),
            dma,
            dma,
            dma,
            dma,
            dma,
            dma,
            dma,
        ],
        compiler_params=pltpu.CompilerParams(
            collective_id=0, has_side_effects=True, vmem_limit_bytes=54_000_000
        ),
        name="deconvolve",
    )(*turned, pltpu.with_memory_space_constraint(sky_index, pltpu.HBM))
    cleaned, model = pl.pallas_call(
        store_kernel,
        out_shape=(jax.ShapeDtypeStruct(field, f32), jax.ShapeDtypeStruct((EXPO, ROWS), f32)),
        in_specs=[vmem, vmem],
        out_specs=(hbm, hbm),
        scratch_shapes=[pltpu.VMEM((EXPO, ROWS), f32), dma((EXPO + 1,))],
        compiler_params=pltpu.CompilerParams(vmem_limit_bytes=54_000_000),
        name="store",
    )(cleaned, model)
    return (jnp.transpose(cleaned, (0, 2, 1, 3)), model)


def solution(mesh):
    in_specs = (
        P(None, "spec", "wave", None),
        P(None, "spec", "wave", None),
        P(None, "spec", "wave", None),
        P(None, "spec", "wave", None),
        P(None, "spec", "wave", None),
        P("spec", None),
    )
    out_specs = (P(None, "spec", "wave", None), P(None, "wave"))
    return jax.shard_map(local, mesh=mesh, in_specs=in_specs, out_specs=out_specs, check_vma=False)
```

```python
import jax
import jax.numpy as jnp
from jax import lax
from jax.experimental import pallas as pl
from jax.experimental.pallas import tpu as pltpu
from jax.sharding import PartitionSpec as P

F = 500
WIDE = 512
EXPO = 8
PAIR = 2
ROWS = 50
EDGE = 4
REG = 0.05
RIDGE = 1.0
MESH = pl.DeviceIdType.MESH

LINE = 8
CORES = 2
PLANE = 8
GROUP = 4
PARTS = 6
HALF = WIDE // 2
LOAD = WIDE + 128
LATE = 4
SLICE = EXPO // LATE
FAR_FIRST = (4, 3, 5, 2, 6, 1, 7)

f32 = jnp.float32


def absorb(front, weight, outer, inner, pixel):
    a, b, d, ra, rb = front
    w_outer, w_inner, w_pixel = weight * outer, weight * inner, weight * pixel
    outer_square, inner_square = w_outer * outer, w_inner * inner
    a = a + outer_square + REG
    b = b + w_outer
    far = w_outer * inner
    d = d + weight
    ra = ra + outer * w_pixel
    rb = rb + w_pixel
    inverse = 1.0 / a
    near_factor, far_factor, start = b * inverse, far * inverse, ra * inverse
    front = (
        d - near_factor * b,
        w_inner - near_factor * far,
        inner_square - far_factor * far,
        rb - b * start,
        inner * w_pixel - far * start,
    )
    return front, (near_factor, far_factor, start), outer_square, inner_square


def main_kernel(
    px_hbm, iv_hbm, mk_hbm, lf_hbm, rt_hbm, index,
    flux, model_ref,
    px, iv, mk, lr, near, far, start, prec,
    near_out, near_in, far_out, far_in, sums, boxes, model_v, model_s, load, box_a, part, box_b, piece, gathered, slope_ref,
    load_sem, near_send, near_recv, far_send, far_recv, spec_send, spec_recv, smem_sem,
    a_send, a_recv, b_send, b_recv, c_send, c_recv,
):
    me = lax.axis_index("wave")
    count = lax.axis_size("wave")
    spec = lax.axis_index("spec")
    specs = lax.axis_size("spec")
    core = lax.rem(me, CORES)
    col = lax.rem(lax.div(me, CORES), LINE)
    row = lax.div(me, CORES * LINE)
    mem = row * CORES + core

    def plane_peer(d):
        other = lax.rem(mem + d, PLANE)
        return other, (lax.div(other, CORES) * LINE + col) * CORES + lax.rem(other, CORES)

    def line_peer(d):
        return (row * LINE + lax.rem(col + d, LINE)) * CORES + core

    partner = me + 1 - 2 * core
    outside = lax.rem(me + 2 * core - 1 + count, count)

    def send(src, dst, send_sem, recv_sem, where):
        return pltpu.make_async_remote_copy(
            src_ref=src, dst_ref=dst, send_sem=send_sem, recv_sem=recv_sem, device_id=where, device_id_type=MESH
        )

    hbm = (iv_hbm, mk_hbm, lf_hbm, rt_hbm, px_hbm)
    vmem = (iv, mk, lr.at[0], lr.at[1], px)
    spans = (pl.ds(ROWS - EDGE, EDGE), pl.ds(0, EDGE), pl.ds(EDGE, ROWS - 2 * EDGE))
    loads = [
        [pltpu.make_async_copy(h.at[:, span], v.at[:, span], load_sem.at[i, j]) for j, (h, v) in enumerate(zip(hbm, vmem))]
        for i, span in enumerate(spans)
    ]
    barrier = pltpu.get_barrier_semaphore()

    def greet(peers):
        for peer in peers:
            pl.semaphore_signal(barrier, inc=1, device_id=peer, device_id_type=MESH)
        return len(peers)

    greeted = greet([{"wave": line_peer(d)} for d in FAR_FIRST])
    for group in loads[:2]:
        for copy in group:
            copy.start()
    greeted += greet([{"wave": plane_peer(d)[1]} for d in FAR_FIRST])
    greeted += greet([{"spec": lax.rem(spec + d, specs)} for d in range(1, specs)])
    greeted += greet([{"wave": outside}, {"wave": partner}])

    def weight_of(es, n):
        return iv[es, n] * (1.0 - mk[es, n].astype(f32))

    sides = ((46 - 43 * core, 1 - 2 * core, core, partner), (3 + 43 * core, 2 * core - 1, 1 - core, outside))

    def reduce_edge(side, g, size, out):
        base, step, outer, _ = sides[side]
        es = pl.ds(g * size, size)
        weight, inner = weight_of(es, base), lr[1 - outer, es, base]
        w_inner, w_pixel = weight * inner, weight * px[es, base]
        front = (weight, w_inner, w_inner * inner, w_pixel, inner * w_pixel)
        for i in range(1, EDGE):
            n = base + step * i
            front, _, _, inner_square = absorb(front, weight_of(es, n), lr[outer, es, n], lr[1 - outer, es, n], px[es, n])
        for i, value in enumerate(front + (inner_square,)):
            out[g, i] = value

    for group in loads[:2]:
        for copy in group:
            copy.wait()
    for copy in loads[2]:
        copy.start()
    for g in range(LATE):
        reduce_edge(1, g, SLICE, far_out)
    for g in range(EXPO // GROUP):
        reduce_edge(0, g, GROUP, near_out)

    pl.semaphore_wait(barrier, greeted)
    far_edges = [
        send(far_out.at[g], far_in.at[g], far_send.at[g], far_recv.at[g], {"wave": outside}) for g in range(LATE)
    ]
    near_edges = [
        send(near_out.at[g], near_in.at[g], near_send.at[g], near_recv.at[g], {"wave": partner})
        for g in range(EXPO // GROUP)
    ]
    far_edges[0].start()
    for copy in near_edges:
        copy.start()
    for copy in far_edges[1:]:
        copy.start()
    fibre = lax.broadcasted_iota(jnp.int32, (PAIR, F), 1)
    second_row = lax.broadcasted_iota(jnp.int32, (PAIR, F), 0) == 1
    is_sky = jnp.zeros((PAIR, F), f32)
    for j in range(index.shape[1]):
        is_sky = is_sky + jnp.where(fibre == jnp.where(second_row, index[1, j], index[0, j]), 1.0, 0.0)
    is_sky = is_sky[None]
    for copy in loads[2]:
        copy.wait()

    lane4 = lax.broadcasted_iota(jnp.int32, (SLICE * PAIR, 128), 1)
    zero4 = jnp.zeros((SLICE * PAIR, 128), f32)

    def fold(value):
        return jnp.sum(value.reshape(SLICE * PAIR, F), axis=1, keepdims=True)

    first_row, row_step = (ROWS - 1) * (1 - core), 2 * core - 1
    fronts = []
    for g in range(EXPO // GROUP):
        es = pl.ds(g * GROUP, GROUP)
        near_edges[g].wait_recv()
        a, b, d, ra, rb, last_square = (near_in[g, i] for i in range(PARTS))

        def forward(k, carry, es=es):
            front, partial, last_square = carry
            n = first_row + row_step * k
            weight = weight_of(es, n)
            front, factors, outer_square, inner_square = absorb(
                front, weight, lr[1 - core, es, n], lr[core, es, n], px[es, n]
            )
            prec[es, k] = partial + outer_square
            near[es, k], far[es, k], start[es, k] = factors
            return front, weight + last_square + REG, inner_square

        front, partial, _ = lax.fori_loop(
            0, ROWS, forward, ((a, b, d, ra, rb), jnp.zeros_like(a), last_square), unroll=5
        )
        fronts.append((front, partial))

    alone = (me == 0) | (me == count - 1)
    sky_copies = []
    for q in range(LATE):
        es = pl.ds(q * SLICE, SLICE)
        g, low = divmod(q * SLICE, GROUP)
        far_edges[q].wait_recv()
        a2, b2, d2, ra2, rb2, next_square = (jnp.where(alone, 0.0, far_in[q, i]) for i in range(PARTS))
        (a, b, d, ra, rb), partial = fronts[g]
        a, b, d, ra, rb, partial = (v[low : low + SLICE] for v in (a, b, d, ra, rb, partial))
        prec[es, ROWS] = partial + next_square
        b = b + b2
        inverse = 1.0 / (a + d2 + REG)
        factor, base = b * inverse, (ra + rb2) * inverse
        beyond = (rb + ra2 - b * base) / (d + a2 + REG - factor * b)
        edge_flux = base - factor * beyond

        def sky_row(k, value, top, bottom, es=es):
            n = first_row + row_step * k
            flux[es, n] = value
            share = prec[es, k + 1] * is_sky
            return jnp.where(lane4 == n, fold(share * value), top), jnp.where(lane4 == n, fold(share), bottom)

        def backward(i, carry, es=es, sky_row=sky_row):
            next_one, next_two, top, bottom = carry
            k = ROWS - 1 - i
            value = start[es, k] - near[es, k] * next_one - far[es, k] * next_two
            top, bottom = sky_row(k, next_one, top, bottom)
            return value, next_one, top, bottom

        value, _, top, bottom = lax.fori_loop(0, ROWS - 1, backward, (edge_flux, beyond, zero4, zero4), unroll=7)
        top, bottom = sky_row(0, value, top, bottom)
        sums[g, 0, low * PAIR : (low + SLICE) * PAIR] = top
        sums[g, 1, low * PAIR : (low + SLICE) * PAIR] = bottom
        if low + SLICE == GROUP:
            sky_copies.append(
                [
                    send(
                        sums.at[g], boxes.at[g, specs - 1 - d], spec_send.at[g, d - 1], spec_recv.at[g, specs - 1 - d],
                        {"spec": lax.rem(spec + d, specs)},
                    )
                    for d in range(1, specs)
                ]
            )
            for copy in sky_copies[g]:
                copy.start()

    scale = 2.0 / (count * ROWS - 1)
    base_row = me * ROWS
    lane2 = lax.broadcasted_iota(jnp.int32, (PAIR, 128), 1)
    used = lax.broadcasted_iota(jnp.int32, (GROUP, 128), 1) < ROWS
    zero = jnp.zeros((PAIR, F), f32)
    zero_moment = jnp.zeros((PAIR, 128), f32)
    for g in range(EXPO // GROUP):
        for copy in sky_copies[g]:
            copy.wait_recv()
        held = [sums[g]] + [boxes[g, k] for k in range(specs - 1)]
        total = None
        for s in range(specs):
            place = lax.rem(s - spec + specs, specs)
            term = held[0]
            for k in range(1, specs):
                term = jnp.where(place == k, held[k], term)
            total = term if total is None else total + term
        total = total.reshape(2, GROUP, PAIR, 128).sum(2)
        model = jnp.where(used, total[0], 0.0) / jnp.where(used, total[1], 1.0)
        model_v[g] = model
        to_scalar = pltpu.make_async_copy(model_v.at[g], model_s.at[g], smem_sem)
        to_scalar.start()
        model_ref[g * GROUP : (g + 1) * GROUP] = model
        to_scalar.wait()

        def regress(n, carry, g=g):
            first, second, moment = (list(v) for v in carry)
            place = (base_row + n).astype(f32) * scale - 1.0
            powers = jnp.where(lane2 == 0, 1.0, jnp.where(lane2 == 1, place, place * place))
            for i in range(GROUP):
                sky = model_s[g, i, n]
                term = flux[g * GROUP + i, n] * sky
                first[i] = first[i] + term
                second[i] = second[i] + term * place
                moment[i] = moment[i] + powers * (sky * sky)
            return tuple(first), tuple(second), tuple(moment)

        first, second, moment = lax.fori_loop(
            0, ROWS, regress, ((zero,) * GROUP, (zero,) * GROUP, (zero_moment,) * GROUP), unroll=5
        )
        for i in range(GROUP):
            e = g * GROUP + i
            for half, width in ((0, HALF), (1, F - HALF)):
                load[e, half, :, 0:width] = first[i][:, half * HALF : half * HALF + width]
                load[e, half, :, HALF : HALF + width] = second[i][:, half * HALF : half * HALF + width]
                load[e, half, :, WIDE:LOAD] = moment[i]
        for t in range(PLANE):
            where = ((t // CORES) * LINE + col) * CORES + t % CORES
            slot = lax.rem(mem - t + PLANE, PLANE) - 1

            @pl.when(mem != t)
            def _(t=t, where=where, slot=slot, g=g):
                source = load.at[g * GROUP + t % GROUP, t // GROUP]
                send(source, box_a.at[g, slot], a_send.at[g], a_recv.at[g], {"wave": where}).start()

    groups = range(EXPO // GROUP)
    whole_a = [send(box_a.at[g], box_a.at[g], a_send.at[g], a_recv.at[g], {"wave": partner}) for g in groups]
    whole_b = [send(box_b.at[g], box_b.at[g], b_send.at[g], b_recv.at[g], {"wave": partner}) for g in groups]
    whole_c = []
    for g in groups:
        seven = gathered.at[g, pl.ds(0, PLANE - 1)]
        whole_c.append(send(seven, seven, c_send.at[g], c_recv.at[g], {"wave": partner}))
    for g in groups:
        whole_a[g].wait_recv()
        acc = load[g * GROUP + lax.rem(mem, GROUP), lax.div(mem, GROUP)]
        for k in range(PLANE - 1):
            acc = acc + box_a[g, k]
        part[g] = acc
        for d in FAR_FIRST:
            send(part.at[g], box_b.at[g, LINE - 1 - d], b_send.at[g], b_recv.at[g], {"wave": line_peer(d)}).start()
    for g in groups:
        whole_b[g].wait_recv()
        acc = part[g]
        for k in range(LINE - 1):
            acc = acc + box_b[g, k]
        first_sum, second_sum, powers_sum = acc[:, :HALF], acc[:, HALF:WIDE], acc[:, WIDE:LOAD]

        def pick(i, powers_sum=powers_sum):
            return jnp.sum(jnp.where(lane2 == i, powers_sum, 0.0), axis=1, keepdims=True)

        upper, cross, lower = pick(0) + RIDGE, pick(1), pick(2) + RIDGE
        inverse = 1.0 / (upper * lower - cross * cross)
        piece[g, 0] = (lower * first_sum - cross * second_sum) * inverse
        piece[g, 1] = (upper * second_sum - cross * first_sum) * inverse
        for d in FAR_FIRST:
            send(piece.at[g], gathered.at[g, mem], c_send.at[g], c_recv.at[g], {"wave": plane_peer(d)[1]}).start()
        gathered[g, mem] = piece[g]
    for g in groups:
        whole_c[g].wait_recv()
        slope_a, slope_b = [], []
        for i in range(GROUP):
            for half in range(2):
                slope_ref[i, :, :, half * HALF : (half + 1) * HALF] = gathered[g, half * GROUP + i]
            slope_a.append(slope_ref[i, 0, :, 0:F])
            slope_b.append(slope_ref[i, 1, :, 0:F])

        def clean(n, carry, g=g, slope_a=slope_a, slope_b=slope_b):
            place = (base_row + n).astype(f32) * scale - 1.0
            for i in range(GROUP):
                fitted = slope_a[i] + slope_b[i] * place
                e = g * GROUP + i
                flux[e, n] = flux[e, n] - fitted * model_s[g, i, n]
            return carry

        lax.fori_loop(0, ROWS, clean, 0, unroll=5)
    for copy in far_edges + near_edges + sky_copies[0] + sky_copies[1] + whole_a + whole_b + whole_c:
        copy.wait_send()


def store_kernel(cleaned, model, cleaned_out, model_out, model_rows, sems):
    copies = [pltpu.make_async_copy(cleaned.at[e], cleaned_out.at[e], sems.at[e]) for e in range(EXPO)]
    for copy in copies:
        copy.start()
    model_rows[...] = model[:, 0:ROWS]
    copies.append(pltpu.make_async_copy(model_rows, model_out, sems.at[EXPO]))
    copies[-1].start()
    for copy in copies:
        copy.wait()


def local(pixels, ivar, mask, psf_left, psf_right, sky_index):
    turned = [jnp.transpose(v, (0, 2, 1, 3)) for v in (pixels, ivar, mask, psf_left, psf_right)]
    field = (EXPO, ROWS, PAIR, F)
    specs = lax.axis_size("spec")
    hbm, vmem = pl.BlockSpec(memory_space=pltpu.HBM), pl.BlockSpec(memory_space=pltpu.VMEM)
    dma = pltpu.SemaphoreType.DMA
    groups = EXPO // GROUP
    near_edge, far_edge = (groups, PARTS, GROUP, PAIR, F), (LATE, PARTS, SLICE, PAIR, F)
    cleaned, model = pl.pallas_call(
        main_kernel,
        out_shape=(
            jax.ShapeDtypeStruct(field, f32),
            jax.ShapeDtypeStruct((EXPO, 128), f32),
        ),
        in_specs=[hbm] * 5 + [pl.BlockSpec(memory_space=pltpu.SMEM)],
        out_specs=(vmem, vmem),
        scratch_shapes=[
            pltpu.VMEM(field, f32),
            pltpu.VMEM(field, f32),
            pltpu.VMEM(field, jnp.int32),
            pltpu.VMEM((2,) + field, f32),
            pltpu.VMEM(field, f32),
            pltpu.VMEM(field, f32),
            pltpu.VMEM(field, f32),
            pltpu.VMEM((EXPO, ROWS + 1, PAIR, F), f32),
            pltpu.VMEM(near_edge, f32),
            pltpu.VMEM(near_edge, f32),
            pltpu.VMEM(far_edge, f32),
            pltpu.VMEM(far_edge, f32),
            pltpu.VMEM((groups, 2, GROUP * PAIR, 128), f32),
            pltpu.VMEM((groups, specs - 1, 2, GROUP * PAIR, 128), f32),
            pltpu.VMEM((groups, GROUP, 128), f32),
            pltpu.SMEM((groups, GROUP, 128), f32),
            pltpu.VMEM((EXPO, 2, PAIR, LOAD), f32),
            pltpu.VMEM((groups, PLANE - 1, PAIR, LOAD), f32),
            pltpu.VMEM((groups, PAIR, LOAD), f32),
            pltpu.VMEM((groups, LINE - 1, PAIR, LOAD), f32),
            pltpu.VMEM((groups, 2, PAIR, HALF), f32),
            pltpu.VMEM((groups, PLANE, 2, PAIR, HALF), f32),
            pltpu.VMEM((GROUP, 2, PAIR, WIDE), f32),
            dma((3, 5)),
            dma((groups,)),
            dma((groups,)),
            dma((LATE,)),
            dma((LATE,)),
            dma((groups, specs - 1)),
            dma((groups, specs - 1)),
            dma,
            dma((groups,)),
            dma((groups,)),
            dma((groups,)),
            dma((groups,)),
            dma((groups,)),
            dma((groups,)),
        ],
        compiler_params=pltpu.CompilerParams(
            collective_id=0, has_side_effects=True, vmem_limit_bytes=54_000_000
        ),
        name="deconvolve",
    )(*turned, pltpu.with_memory_space_constraint(sky_index, pltpu.HBM))
    cleaned, model = pl.pallas_call(
        store_kernel,
        out_shape=(jax.ShapeDtypeStruct(field, f32), jax.ShapeDtypeStruct((EXPO, ROWS), f32)),
        in_specs=[vmem, vmem],
        out_specs=(hbm, hbm),
        scratch_shapes=[pltpu.VMEM((EXPO, ROWS), f32), dma((EXPO + 1,))],
        compiler_params=pltpu.CompilerParams(vmem_limit_bytes=54_000_000),
        name="store",
    )(cleaned, model)
    return (jnp.transpose(cleaned, (0, 2, 1, 3)), model)


def solution(mesh):
    in_specs = (
        P(None, "spec", "wave", None),
        P(None, "spec", "wave", None),
        P(None, "spec", "wave", None),
        P(None, "spec", "wave", None),
        P(None, "spec", "wave", None),
        P("spec", None),
    )
    out_specs = (P(None, "spec", "wave", None), P(None, "wave"))
    return jax.shard_map(local, mesh=mesh, in_specs=in_specs, out_specs=out_specs, check_vma=False)
```

```python
import jax
import jax.numpy as jnp
from jax import lax
from jax.experimental import pallas as pl
from jax.experimental.pallas import tpu as pltpu
from jax.sharding import PartitionSpec as P

F = 500
WIDE = 512
EXPO = 8
PAIR = 2
ROWS = 50
EDGE = 4
REG = 0.05
RIDGE = 1.0
MESH = pl.DeviceIdType.MESH

LINE = 8
CORES = 2
PLANE = 8
GROUP = 4
PARTS = 6
LOAD = 2 * WIDE + 128
FAR_FIRST = (4, 3, 5, 2, 6, 1, 7)

f32 = jnp.float32


def absorb(front, weight, outer, inner, pixel):
    a, b, d, ra, rb = front
    w_outer, w_inner, w_pixel = weight * outer, weight * inner, weight * pixel
    outer_square, inner_square = w_outer * outer, w_inner * inner
    a = a + outer_square + REG
    b = b + w_outer
    far = w_outer * inner
    d = d + weight
    ra = ra + outer * w_pixel
    rb = rb + w_pixel
    inverse = 1.0 / a
    near_factor, far_factor, start = b * inverse, far * inverse, ra * inverse
    front = (
        d - near_factor * b,
        w_inner - near_factor * far,
        inner_square - far_factor * far,
        rb - b * start,
        inner * w_pixel - far * start,
    )
    return front, (near_factor, far_factor, start), outer_square, inner_square


def main_kernel(
    px_hbm, iv_hbm, mk_hbm, lf_hbm, rt_hbm, index,
    flux, model_ref,
    px, iv, mk, lr, near, far, start, prec,
    out_edge, in_edge, sums, boxes, model_v, model_s, load, box_a, part, box_b, piece, slope_ref,
    load_sem, edge_send, edge_recv, spec_send, spec_recv, smem_sem,
    a_send, a_recv, b_send, b_recv, c_send, c_recv, known_one, known_two,
):
    me = lax.axis_index("wave")
    count = lax.axis_size("wave")
    spec = lax.axis_index("spec")
    specs = lax.axis_size("spec")
    core = lax.rem(me, CORES)
    col = lax.rem(lax.div(me, CORES), LINE)
    row = lax.div(me, CORES * LINE)
    mem = row * CORES + core

    def plane_peer(d):
        other = lax.rem(mem + d, PLANE)
        return other, (lax.div(other, CORES) * LINE + col) * CORES + lax.rem(other, CORES)

    def line_peer(d):
        return (row * LINE + lax.rem(col + d, LINE)) * CORES + core

    partner = me + 1 - 2 * core
    outside = lax.rem(me + 2 * core - 1 + count, count)

    def send(src, dst, send_sem, recv_sem, where):
        return pltpu.make_async_remote_copy(
            src_ref=src, dst_ref=dst, send_sem=send_sem, recv_sem=recv_sem, device_id=where, device_id_type=MESH
        )

    hbm = (iv_hbm, mk_hbm, lf_hbm, rt_hbm, px_hbm)
    vmem = (iv, mk, lr.at[0], lr.at[1], px)
    spans = (pl.ds((ROWS - EDGE) * core, EDGE), pl.ds((ROWS - EDGE) * (1 - core), EDGE), pl.ds(EDGE, ROWS - 2 * EDGE))
    everything = pl.ds(0, EXPO)
    cuts = [(everything, span) for span in spans[:2]] + [(pl.ds(g * GROUP, GROUP), spans[2]) for g in range(EXPO // GROUP)]
    loads = [
        [pltpu.make_async_copy(h.at[cut], v.at[cut], load_sem.at[i, j]) for j, (h, v) in enumerate(zip(hbm, vmem))]
        for i, cut in enumerate(cuts)
    ]

    barrier = pltpu.get_barrier_semaphore()

    def greet(peers):
        for peer in peers:
            pl.semaphore_signal(barrier, inc=1, device_id=peer, device_id_type=MESH)
        return len(peers)

    greeted = greet([{"wave": outside}, {"wave": partner}])
    for group in loads[:3]:
        for copy in group:
            copy.start()
    greeted += greet([{"wave": plane_peer(d)[1]} for d in FAR_FIRST])
    greeted += greet([{"spec": lax.rem(spec + d, specs)} for d in (2, 1, 3)])
    greeted += greet([{"wave": line_peer(1)}, {"wave": line_peer(LINE - 1)}])

    def weight_of(es, n):
        return iv[es, n] * (1.0 - mk[es, n].astype(f32))

    sides = ((46 - 43 * core, 1 - 2 * core, core, partner), (3 + 43 * core, 2 * core - 1, 1 - core, outside))

    def reduce_edge(side, g):
        base, step, outer, _ = sides[side]
        es = pl.ds(g * GROUP, GROUP)
        weight, inner = weight_of(es, base), lr[1 - outer, es, base]
        w_inner, w_pixel = weight * inner, weight * px[es, base]
        front = (weight, w_inner, w_inner * inner, w_pixel, inner * w_pixel)
        for i in range(1, EDGE):
            n = base + step * i
            front, _, _, inner_square = absorb(front, weight_of(es, n), lr[outer, es, n], lr[1 - outer, es, n], px[es, n])
        for i, value in enumerate(front + (inner_square,)):
            out_edge[side, g, i] = value

    edges = {}

    def hand_over(side, g):
        copy = send(
            out_edge.at[side, g], in_edge.at[side, g], edge_send.at[side, g], edge_recv.at[side, g],
            {"wave": sides[side][3]},
        )
        copy.start()
        edges[side, g] = copy

    for copy in loads[3]:
        copy.start()
    for copy in loads[0]:
        copy.wait()
    for g in range(EXPO // GROUP):
        reduce_edge(1, g)
        if g == 0:
            pl.semaphore_wait(barrier, greeted)
        hand_over(1, g)
    for copy in loads[1]:
        copy.wait()
    for g in range(EXPO // GROUP):
        reduce_edge(0, g)
        hand_over(0, g)
    for d in (1, LINE - 1):
        pl.semaphore_signal(known_one, inc=1, device_id={"wave": line_peer(d)}, device_id_type=MESH)
    fibre = lax.broadcasted_iota(jnp.int32, (PAIR, F), 1)
    second_row = lax.broadcasted_iota(jnp.int32, (PAIR, F), 0) == 1
    is_sky = jnp.zeros((PAIR, F), f32)
    for j in range(index.shape[1]):
        is_sky = is_sky + jnp.where(fibre == jnp.where(second_row, index[1, j], index[0, j]), 1.0, 0.0)
    is_sky = is_sky[None]

    lane8 = lax.broadcasted_iota(jnp.int32, (GROUP * PAIR, 128), 1)
    zero8 = jnp.zeros((GROUP * PAIR, 128), f32)

    def fold(value):
        return jnp.sum(value.reshape(GROUP * PAIR, F), axis=1, keepdims=True)

    first_row, row_step = (ROWS - 1) * (1 - core), 2 * core - 1
    fronts = []
    for g in range(EXPO // GROUP):
        es = pl.ds(g * GROUP, GROUP)
        for copy in loads[2 + g]:
            copy.wait()
        edges[0, g].wait_recv()
        a, b, d, ra, rb, last_square = (in_edge[0, g, i] for i in range(PARTS))

        def forward(k, carry, es=es):
            front, partial, last_square = carry
            n = first_row + row_step * k
            weight = weight_of(es, n)
            front, factors, outer_square, inner_square = absorb(
                front, weight, lr[1 - core, es, n], lr[core, es, n], px[es, n]
            )
            prec[es, k] = partial + outer_square
            near[es, k], far[es, k], start[es, k] = factors
            return front, weight + last_square + REG, inner_square

        front, partial, _ = lax.fori_loop(
            0, ROWS, forward, ((a, b, d, ra, rb), jnp.zeros_like(a), last_square), unroll=5
        )
        fronts.append((front, partial))

    pl.semaphore_wait(known_one, 2)
    for d in (2, LINE - 2):
        pl.semaphore_signal(known_two, inc=1, device_id={"wave": line_peer(d)}, device_id_type=MESH)
    alone = (me == 0) | (me == count - 1)
    sky_copies = []
    for g in range(EXPO // GROUP):
        es = pl.ds(g * GROUP, GROUP)
        edges[1, g].wait_recv()
        a2, b2, d2, ra2, rb2, next_square = (jnp.where(alone, 0.0, in_edge[1, g, i]) for i in range(PARTS))
        (a, b, d, ra, rb), partial = fronts[g]
        prec[es, ROWS] = partial + next_square
        b = b + b2
        inverse = 1.0 / (a + d2 + REG)
        factor, base = b * inverse, (ra + rb2) * inverse
        beyond = (rb + ra2 - b * base) / (d + a2 + REG - factor * b)
        edge_flux = base - factor * beyond
        flux[es, first_row + row_step * (ROWS - 1)] = edge_flux

        def backward(i, carry, es=es):
            next_one, next_two = carry
            k = ROWS - 1 - i
            value = start[es, k] - near[es, k] * next_one - far[es, k] * next_two
            flux[es, first_row + row_step * (k - 1)] = value
            return value, next_one

        lax.fori_loop(0, ROWS - 1, backward, (edge_flux, beyond), unroll=7)

        def sky_row(k, carry, es=es):
            top, bottom = carry
            n = first_row + row_step * k
            share = prec[es, k + 1] * is_sky
            scaled = share * flux[es, n]
            return jnp.where(lane8 == n, fold(scaled), top), jnp.where(lane8 == n, fold(share), bottom)

        sums[g, 0], sums[g, 1] = lax.fori_loop(0, ROWS, sky_row, (zero8, zero8), unroll=25)
        sky_copies.append(
            [
                send(
                    sums.at[g], boxes.at[g, specs - 1 - d], spec_send.at[g, d - 1], spec_recv.at[g, specs - 1 - d],
                    {"spec": lax.rem(spec + d, specs)},
                )
                for d in range(1, specs)
            ]
        )
        for copy in sky_copies[g]:
            copy.start()

    scale = 2.0 / (count * ROWS - 1)
    base_row = me * ROWS
    lane2 = lax.broadcasted_iota(jnp.int32, (PAIR, 128), 1)
    used = lax.broadcasted_iota(jnp.int32, (GROUP, 128), 1) < ROWS
    zero = jnp.zeros((PAIR, F), f32)
    zero_moment = jnp.zeros((PAIR, 128), f32)
    for g in range(EXPO // GROUP):
        for copy in sky_copies[g]:
            copy.wait_recv()
        held = [sums[g]] + [boxes[g, k] for k in range(specs - 1)]
        total = None
        for s in range(specs):
            place = lax.rem(s - spec + specs, specs)
            term = held[0]
            for k in range(1, specs):
                term = jnp.where(place == k, held[k], term)
            total = term if total is None else total + term
        total = total.reshape(2, GROUP, PAIR, 128).sum(2)
        model = jnp.where(used, total[0], 0.0) / jnp.where(used, total[1], 1.0)
        model_v[g] = model
        to_scalar = pltpu.make_async_copy(model_v.at[g], model_s.at[g], smem_sem)
        to_scalar.start()
        model_ref[g * GROUP : (g + 1) * GROUP] = model
        to_scalar.wait()

        def regress(n, carry, g=g):
            first, second, moment = (list(v) for v in carry)
            place = (base_row + n).astype(f32) * scale - 1.0
            powers = jnp.where(lane2 == 0, 1.0, jnp.where(lane2 == 1, place, place * place))
            for i in range(GROUP):
                sky = model_s[g, i, n]
                term = flux[g * GROUP + i, n] * sky
                first[i] = first[i] + term
                second[i] = second[i] + term * place
                moment[i] = moment[i] + powers * (sky * sky)
            return tuple(first), tuple(second), tuple(moment)

        first, second, moment = lax.fori_loop(
            0, ROWS, regress, ((zero,) * GROUP, (zero,) * GROUP, (zero_moment,) * GROUP), unroll=5
        )
        for i in range(GROUP):
            e = g * GROUP + i
            load[e, :, 0:F] = first[i]
            load[e, :, WIDE : WIDE + F] = second[i]
            load[e, :, 2 * WIDE : LOAD] = moment[i]
        for i in range(GROUP):
            e = g * GROUP + i
            where = ((e // CORES) * LINE + col) * CORES + e % CORES
            slot = lax.rem(mem - e + PLANE, PLANE) - 1

            @pl.when(mem != e)
            def _(e=e, where=where, slot=slot):
                send(load.at[e], box_a.at[slot], a_send, a_recv, {"wave": where}).start()

    whole_a = send(box_a, box_a, a_send, a_recv, {"wave": partner})
    whole_a.wait_recv()
    pl.semaphore_wait(known_two, 2)
    acc = load[mem]
    for k in range(PLANE - 1):
        acc = acc + box_a[k]
    part[...] = acc
    for d in FAR_FIRST:
        send(part, box_b.at[LINE - 1 - d], b_send, b_recv, {"wave": line_peer(d)}).start()
    whole_b = send(box_b, box_b, b_send, b_recv, {"wave": partner})
    whole_b.wait_recv()
    for k in range(LINE - 1):
        acc = acc + box_b[k]
    first_sum, second_sum, powers_sum = acc[:, :WIDE], acc[:, WIDE : 2 * WIDE], acc[:, 2 * WIDE : LOAD]

    def pick(i):
        return jnp.sum(jnp.where(lane2 == i, powers_sum, 0.0), axis=1, keepdims=True)

    upper, cross, lower = pick(0) + RIDGE, pick(1), pick(2) + RIDGE
    inverse = 1.0 / (upper * lower - cross * cross)
    piece[0] = (lower * first_sum - cross * second_sum) * inverse
    piece[1] = (upper * second_sum - cross * first_sum) * inverse
    slope_ref[mem] = piece[...]
    for d in FAR_FIRST:
        send(piece, slope_ref.at[mem], c_send, c_recv, {"wave": plane_peer(d)[1]}).start()
    whole_c = send(slope_ref.at[pl.ds(0, PLANE - 1)], slope_ref.at[pl.ds(0, PLANE - 1)], c_send, c_recv, {"wave": partner})
    whole_c.wait_recv()

    slope_a = [slope_ref[e, 0, :, 0:F] for e in range(EXPO)]
    slope_b = [slope_ref[e, 1, :, 0:F] for e in range(EXPO)]

    def clean(n, carry):
        place = (base_row + n).astype(f32) * scale - 1.0
        for e in range(EXPO):
            fitted = slope_a[e] + slope_b[e] * place
            flux[e, n] = flux[e, n] - fitted * model_s[e // GROUP, e % GROUP, n]
        return carry

    lax.fori_loop(0, ROWS, clean, 0, unroll=5)
    for copy in list(edges.values()) + sky_copies[0] + sky_copies[1]:
        copy.wait_send()
    whole_a.wait_send()
    whole_b.wait_send()
    whole_c.wait_send()


def store_kernel(cleaned, model, cleaned_out, model_out, model_rows, sems):
    copies = [pltpu.make_async_copy(cleaned.at[e], cleaned_out.at[e], sems.at[e]) for e in range(EXPO)]
    for copy in copies:
        copy.start()
    model_rows[...] = model[:, 0:ROWS]
    copies.append(pltpu.make_async_copy(model_rows, model_out, sems.at[EXPO]))
    copies[-1].start()
    for copy in copies:
        copy.wait()


def local(pixels, ivar, mask, psf_left, psf_right, sky_index):
    turned = [jnp.transpose(v, (0, 2, 1, 3)) for v in (pixels, ivar, mask, psf_left, psf_right)]
    field = (EXPO, ROWS, PAIR, F)
    specs = lax.axis_size("spec")
    hbm, vmem = pl.BlockSpec(memory_space=pltpu.HBM), pl.BlockSpec(memory_space=pltpu.VMEM)
    dma = pltpu.SemaphoreType.DMA
    groups = EXPO // GROUP
    edge = (2, groups, PARTS, GROUP, PAIR, F)
    cleaned, model = pl.pallas_call(
        main_kernel,
        out_shape=(
            jax.ShapeDtypeStruct(field, f32),
            jax.ShapeDtypeStruct((EXPO, 128), f32),
        ),
        in_specs=[hbm] * 5 + [pl.BlockSpec(memory_space=pltpu.SMEM)],
        out_specs=(vmem, vmem),
        scratch_shapes=[
            pltpu.VMEM(field, f32),
            pltpu.VMEM(field, f32),
            pltpu.VMEM(field, jnp.int32),
            pltpu.VMEM((2,) + field, f32),
            pltpu.VMEM(field, f32),
            pltpu.VMEM(field, f32),
            pltpu.VMEM(field, f32),
            pltpu.VMEM((EXPO, ROWS + 1, PAIR, F), f32),
            pltpu.VMEM(edge, f32),
            pltpu.VMEM(edge, f32),
            pltpu.VMEM((groups, 2, GROUP * PAIR, 128), f32),
            pltpu.VMEM((groups, specs - 1, 2, GROUP * PAIR, 128), f32),
            pltpu.VMEM((groups, GROUP, 128), f32),
            pltpu.SMEM((groups, GROUP, 128), f32),
            pltpu.VMEM((EXPO, PAIR, LOAD), f32),
            pltpu.VMEM((PLANE - 1, PAIR, LOAD), f32),
            pltpu.VMEM((PAIR, LOAD), f32),
            pltpu.VMEM((LINE - 1, PAIR, LOAD), f32),
            pltpu.VMEM((2, PAIR, WIDE), f32),
            pltpu.VMEM((EXPO, 2, PAIR, WIDE), f32),
            dma((2 + groups, 5)),
            dma((2, groups)),
            dma((2, groups)),
            dma((groups, specs - 1)),
            dma((groups, specs - 1)),
            dma,
            dma,
            dma,
            dma,
            dma,
            dma,
            dma,
            pltpu.SemaphoreType.REGULAR,
            pltpu.SemaphoreType.REGULAR,
        ],
        compiler_params=pltpu.CompilerParams(
            collective_id=0, has_side_effects=True, vmem_limit_bytes=54_000_000
        ),
        name="deconvolve",
    )(*turned, pltpu.with_memory_space_constraint(sky_index, pltpu.HBM))
    cleaned, model = pl.pallas_call(
        store_kernel,
        out_shape=(jax.ShapeDtypeStruct(field, f32), jax.ShapeDtypeStruct((EXPO, ROWS), f32)),
        in_specs=[vmem, vmem],
        out_specs=(hbm, hbm),
        scratch_shapes=[pltpu.VMEM((EXPO, ROWS), f32), dma((EXPO + 1,))],
        compiler_params=pltpu.CompilerParams(vmem_limit_bytes=54_000_000),
        name="store",
    )(cleaned, model)
    return (jnp.transpose(cleaned, (0, 2, 1, 3)), model)


def solution(mesh):
    in_specs = (
        P(None, "spec", "wave", None),
        P(None, "spec", "wave", None),
        P(None, "spec", "wave", None),
        P(None, "spec", "wave", None),
        P(None, "spec", "wave", None),
        P("spec", None),
    )
    out_specs = (P(None, "spec", "wave", None), P(None, "wave"))
    return jax.shard_map(local, mesh=mesh, in_specs=in_specs, out_specs=out_specs, check_vma=False)
```

```python
import jax
import jax.numpy as jnp
from jax import lax
from jax.experimental import pallas as pl
from jax.experimental.pallas import tpu as pltpu
from jax.sharding import PartitionSpec as P

F = 500
WIDE = 512
EXPO = 8
PAIR = 2
ROWS = 50
EDGE = 4
REG = 0.05
RIDGE = 1.0
MESH = pl.DeviceIdType.MESH

LINE = 8
CORES = 2
PLANE = 8
GROUP = 4
PARTS = 6
LOAD = 2 * WIDE + 128
FAR_FIRST = (4, 3, 5, 2, 6, 1, 7)

f32 = jnp.float32


def absorb(front, weight, outer, inner, pixel):
    a, b, d, ra, rb = front
    w_outer, w_inner, w_pixel = weight * outer, weight * inner, weight * pixel
    outer_square, inner_square = w_outer * outer, w_inner * inner
    own = weight + REG
    a = a + outer_square
    b = b + w_outer
    far = w_outer * inner
    d = d + own
    ra = ra + outer * w_pixel
    rb = rb + w_pixel
    inverse = 1.0 / a
    near_factor, far_factor, start = b * inverse, far * inverse, ra * inverse
    front = (
        d - near_factor * b,
        w_inner - near_factor * far,
        inner_square - far_factor * far,
        rb - b * start,
        inner * w_pixel - far * start,
    )
    return front, (near_factor, far_factor, start), outer_square, inner_square, own


def main_kernel(
    px_hbm, iv_hbm, mk_hbm, lf_hbm, rt_hbm, index_hbm,
    flux, model_ref,
    px, iv, mk, lr, index, near, far, start, prec,
    out_edge, in_edge, sums, boxes, model_v, model_s, load, box_a, part, box_b, piece, slope_ref,
    load_sem, index_sem, edge_send, edge_recv, spec_send, spec_recv, smem_sem,
    a_send, a_recv, b_send, b_recv, c_send, c_recv, known_one, known_two,
):
    me = lax.axis_index("wave")
    count = lax.axis_size("wave")
    spec = lax.axis_index("spec")
    specs = lax.axis_size("spec")
    core = lax.rem(me, CORES)
    col = lax.rem(lax.div(me, CORES), LINE)
    row = lax.div(me, CORES * LINE)
    mem = row * CORES + core

    def plane_peer(d):
        other = lax.rem(mem + d, PLANE)
        return other, (lax.div(other, CORES) * LINE + col) * CORES + lax.rem(other, CORES)

    def line_peer(d):
        return (row * LINE + lax.rem(col + d, LINE)) * CORES + core

    partner = me + 1 - 2 * core
    outside = lax.rem(me + 2 * core - 1 + count, count)

    def send(src, dst, send_sem, recv_sem, where):
        return pltpu.make_async_remote_copy(
            src_ref=src, dst_ref=dst, send_sem=send_sem, recv_sem=recv_sem, device_id=where, device_id_type=MESH
        )

    hbm = (iv_hbm, mk_hbm, lf_hbm, rt_hbm, px_hbm)
    vmem = (iv, mk, lr.at[0], lr.at[1], px)
    spans = (pl.ds((ROWS - EDGE) * core, EDGE), pl.ds((ROWS - EDGE) * (1 - core), EDGE), pl.ds(EDGE, ROWS - 2 * EDGE))
    everything = pl.ds(0, EXPO)
    cuts = [(everything, span) for span in spans[:2]] + [(pl.ds(g * GROUP, GROUP), spans[2]) for g in range(EXPO // GROUP)]
    loads = [
        [pltpu.make_async_copy(h.at[cut], v.at[cut], load_sem.at[i, j]) for j, (h, v) in enumerate(zip(hbm, vmem))]
        for i, cut in enumerate(cuts)
    ]

    barrier = pltpu.get_barrier_semaphore()

    def greet(peers):
        for peer in peers:
            pl.semaphore_signal(barrier, inc=1, device_id=peer, device_id_type=MESH)
        return len(peers)

    greeted = greet([{"wave": outside}, {"wave": partner}])
    for group in loads[:3]:
        for copy in group:
            copy.start()
    greeted += greet([{"wave": plane_peer(d)[1]} for d in FAR_FIRST])
    greeted += greet([{"spec": lax.rem(spec + d, specs)} for d in (2, 1, 3)])
    greeted += greet([{"wave": line_peer(1)}, {"wave": line_peer(LINE - 1)}])

    def weight_of(es, n):
        return jnp.where(mk[es, n] == 0, iv[es, n], 0.0)

    sides = ((46 - 43 * core, 1 - 2 * core, core, partner), (3 + 43 * core, 2 * core - 1, 1 - core, outside))

    def reduce_edge(side, g):
        base, step, outer, _ = sides[side]
        es = pl.ds(g * GROUP, GROUP)
        weight, inner = weight_of(es, base), lr[1 - outer, es, base]
        w_inner, w_pixel = weight * inner, weight * px[es, base]
        front = (weight + REG, w_inner, w_inner * inner, w_pixel, inner * w_pixel)
        for i in range(1, EDGE):
            n = base + step * i
            front, _, _, inner_square, _ = absorb(front, weight_of(es, n), lr[outer, es, n], lr[1 - outer, es, n], px[es, n])
        for i, value in enumerate(front + (inner_square,)):
            out_edge[side, g, i] = value

    edges = {}

    def hand_over(side, g):
        copy = send(
            out_edge.at[side, g], in_edge.at[side, g], edge_send.at[side, g], edge_recv.at[side, g],
            {"wave": sides[side][3]},
        )
        copy.start()
        edges[side, g] = copy

    for copy in loads[3]:
        copy.start()
    index_copy = pltpu.make_async_copy(index_hbm, index, index_sem)
    index_copy.start()
    for copy in loads[0]:
        copy.wait()
    for g in range(EXPO // GROUP):
        reduce_edge(1, g)
        if g == 0:
            pl.semaphore_wait(barrier, greeted)
        hand_over(1, g)
    for copy in loads[1]:
        copy.wait()
    for g in range(EXPO // GROUP):
        reduce_edge(0, g)
        hand_over(0, g)
    for d in (1, LINE - 1):
        pl.semaphore_signal(known_one, inc=1, device_id={"wave": line_peer(d)}, device_id_type=MESH)
    fibre = lax.broadcasted_iota(jnp.int32, (PAIR, F), 1)
    index_copy.wait()
    second_row = lax.broadcasted_iota(jnp.int32, (PAIR, F), 0) == 1
    is_sky = jnp.zeros((PAIR, F), f32)
    for j in range(index.shape[1]):
        is_sky = is_sky + jnp.where(fibre == jnp.where(second_row, index[1, j], index[0, j]), 1.0, 0.0)
    is_sky = is_sky[None]

    lane8 = lax.broadcasted_iota(jnp.int32, (GROUP * PAIR, 128), 1)
    zero8 = jnp.zeros((GROUP * PAIR, 128), f32)

    def fold(value):
        return jnp.sum(value.reshape(GROUP * PAIR, F), axis=1, keepdims=True)

    first_row, row_step = (ROWS - 1) * (1 - core), 2 * core - 1
    fronts = []
    for g in range(EXPO // GROUP):
        es = pl.ds(g * GROUP, GROUP)
        for copy in loads[2 + g]:
            copy.wait()
        edges[0, g].wait_recv()
        a, b, d, ra, rb, last_square = (in_edge[0, g, i] for i in range(PARTS))

        def forward(k, carry, es=es):
            front, partial, last_square = carry
            n = first_row + row_step * k
            weight = weight_of(es, n)
            front, factors, outer_square, inner_square, own = absorb(
                front, weight, lr[1 - core, es, n], lr[core, es, n], px[es, n]
            )
            prec[es, k] = partial + outer_square
            near[es, k], far[es, k], start[es, k] = factors
            return front, own + last_square, inner_square

        front, partial, _ = lax.fori_loop(
            0, ROWS, forward, ((a, b, d, ra, rb), jnp.zeros_like(a), last_square), unroll=5
        )
        fronts.append((front, partial))

    pl.semaphore_wait(known_one, 2)
    for d in (2, LINE - 2):
        pl.semaphore_signal(known_two, inc=1, device_id={"wave": line_peer(d)}, device_id_type=MESH)
    alone = (me == 0) | (me == count - 1)
    sky_copies = []
    for g in range(EXPO // GROUP):
        es = pl.ds(g * GROUP, GROUP)
        edges[1, g].wait_recv()
        a2, b2, d2, ra2, rb2, next_square = (
            jnp.where(alone, 0.0 if i else REG, in_edge[1, g, i]) for i in range(PARTS)
        )
        (a, b, d, ra, rb), partial = fronts[g]
        prec[es, ROWS] = partial + next_square
        b = b + b2
        inverse = 1.0 / (a + d2)
        factor, base = b * inverse, (ra + rb2) * inverse
        beyond = (rb + ra2 - b * base) / (d + a2 - factor * b)
        edge_flux = base - factor * beyond
        flux[es, first_row + row_step * (ROWS - 1)] = edge_flux

        def backward(i, carry, es=es):
            next_one, next_two = carry
            k = ROWS - 1 - i
            value = start[es, k] - near[es, k] * next_one - far[es, k] * next_two
            flux[es, first_row + row_step * (k - 1)] = value
            return value, next_one

        lax.fori_loop(0, ROWS - 1, backward, (edge_flux, beyond), unroll=7)

        def sky_row(k, carry, es=es):
            top, bottom = carry
            n = first_row + row_step * k
            share = prec[es, k + 1] * is_sky
            scaled = share * flux[es, n]
            return jnp.where(lane8 == n, fold(scaled), top), jnp.where(lane8 == n, fold(share), bottom)

        sums[g, 0], sums[g, 1] = lax.fori_loop(0, ROWS, sky_row, (zero8, zero8), unroll=25)
        sky_copies.append(
            [
                send(
                    sums.at[g], boxes.at[g, specs - 1 - d], spec_send.at[g, d - 1], spec_recv.at[g, specs - 1 - d],
                    {"spec": lax.rem(spec + d, specs)},
                )
                for d in range(1, specs)
            ]
        )
        for copy in sky_copies[g]:
            copy.start()

    scale = 2.0 / (count * ROWS - 1)
    base_row = me * ROWS
    lane2 = lax.broadcasted_iota(jnp.int32, (PAIR, 128), 1)
    used = lax.broadcasted_iota(jnp.int32, (GROUP, 128), 1) < ROWS
    zero = jnp.zeros((PAIR, F), f32)
    zero_moment = jnp.zeros((PAIR, 128), f32)
    for g in range(EXPO // GROUP):
        for copy in sky_copies[g]:
            copy.wait_recv()
        held = [sums[g]] + [boxes[g, k] for k in range(specs - 1)]
        total = None
        for s in range(specs):
            place = lax.rem(s - spec + specs, specs)
            term = held[0]
            for k in range(1, specs):
                term = jnp.where(place == k, held[k], term)
            total = term if total is None else total + term
        total = total.reshape(2, GROUP, PAIR, 128).sum(2)
        model = jnp.where(used, total[0], 0.0) / jnp.where(used, total[1], 1.0)
        model_v[g] = model
        to_scalar = pltpu.make_async_copy(model_v.at[g], model_s.at[g], smem_sem)
        to_scalar.start()
        model_ref[g * GROUP : (g + 1) * GROUP] = model
        to_scalar.wait()

        def regress(n, carry, g=g):
            first, second, moment = (list(v) for v in carry)
            place = (base_row + n).astype(f32) * scale - 1.0
            powers = jnp.where(lane2 == 0, 1.0, jnp.where(lane2 == 1, place, place * place))
            for i in range(GROUP):
                sky = model_s[g, i, n]
                term = flux[g * GROUP + i, n] * sky
                first[i] = first[i] + term
                second[i] = second[i] + term * place
                moment[i] = moment[i] + powers * (sky * sky)
            return tuple(first), tuple(second), tuple(moment)

        first, second, moment = lax.fori_loop(
            0, ROWS, regress, ((zero,) * GROUP, (zero,) * GROUP, (zero_moment,) * GROUP), unroll=5
        )
        for i in range(GROUP):
            e = g * GROUP + i
            load[e, :, 0:F] = first[i]
            load[e, :, WIDE : WIDE + F] = second[i]
            load[e, :, 2 * WIDE : LOAD] = moment[i]
        for i in range(GROUP):
            e = g * GROUP + i
            where = ((e // CORES) * LINE + col) * CORES + e % CORES
            slot = lax.rem(mem - e + PLANE, PLANE) - 1

            @pl.when(mem != e)
            def _(e=e, where=where, slot=slot):
                send(load.at[e], box_a.at[slot], a_send, a_recv, {"wave": where}).start()

    whole_a = send(box_a, box_a, a_send, a_recv, {"wave": partner})
    whole_a.wait_recv()
    pl.semaphore_wait(known_two, 2)
    acc = load[mem]
    for k in range(PLANE - 1):
        acc = acc + box_a[k]
    part[...] = acc
    for d in FAR_FIRST:
        send(part, box_b.at[LINE - 1 - d], b_send, b_recv, {"wave": line_peer(d)}).start()
    whole_b = send(box_b, box_b, b_send, b_recv, {"wave": partner})
    whole_b.wait_recv()
    for k in range(LINE - 1):
        acc = acc + box_b[k]
    first_sum, second_sum, powers_sum = acc[:, :WIDE], acc[:, WIDE : 2 * WIDE], acc[:, 2 * WIDE : LOAD]

    def pick(i):
        return jnp.sum(jnp.where(lane2 == i, powers_sum, 0.0), axis=1, keepdims=True)

    upper, cross, lower = pick(0) + RIDGE, pick(1), pick(2) + RIDGE
    inverse = 1.0 / (upper * lower - cross * cross)
    piece[0] = (lower * first_sum - cross * second_sum) * inverse
    piece[1] = (upper * second_sum - cross * first_sum) * inverse
    slope_ref[mem] = piece[...]
    for d in FAR_FIRST:
        send(piece, slope_ref.at[mem], c_send, c_recv, {"wave": plane_peer(d)[1]}).start()
    whole_c = send(slope_ref.at[pl.ds(0, PLANE - 1)], slope_ref.at[pl.ds(0, PLANE - 1)], c_send, c_recv, {"wave": partner})
    whole_c.wait_recv()

    slope_a = [slope_ref[e, 0, :, 0:F] for e in range(EXPO)]
    slope_b = [slope_ref[e, 1, :, 0:F] for e in range(EXPO)]

    def clean(n, carry):
        place = (base_row + n).astype(f32) * scale - 1.0
        for e in range(EXPO):
            fitted = slope_a[e] + slope_b[e] * place
            flux[e, n] = flux[e, n] - fitted * model_s[e // GROUP, e % GROUP, n]
        return carry

    lax.fori_loop(0, ROWS, clean, 0, unroll=5)
    for copy in list(edges.values()) + sky_copies[0] + sky_copies[1]:
        copy.wait_send()
    whole_a.wait_send()
    whole_b.wait_send()
    whole_c.wait_send()


def store_kernel(cleaned, model, cleaned_out, model_out, model_rows, sems):
    main = pltpu.make_async_copy(cleaned, cleaned_out, sems.at[0])
    main.start()
    model_rows[...] = model[:, 0:ROWS]
    small = pltpu.make_async_copy(model_rows, model_out, sems.at[1])
    small.start()
    small.wait()
    main.wait()


def local(pixels, ivar, mask, psf_left, psf_right, sky_index):
    turned = [jnp.transpose(v, (0, 2, 1, 3)) for v in (pixels, ivar, mask, psf_left, psf_right)]
    field = (EXPO, ROWS, PAIR, F)
    specs = lax.axis_size("spec")
    hbm, vmem = pl.BlockSpec(memory_space=pltpu.HBM), pl.BlockSpec(memory_space=pltpu.VMEM)
    dma = pltpu.SemaphoreType.DMA
    groups = EXPO // GROUP
    edge = (2, groups, PARTS, GROUP, PAIR, F)
    cleaned, model = pl.pallas_call(
        main_kernel,
        out_shape=(
            jax.ShapeDtypeStruct(field, f32),
            jax.ShapeDtypeStruct((EXPO, 128), f32),
        ),
        in_specs=[hbm] * 6,
        out_specs=(vmem, vmem),
        scratch_shapes=[
            pltpu.VMEM(field, f32),
            pltpu.VMEM(field, f32),
            pltpu.VMEM(field, jnp.int32),
            pltpu.VMEM((2,) + field, f32),
            pltpu.SMEM(sky_index.shape, jnp.int32),
            pltpu.VMEM(field, f32),
            pltpu.VMEM(field, f32),
            pltpu.VMEM(field, f32),
            pltpu.VMEM((EXPO, ROWS + 1, PAIR, F), f32),
            pltpu.VMEM(edge, f32),
            pltpu.VMEM(edge, f32),
            pltpu.VMEM((groups, 2, GROUP * PAIR, 128), f32),
            pltpu.VMEM((groups, specs - 1, 2, GROUP * PAIR, 128), f32),
            pltpu.VMEM((groups, GROUP, 128), f32),
            pltpu.SMEM((groups, GROUP, 128), f32),
            pltpu.VMEM((EXPO, PAIR, LOAD), f32),
            pltpu.VMEM((PLANE - 1, PAIR, LOAD), f32),
            pltpu.VMEM((PAIR, LOAD), f32),
            pltpu.VMEM((LINE - 1, PAIR, LOAD), f32),
            pltpu.VMEM((2, PAIR, WIDE), f32),
            pltpu.VMEM((EXPO, 2, PAIR, WIDE), f32),
            dma((2 + groups, 5)),
            dma,
            dma((2, groups)),
            dma((2, groups)),
            dma((groups, specs - 1)),
            dma((groups, specs - 1)),
            dma,
            dma,
            dma,
            dma,
            dma,
            dma,
            dma,
            pltpu.SemaphoreType.REGULAR,
            pltpu.SemaphoreType.REGULAR,
        ],
        compiler_params=pltpu.CompilerParams(
            collective_id=0, has_side_effects=True, vmem_limit_bytes=54_000_000
        ),
        name="deconvolve",
    )(*turned, pltpu.with_memory_space_constraint(sky_index, pltpu.HBM))
    cleaned, model = pl.pallas_call(
        store_kernel,
        out_shape=(jax.ShapeDtypeStruct(field, f32), jax.ShapeDtypeStruct((EXPO, ROWS), f32)),
        in_specs=[vmem, vmem],
        out_specs=(hbm, hbm),
        scratch_shapes=[pltpu.VMEM((EXPO, ROWS), f32), dma((2,))],
        compiler_params=pltpu.CompilerParams(vmem_limit_bytes=54_000_000),
        name="store",
    )(cleaned, model)
    return (jnp.transpose(cleaned, (0, 2, 1, 3)), model)


def solution(mesh):
    in_specs = (
        P(None, "spec", "wave", None),
        P(None, "spec", "wave", None),
        P(None, "spec", "wave", None),
        P(None, "spec", "wave", None),
        P(None, "spec", "wave", None),
        P("spec", None),
    )
    out_specs = (P(None, "spec", "wave", None), P(None, "wave"))
    return jax.shard_map(local, mesh=mesh, in_specs=in_specs, out_specs=out_specs, check_vma=False)
```

```python
import jax
import jax.numpy as jnp
from jax import lax
from jax.experimental import pallas as pl
from jax.experimental.pallas import tpu as pltpu
from jax.sharding import PartitionSpec as P

F = 500
WIDE = 512
EXPO = 8
PAIR = 2
ROWS = 50
EDGE = 4
REG = 0.05
RIDGE = 1.0
MESH = pl.DeviceIdType.MESH

LINE = 8
CORES = 2
PLANE = 8
GROUP = 4
PARTS = 6
LOAD = 2 * WIDE
TILE = WIDE - 128
SPARE = F - TILE
FAR_FIRST = (4, 3, 5, 2, 6, 1, 7)

f32 = jnp.float32


def absorb(front, weight, outer, inner, pixel):
    a, b, d, ra, rb = front
    w_outer, w_inner, w_pixel = weight * outer, weight * inner, weight * pixel
    outer_square, inner_square = w_outer * outer, w_inner * inner
    own = weight + REG
    a = a + outer_square
    b = b + w_outer
    far = w_outer * inner
    d = d + own
    ra = ra + outer * w_pixel
    rb = rb + w_pixel
    inverse = 1.0 / a
    near_factor, far_factor, start = b * inverse, far * inverse, ra * inverse
    front = (
        d - near_factor * b,
        w_inner - near_factor * far,
        inner_square - far_factor * far,
        rb - b * start,
        inner * w_pixel - far * start,
    )
    return front, (near_factor, far_factor, start), outer_square, inner_square, own


def main_kernel(
    px_hbm, iv_hbm, mk_hbm, lf_hbm, rt_hbm, index_hbm,
    flux, model_ref,
    px, iv, mk, lr, index, near, far, start, prec,
    out_edge, in_edge, sums, boxes, model_v, model_s, load, box_a, part, box_b, piece, slope_ref,
    load_sem, index_sem, edge_send, edge_recv, spec_send, spec_recv, smem_sem,
    a_send, a_recv, b_send, b_recv, c_send, c_recv, known_one, known_two,
):
    me = lax.axis_index("wave")
    count = lax.axis_size("wave")
    spec = lax.axis_index("spec")
    specs = lax.axis_size("spec")
    core = lax.rem(me, CORES)
    col = lax.rem(lax.div(me, CORES), LINE)
    row = lax.div(me, CORES * LINE)
    mem = row * CORES + core

    def plane_peer(d):
        other = lax.rem(mem + d, PLANE)
        return other, (lax.div(other, CORES) * LINE + col) * CORES + lax.rem(other, CORES)

    def line_peer(d):
        return (row * LINE + lax.rem(col + d, LINE)) * CORES + core

    partner = me + 1 - 2 * core
    outside = lax.rem(me + 2 * core - 1 + count, count)

    def send(src, dst, send_sem, recv_sem, where):
        return pltpu.make_async_remote_copy(
            src_ref=src, dst_ref=dst, send_sem=send_sem, recv_sem=recv_sem, device_id=where, device_id_type=MESH
        )

    hbm = (iv_hbm, mk_hbm, lf_hbm, rt_hbm, px_hbm)
    vmem = (iv, mk, lr.at[0], lr.at[1], px)
    spans = (pl.ds((ROWS - EDGE) * core, EDGE), pl.ds((ROWS - EDGE) * (1 - core), EDGE), pl.ds(EDGE, ROWS - 2 * EDGE))
    everything = pl.ds(0, EXPO)
    cuts = [(everything, span) for span in spans[:2]] + [(pl.ds(g * GROUP, GROUP), spans[2]) for g in range(EXPO // GROUP)]
    loads = [
        [pltpu.make_async_copy(h.at[cut], v.at[cut], load_sem.at[i, j]) for j, (h, v) in enumerate(zip(hbm, vmem))]
        for i, cut in enumerate(cuts)
    ]

    barrier = pltpu.get_barrier_semaphore()

    def greet(peers):
        for peer in peers:
            pl.semaphore_signal(barrier, inc=1, device_id=peer, device_id_type=MESH)
        return len(peers)

    greeted = greet([{"wave": outside}, {"wave": partner}])
    for group in loads[:3]:
        for copy in group:
            copy.start()
    greeted += greet([{"wave": plane_peer(d)[1]} for d in FAR_FIRST])
    greeted += greet([{"spec": lax.rem(spec + d, specs)} for d in (2, 1, 3)])
    greeted += greet([{"wave": line_peer(1)}, {"wave": line_peer(LINE - 1)}])

    def weight_of(es, n):
        return jnp.where(mk[es, n] == 0, iv[es, n], 0.0)

    sides = ((46 - 43 * core, 1 - 2 * core, core, partner), (3 + 43 * core, 2 * core - 1, 1 - core, outside))

    def reduce_edge(side, g):
        base, step, outer, _ = sides[side]
        es = pl.ds(g * GROUP, GROUP)
        weight, inner = weight_of(es, base), lr[1 - outer, es, base]
        w_inner, w_pixel = weight * inner, weight * px[es, base]
        front = (weight + REG, w_inner, w_inner * inner, w_pixel, inner * w_pixel)
        for i in range(1, EDGE):
            n = base + step * i
            front, _, _, inner_square, _ = absorb(front, weight_of(es, n), lr[outer, es, n], lr[1 - outer, es, n], px[es, n])
        for i, value in enumerate(front + (inner_square,)):
            out_edge[side, g, i] = value

    edges = {}

    def hand_over(side, g):
        copy = send(
            out_edge.at[side, g], in_edge.at[side, g], edge_send.at[side, g], edge_recv.at[side, g],
            {"wave": sides[side][3]},
        )
        copy.start()
        edges[side, g] = copy

    for copy in loads[0]:
        copy.wait()
    reduce_edge(1, 0)
    pl.semaphore_wait(barrier, greeted)
    hand_over(1, 0)
    for copy in loads[1]:
        copy.wait()
    for side, g in ((0, 0), (1, 1), (0, 1)):
        reduce_edge(side, g)
        hand_over(side, g)
    for copy in loads[3]:
        copy.start()
    index_copy = pltpu.make_async_copy(index_hbm, index, index_sem)
    index_copy.start()
    for d in (1, LINE - 1):
        pl.semaphore_signal(known_one, inc=1, device_id={"wave": line_peer(d)}, device_id_type=MESH)
    fibre = lax.broadcasted_iota(jnp.int32, (PAIR, F), 1)
    index_copy.wait()
    second_row = lax.broadcasted_iota(jnp.int32, (PAIR, F), 0) == 1
    is_sky = jnp.zeros((PAIR, F), f32)
    for j in range(index.shape[1]):
        is_sky = is_sky + jnp.where(fibre == jnp.where(second_row, index[1, j], index[0, j]), 1.0, 0.0)
    is_sky = is_sky[None]

    lane8 = lax.broadcasted_iota(jnp.int32, (GROUP * PAIR, 128), 1)
    zero8 = jnp.zeros((GROUP * PAIR, 128), f32)

    def fold(value):
        return jnp.sum(value.reshape(GROUP * PAIR, F), axis=1, keepdims=True)

    first_row, row_step = (ROWS - 1) * (1 - core), 2 * core - 1
    fronts = []
    for g in range(EXPO // GROUP):
        es = pl.ds(g * GROUP, GROUP)
        for copy in loads[2 + g]:
            copy.wait()
        edges[0, g].wait_recv()
        a, b, d, ra, rb, last_square = (in_edge[0, g, i] for i in range(PARTS))

        def forward(k, carry, es=es):
            front, partial, last_square = carry
            n = first_row + row_step * k
            weight = weight_of(es, n)
            front, factors, outer_square, inner_square, own = absorb(
                front, weight, lr[1 - core, es, n], lr[core, es, n], px[es, n]
            )
            prec[es, k] = partial + outer_square
            near[es, k], far[es, k], start[es, k] = factors
            return front, own + last_square, inner_square

        front, partial, _ = lax.fori_loop(
            0, ROWS, forward, ((a, b, d, ra, rb), jnp.zeros_like(a), last_square), unroll=5
        )
        fronts.append((front, partial))

    pl.semaphore_wait(known_one, 2)
    for d in (2, LINE - 2):
        pl.semaphore_signal(known_two, inc=1, device_id={"wave": line_peer(d)}, device_id_type=MESH)
    alone = (me == 0) | (me == count - 1)
    sky_copies = []
    for g in range(EXPO // GROUP):
        es = pl.ds(g * GROUP, GROUP)
        edges[1, g].wait_recv()
        a2, b2, d2, ra2, rb2, next_square = (
            jnp.where(alone, 0.0 if i else REG, in_edge[1, g, i]) for i in range(PARTS)
        )
        (a, b, d, ra, rb), partial = fronts[g]
        prec[es, ROWS] = partial + next_square
        b = b + b2
        inverse = 1.0 / (a + d2)
        factor, base = b * inverse, (ra + rb2) * inverse
        beyond = (rb + ra2 - b * base) / (d + a2 - factor * b)
        edge_flux = base - factor * beyond
        flux[es, first_row + row_step * (ROWS - 1)] = edge_flux

        def backward(i, carry, es=es):
            next_one, next_two = carry
            k = ROWS - 1 - i
            value = start[es, k] - near[es, k] * next_one - far[es, k] * next_two
            flux[es, first_row + row_step * (k - 1)] = value
            return value, next_one

        lax.fori_loop(0, ROWS - 1, backward, (edge_flux, beyond), unroll=7)

        def sky_row(k, carry, es=es):
            top, bottom = carry
            n = first_row + row_step * k
            share = prec[es, k + 1] * is_sky
            scaled = share * flux[es, n]
            return jnp.where(lane8 == n, fold(scaled), top), jnp.where(lane8 == n, fold(share), bottom)

        sums[g, 0], sums[g, 1] = lax.fori_loop(0, ROWS, sky_row, (zero8, zero8), unroll=25)
        sky_copies.append(
            [
                send(
                    sums.at[g], boxes.at[g, specs - 1 - d], spec_send.at[g, d - 1], spec_recv.at[g, specs - 1 - d],
                    {"spec": lax.rem(spec + d, specs)},
                )
                for d in range(1, specs)
            ]
        )
        for copy in sky_copies[g]:
            copy.start()

    scale = 2.0 / (count * ROWS - 1)
    base_row = me * ROWS
    lane2 = lax.broadcasted_iota(jnp.int32, (PAIR, 128), 1)
    used = lax.broadcasted_iota(jnp.int32, (GROUP, 128), 1) < ROWS
    zero = jnp.zeros((PAIR, F), f32)
    zero_moment = jnp.zeros((PAIR, 128), f32)
    for g in range(EXPO // GROUP):
        for copy in sky_copies[g]:
            copy.wait_recv()
        held = [sums[g]] + [boxes[g, k] for k in range(specs - 1)]
        total = None
        for s in range(specs):
            place = lax.rem(s - spec + specs, specs)
            term = held[0]
            for k in range(1, specs):
                term = jnp.where(place == k, held[k], term)
            total = term if total is None else total + term
        total = total.reshape(2, GROUP, PAIR, 128).sum(2)
        model = jnp.where(used, total[0], 0.0) / jnp.where(used, total[1], 1.0)
        model_v[g] = model
        to_scalar = pltpu.make_async_copy(model_v.at[g], model_s.at[g], smem_sem)
        to_scalar.start()
        model_ref[g * GROUP : (g + 1) * GROUP] = model
        to_scalar.wait()

        def regress(n, carry, g=g):
            first, second, moment = (list(v) for v in carry)
            place = (base_row + n).astype(f32) * scale - 1.0
            powers = jnp.where(lane2 == SPARE, 1.0, jnp.where(lane2 == SPARE + 1, place, place * place))
            for i in range(GROUP):
                sky = model_s[g, i, n]
                term = flux[g * GROUP + i, n] * sky
                first[i] = first[i] + term
                second[i] = second[i] + term * place
                moment[i] = moment[i] + powers * (sky * sky)
            return tuple(first), tuple(second), tuple(moment)

        first, second, moment = lax.fori_loop(
            0, ROWS, regress, ((zero,) * GROUP, (zero,) * GROUP, (zero_moment,) * GROUP), unroll=5
        )
        for i in range(GROUP):
            e = g * GROUP + i
            load[e, :, 0:F] = first[i]
            load[e, :, WIDE : WIDE + F] = second[i]
            load[e, :, TILE:WIDE] = jnp.where(lane2 < SPARE, load[e, :, TILE:WIDE], moment[i])
        for i in range(GROUP):
            e = g * GROUP + i
            where = ((e // CORES) * LINE + col) * CORES + e % CORES
            slot = lax.rem(mem - e + PLANE, PLANE) - 1

            @pl.when(mem != e)
            def _(e=e, where=where, slot=slot):
                send(load.at[e], box_a.at[slot], a_send, a_recv, {"wave": where}).start()

    whole_a = send(box_a, box_a, a_send, a_recv, {"wave": partner})
    whole_a.wait_recv()
    pl.semaphore_wait(known_two, 2)
    acc = load[mem]
    for k in range(PLANE - 1):
        acc = acc + box_a[k]
    part[...] = acc
    for d in FAR_FIRST:
        send(part, box_b.at[LINE - 1 - d], b_send, b_recv, {"wave": line_peer(d)}).start()
    whole_b = send(box_b, box_b, b_send, b_recv, {"wave": partner})
    whole_b.wait_recv()
    for k in range(LINE - 1):
        acc = acc + box_b[k]
    first_sum, second_sum, powers_sum = acc[:, :WIDE], acc[:, WIDE:LOAD], acc[:, TILE:WIDE]

    def pick(i):
        return jnp.sum(jnp.where(lane2 == SPARE + i, powers_sum, 0.0), axis=1, keepdims=True)

    upper, cross, lower = pick(0) + RIDGE, pick(1), pick(2) + RIDGE
    inverse = 1.0 / (upper * lower - cross * cross)
    piece[0] = (lower * first_sum - cross * second_sum) * inverse
    piece[1] = (upper * second_sum - cross * first_sum) * inverse
    slope_ref[mem] = piece[...]
    for d in FAR_FIRST:
        send(piece, slope_ref.at[mem], c_send, c_recv, {"wave": plane_peer(d)[1]}).start()
    whole_c = send(slope_ref.at[pl.ds(0, PLANE - 1)], slope_ref.at[pl.ds(0, PLANE - 1)], c_send, c_recv, {"wave": partner})
    whole_c.wait_recv()

    slope_a = [slope_ref[e, 0, :, 0:F] for e in range(EXPO)]
    slope_b = [slope_ref[e, 1, :, 0:F] for e in range(EXPO)]

    def clean(n, carry):
        place = (base_row + n).astype(f32) * scale - 1.0
        for e in range(EXPO):
            fitted = slope_a[e] + slope_b[e] * place
            flux[e, n] = flux[e, n] - fitted * model_s[e // GROUP, e % GROUP, n]
        return carry

    lax.fori_loop(0, ROWS, clean, 0, unroll=5)
    for copy in list(edges.values()) + sky_copies[0] + sky_copies[1]:
        copy.wait_send()
    whole_a.wait_send()
    whole_b.wait_send()
    whole_c.wait_send()


def store_kernel(cleaned, model, cleaned_out, model_out, model_rows, sems):
    main = pltpu.make_async_copy(cleaned, cleaned_out, sems.at[0])
    main.start()
    model_rows[...] = model[:, 0:ROWS]
    small = pltpu.make_async_copy(model_rows, model_out, sems.at[1])
    small.start()
    small.wait()
    main.wait()


def local(pixels, ivar, mask, psf_left, psf_right, sky_index):
    turned = [jnp.transpose(v, (0, 2, 1, 3)) for v in (pixels, ivar, mask, psf_left, psf_right)]
    field = (EXPO, ROWS, PAIR, F)
    specs = lax.axis_size("spec")
    hbm, vmem = pl.BlockSpec(memory_space=pltpu.HBM), pl.BlockSpec(memory_space=pltpu.VMEM)
    dma = pltpu.SemaphoreType.DMA
    groups = EXPO // GROUP
    edge = (2, groups, PARTS, GROUP, PAIR, F)
    cleaned, model = pl.pallas_call(
        main_kernel,
        out_shape=(
            jax.ShapeDtypeStruct(field, f32),
            jax.ShapeDtypeStruct((EXPO, 128), f32),
        ),
        in_specs=[hbm] * 6,
        out_specs=(vmem, vmem),
        scratch_shapes=[
            pltpu.VMEM(field, f32),
            pltpu.VMEM(field, f32),
            pltpu.VMEM(field, jnp.int32),
            pltpu.VMEM((2,) + field, f32),
            pltpu.SMEM(sky_index.shape, jnp.int32),
            pltpu.VMEM(field, f32),
            pltpu.VMEM(field, f32),
            pltpu.VMEM(field, f32),
            pltpu.VMEM((EXPO, ROWS + 1, PAIR, F), f32),
            pltpu.VMEM(edge, f32),
            pltpu.VMEM(edge, f32),
            pltpu.VMEM((groups, 2, GROUP * PAIR, 128), f32),
            pltpu.VMEM((groups, specs - 1, 2, GROUP * PAIR, 128), f32),
            pltpu.VMEM((groups, GROUP, 128), f32),
            pltpu.SMEM((groups, GROUP, 128), f32),
            pltpu.VMEM((EXPO, PAIR, LOAD), f32),
            pltpu.VMEM((PLANE - 1, PAIR, LOAD), f32),
            pltpu.VMEM((PAIR, LOAD), f32),
            pltpu.VMEM((LINE - 1, PAIR, LOAD), f32),
            pltpu.VMEM((2, PAIR, WIDE), f32),
            pltpu.VMEM((EXPO, 2, PAIR, WIDE), f32),
            dma((2 + groups, 5)),
            dma,
            dma((2, groups)),
            dma((2, groups)),
            dma((groups, specs - 1)),
            dma((groups, specs - 1)),
            dma,
            dma,
            dma,
            dma,
            dma,
            dma,
            dma,
            pltpu.SemaphoreType.REGULAR,
            pltpu.SemaphoreType.REGULAR,
        ],
        compiler_params=pltpu.CompilerParams(
            collective_id=0, has_side_effects=True, vmem_limit_bytes=54_000_000
        ),
        name="deconvolve",
    )(*turned, pltpu.with_memory_space_constraint(sky_index, pltpu.HBM))
    cleaned, model = pl.pallas_call(
        store_kernel,
        out_shape=(jax.ShapeDtypeStruct(field, f32), jax.ShapeDtypeStruct((EXPO, ROWS), f32)),
        in_specs=[vmem, vmem],
        out_specs=(hbm, hbm),
        scratch_shapes=[pltpu.VMEM((EXPO, ROWS), f32), dma((2,))],
        compiler_params=pltpu.CompilerParams(vmem_limit_bytes=54_000_000),
        name="store",
    )(cleaned, model)
    return (jnp.transpose(cleaned, (0, 2, 1, 3)), model)


def solution(mesh):
    in_specs = (
        P(None, "spec", "wave", None),
        P(None, "spec", "wave", None),
        P(None, "spec", "wave", None),
        P(None, "spec", "wave", None),
        P(None, "spec", "wave", None),
        P("spec", None),
    )
    out_specs = (P(None, "spec", "wave", None), P(None, "wave"))
    return jax.shard_map(local, mesh=mesh, in_specs=in_specs, out_specs=out_specs, check_vma=False)
```

```python
import jax
import jax.numpy as jnp
from jax import lax
from jax.experimental import pallas as pl
from jax.experimental.pallas import tpu as pltpu
from jax.sharding import PartitionSpec as P

F = 500
WIDE = 512
EXPO = 8
PAIR = 2
ROWS = 50
EDGE = 4
REG = 0.05
RIDGE = 1.0
MESH = pl.DeviceIdType.MESH

LINE = 8
CORES = 2
PLANE = 8
GROUP = 4
PARTS = 6
LOAD = 2 * WIDE
TILE = WIDE - 128
SPARE = F - TILE
FAR_FIRST = (4, 3, 5, 2, 6, 1, 7)

f32 = jnp.float32


def absorb(front, weight, outer, inner, pixel):
    a, b, d, ra, rb = front
    w_outer, w_inner, w_pixel = weight * outer, weight * inner, weight * pixel
    outer_square, inner_square = w_outer * outer, w_inner * inner
    own = weight + REG
    a = a + outer_square
    b = b + w_outer
    far = w_outer * inner
    d = d + own
    ra = ra + outer * w_pixel
    rb = rb + w_pixel
    inverse = 1.0 / a
    near_factor, far_factor, start = b * inverse, far * inverse, ra * inverse
    front = (
        d - near_factor * b,
        w_inner - near_factor * far,
        inner_square - far_factor * far,
        rb - b * start,
        inner * w_pixel - far * start,
    )
    return front, (near_factor, far_factor, start), outer_square, inner_square, own


def main_kernel(
    px_hbm, iv_hbm, mk_hbm, lf_hbm, rt_hbm, index_hbm,
    flux, model_ref,
    px, iv, mk, lr, index, near, far, start, prec,
    out_edge, in_edge, sums, boxes, model_v, model_s, load, box_a, part, box_b, piece, slope_ref,
    load_sem, index_sem, edge_send, edge_recv, spec_send, spec_recv, smem_sem,
    a_send, a_recv, b_send, b_recv, c_send, c_recv, known_one, known_two,
):
    me = lax.axis_index("wave")
    count = lax.axis_size("wave")
    spec = lax.axis_index("spec")
    specs = lax.axis_size("spec")
    core = lax.rem(me, CORES)
    col = lax.rem(lax.div(me, CORES), LINE)
    row = lax.div(me, CORES * LINE)
    mem = row * CORES + core

    def plane_peer(d):
        other = lax.rem(mem + d, PLANE)
        return other, (lax.div(other, CORES) * LINE + col) * CORES + lax.rem(other, CORES)

    def line_peer(d):
        return (row * LINE + lax.rem(col + d, LINE)) * CORES + core

    partner = me + 1 - 2 * core
    outside = lax.rem(me + 2 * core - 1 + count, count)

    def send(src, dst, send_sem, recv_sem, where):
        return pltpu.make_async_remote_copy(
            src_ref=src, dst_ref=dst, send_sem=send_sem, recv_sem=recv_sem, device_id=where, device_id_type=MESH
        )

    hbm = (iv_hbm, mk_hbm, lf_hbm, rt_hbm, px_hbm)
    vmem = (iv, mk, lr.at[0], lr.at[1], px)
    spans = (pl.ds((ROWS - EDGE) * core, EDGE), pl.ds((ROWS - EDGE) * (1 - core), EDGE), pl.ds(EDGE, ROWS - 2 * EDGE))
    everything = pl.ds(0, EXPO)
    cuts = [(everything, span) for span in spans[:2]] + [(pl.ds(g * GROUP, GROUP), spans[2]) for g in range(EXPO // GROUP)]
    loads = [
        [pltpu.make_async_copy(h.at[cut], v.at[cut], load_sem.at[i, j]) for j, (h, v) in enumerate(zip(hbm, vmem))]
        for i, cut in enumerate(cuts)
    ]

    barrier = pltpu.get_barrier_semaphore()

    def greet(peers):
        for peer in peers:
            pl.semaphore_signal(barrier, inc=1, device_id=peer, device_id_type=MESH)
        return len(peers)

    for copy in loads[0]:
        copy.start()
    greeted = greet([{"wave": outside}, {"wave": partner}])
    for group in loads[1:3]:
        for copy in group:
            copy.start()
    greeted += greet([{"wave": plane_peer(d)[1]} for d in FAR_FIRST])
    greeted += greet([{"spec": lax.rem(spec + d, specs)} for d in (2, 1, 3)])
    greeted += greet([{"wave": line_peer(1)}, {"wave": line_peer(LINE - 1)}])

    def weight_of(es, n):
        return jnp.where(mk[es, n] == 0, iv[es, n], 0.0)

    sides = ((46 - 43 * core, 1 - 2 * core, core, partner), (3 + 43 * core, 2 * core - 1, 1 - core, outside))

    def reduce_edge(side, g):
        base, step, outer, _ = sides[side]
        es = pl.ds(g * GROUP, GROUP)
        weight, inner = weight_of(es, base), lr[1 - outer, es, base]
        w_inner, w_pixel = weight * inner, weight * px[es, base]
        front = (weight + REG, w_inner, w_inner * inner, w_pixel, inner * w_pixel)
        for i in range(1, EDGE):
            n = base + step * i
            front, _, _, inner_square, _ = absorb(front, weight_of(es, n), lr[outer, es, n], lr[1 - outer, es, n], px[es, n])
        for i, value in enumerate(front + (inner_square,)):
            out_edge[side, g, i] = value

    edges = {}

    def hand_over(side, g):
        copy = send(
            out_edge.at[side, g], in_edge.at[side, g], edge_send.at[side, g], edge_recv.at[side, g],
            {"wave": sides[side][3]},
        )
        copy.start()
        edges[side, g] = copy

    for copy in loads[0]:
        copy.wait()
    reduce_edge(1, 0)
    pl.semaphore_wait(barrier, greeted)
    hand_over(1, 0)
    for copy in loads[1]:
        copy.wait()
    for side, g in ((0, 0), (1, 1), (0, 1)):
        reduce_edge(side, g)
        hand_over(side, g)
    for copy in loads[3]:
        copy.start()
    index_copy = pltpu.make_async_copy(index_hbm, index, index_sem)
    index_copy.start()
    for d in (1, LINE - 1):
        pl.semaphore_signal(known_one, inc=1, device_id={"wave": line_peer(d)}, device_id_type=MESH)
    fibre = lax.broadcasted_iota(jnp.int32, (PAIR, F), 1)
    index_copy.wait()
    second_row = lax.broadcasted_iota(jnp.int32, (PAIR, F), 0) == 1
    is_sky = jnp.zeros((PAIR, F), f32)
    for j in range(index.shape[1]):
        is_sky = is_sky + jnp.where(fibre == jnp.where(second_row, index[1, j], index[0, j]), 1.0, 0.0)
    is_sky = is_sky[None]

    lane8 = lax.broadcasted_iota(jnp.int32, (GROUP * PAIR, 128), 1)
    zero8 = jnp.zeros((GROUP * PAIR, 128), f32)

    def fold(value):
        return jnp.sum(value.reshape(GROUP * PAIR, F), axis=1, keepdims=True)

    first_row, row_step = (ROWS - 1) * (1 - core), 2 * core - 1
    fronts = []
    for g in range(EXPO // GROUP):
        es = pl.ds(g * GROUP, GROUP)
        for copy in loads[2 + g]:
            copy.wait()
        edges[0, g].wait_recv()
        a, b, d, ra, rb, last_square = (in_edge[0, g, i] for i in range(PARTS))

        def forward(k, carry, es=es):
            front, partial, last_square = carry
            n = first_row + row_step * k
            weight = weight_of(es, n)
            front, factors, outer_square, inner_square, own = absorb(
                front, weight, lr[1 - core, es, n], lr[core, es, n], px[es, n]
            )
            prec[es, k] = partial + outer_square
            near[es, k], far[es, k], start[es, k] = factors
            return front, own + last_square, inner_square

        front, partial, _ = lax.fori_loop(
            0, ROWS, forward, ((a, b, d, ra, rb), jnp.zeros_like(a), last_square), unroll=5
        )
        fronts.append((front, partial))

    pl.semaphore_wait(known_one, 2)
    for d in (2, LINE - 2):
        pl.semaphore_signal(known_two, inc=1, device_id={"wave": line_peer(d)}, device_id_type=MESH)
    alone = (me == 0) | (me == count - 1)
    sky_copies = []
    for g in range(EXPO // GROUP):
        es = pl.ds(g * GROUP, GROUP)
        edges[1, g].wait_recv()
        a2, b2, d2, ra2, rb2, next_square = (
            jnp.where(alone, 0.0 if i else REG, in_edge[1, g, i]) for i in range(PARTS)
        )
        (a, b, d, ra, rb), partial = fronts[g]
        prec[es, ROWS] = partial + next_square
        b = b + b2
        inverse = 1.0 / (a + d2)
        factor, base = b * inverse, (ra + rb2) * inverse
        beyond = (rb + ra2 - b * base) / (d + a2 - factor * b)
        edge_flux = base - factor * beyond
        flux[es, first_row + row_step * (ROWS - 1)] = edge_flux

        def backward(i, carry, es=es):
            next_one, next_two = carry
            k = ROWS - 1 - i
            value = start[es, k] - near[es, k] * next_one - far[es, k] * next_two
            flux[es, first_row + row_step * (k - 1)] = value
            return value, next_one

        lax.fori_loop(0, ROWS - 1, backward, (edge_flux, beyond), unroll=7)

        def sky_row(k, carry, es=es):
            top, bottom = carry
            n = first_row + row_step * k
            share = prec[es, k + 1] * is_sky
            scaled = share * flux[es, n]
            return jnp.where(lane8 == n, fold(scaled), top), jnp.where(lane8 == n, fold(share), bottom)

        sums[g, 0], sums[g, 1] = lax.fori_loop(0, ROWS, sky_row, (zero8, zero8), unroll=50)
        sky_copies.append(
            [
                send(
                    sums.at[g], boxes.at[g, specs - 1 - d], spec_send.at[g, d - 1], spec_recv.at[g, specs - 1 - d],
                    {"spec": lax.rem(spec + d, specs)},
                )
                for d in (2, 1, 3)
            ]
        )
        for copy in sky_copies[g]:
            copy.start()

    scale = 2.0 / (count * ROWS - 1)
    base_row = me * ROWS
    lane2 = lax.broadcasted_iota(jnp.int32, (PAIR, 128), 1)
    used = lax.broadcasted_iota(jnp.int32, (GROUP, 128), 1) < ROWS
    zero = jnp.zeros((PAIR, F), f32)
    zero_moment = jnp.zeros((PAIR, 128), f32)
    for g in range(EXPO // GROUP):
        for copy in sky_copies[g]:
            copy.wait_recv()
        held = [sums[g]] + [boxes[g, k] for k in range(specs - 1)]
        total = None
        for s in range(specs):
            place = lax.rem(s - spec + specs, specs)
            term = held[0]
            for k in range(1, specs):
                term = jnp.where(place == k, held[k], term)
            total = term if total is None else total + term
        total = total.reshape(2, GROUP, PAIR, 128).sum(2)
        model = jnp.where(used, total[0], 0.0) / jnp.where(used, total[1], 1.0)
        model_v[g] = model
        to_scalar = pltpu.make_async_copy(model_v.at[g], model_s.at[g], smem_sem)
        to_scalar.start()
        model_ref[g * GROUP : (g + 1) * GROUP] = model
        to_scalar.wait()

        def regress(n, carry, g=g):
            first, second, moment = (list(v) for v in carry)
            place = (base_row + n).astype(f32) * scale - 1.0
            powers = jnp.where(lane2 == SPARE, 1.0, jnp.where(lane2 == SPARE + 1, place, place * place))
            for i in range(GROUP):
                sky = model_s[g, i, n]
                term = flux[g * GROUP + i, n] * sky
                first[i] = first[i] + term
                second[i] = second[i] + term * place
                moment[i] = moment[i] + powers * (sky * sky)
            return tuple(first), tuple(second), tuple(moment)

        first, second, moment = lax.fori_loop(
            0, ROWS, regress, ((zero,) * GROUP, (zero,) * GROUP, (zero_moment,) * GROUP), unroll=5
        )
        for i in range(GROUP):
            e = g * GROUP + i
            load[e, :, 0:F] = first[i]
            load[e, :, WIDE : WIDE + F] = second[i]
            load[e, :, TILE:WIDE] = jnp.where(lane2 < SPARE, load[e, :, TILE:WIDE], moment[i])
        for d in FAR_FIRST:
            other, where = plane_peer(d)

            @pl.when(lax.div(other, GROUP) == g)
            def _(d=d, other=other, where=where):
                send(load.at[other], box_a.at[PLANE - 1 - d], a_send, a_recv, {"wave": where}).start()

    whole_a = send(box_a, box_a, a_send, a_recv, {"wave": partner})
    whole_a.wait_recv()
    pl.semaphore_wait(known_two, 2)
    acc = load[mem]
    for k in range(PLANE - 1):
        acc = acc + box_a[k]
    part[...] = acc
    for d in FAR_FIRST:
        send(part, box_b.at[LINE - 1 - d], b_send, b_recv, {"wave": line_peer(d)}).start()
    whole_b = send(box_b, box_b, b_send, b_recv, {"wave": partner})
    whole_b.wait_recv()
    for k in range(LINE - 1):
        acc = acc + box_b[k]
    first_sum, second_sum, powers_sum = acc[:, :WIDE], acc[:, WIDE:LOAD], acc[:, TILE:WIDE]

    def pick(i):
        return jnp.sum(jnp.where(lane2 == SPARE + i, powers_sum, 0.0), axis=1, keepdims=True)

    upper, cross, lower = pick(0) + RIDGE, pick(1), pick(2) + RIDGE
    inverse = 1.0 / (upper * lower - cross * cross)
    piece[0] = (lower * first_sum - cross * second_sum) * inverse
    piece[1] = (upper * second_sum - cross * first_sum) * inverse
    slope_ref[mem] = piece[...]
    for d in FAR_FIRST:
        send(piece, slope_ref.at[mem], c_send, c_recv, {"wave": plane_peer(d)[1]}).start()
    whole_c = send(slope_ref.at[pl.ds(0, PLANE - 1)], slope_ref.at[pl.ds(0, PLANE - 1)], c_send, c_recv, {"wave": partner})
    whole_c.wait_recv()

    slope_a = [slope_ref[e, 0, :, 0:F] for e in range(EXPO)]
    slope_b = [slope_ref[e, 1, :, 0:F] for e in range(EXPO)]

    def clean(n, carry):
        place = (base_row + n).astype(f32) * scale - 1.0
        for e in range(EXPO):
            fitted = slope_a[e] + slope_b[e] * place
            flux[e, n] = flux[e, n] - fitted * model_s[e // GROUP, e % GROUP, n]
        return carry

    lax.fori_loop(0, ROWS, clean, 0, unroll=5)
    for copy in list(edges.values()) + sky_copies[0] + sky_copies[1]:
        copy.wait_send()
    whole_a.wait_send()
    whole_b.wait_send()
    whole_c.wait_send()


def store_kernel(cleaned, model, cleaned_out, model_out, model_rows, sems):
    main = pltpu.make_async_copy(cleaned, cleaned_out, sems.at[0])
    main.start()
    model_rows[...] = model[:, 0:ROWS]
    small = pltpu.make_async_copy(model_rows, model_out, sems.at[1])
    small.start()
    small.wait()
    main.wait()


def local(pixels, ivar, mask, psf_left, psf_right, sky_index):
    turned = [jnp.transpose(v, (0, 2, 1, 3)) for v in (pixels, ivar, mask, psf_left, psf_right)]
    field = (EXPO, ROWS, PAIR, F)
    specs = lax.axis_size("spec")
    hbm, vmem = pl.BlockSpec(memory_space=pltpu.HBM), pl.BlockSpec(memory_space=pltpu.VMEM)
    dma = pltpu.SemaphoreType.DMA
    groups = EXPO // GROUP
    edge = (2, groups, PARTS, GROUP, PAIR, F)
    cleaned, model = pl.pallas_call(
        main_kernel,
        out_shape=(
            jax.ShapeDtypeStruct(field, f32),
            jax.ShapeDtypeStruct((EXPO, 128), f32),
        ),
        in_specs=[hbm] * 6,
        out_specs=(vmem, vmem),
        scratch_shapes=[
            pltpu.VMEM(field, f32),
            pltpu.VMEM(field, f32),
            pltpu.VMEM(field, jnp.int32),
            pltpu.VMEM((2,) + field, f32),
            pltpu.SMEM(sky_index.shape, jnp.int32),
            pltpu.VMEM(field, f32),
            pltpu.VMEM(field, f32),
            pltpu.VMEM(field, f32),
            pltpu.VMEM((EXPO, ROWS + 1, PAIR, F), f32),
            pltpu.VMEM(edge, f32),
            pltpu.VMEM(edge, f32),
            pltpu.VMEM((groups, 2, GROUP * PAIR, 128), f32),
            pltpu.VMEM((groups, specs - 1, 2, GROUP * PAIR, 128), f32),
            pltpu.VMEM((groups, GROUP, 128), f32),
            pltpu.SMEM((groups, GROUP, 128), f32),
            pltpu.VMEM((EXPO, PAIR, LOAD), f32),
            pltpu.VMEM((PLANE - 1, PAIR, LOAD), f32),
            pltpu.VMEM((PAIR, LOAD), f32),
            pltpu.VMEM((LINE - 1, PAIR, LOAD), f32),
            pltpu.VMEM((2, PAIR, WIDE), f32),
            pltpu.VMEM((EXPO, 2, PAIR, WIDE), f32),
            dma((2 + groups, 5)),
            dma,
            dma((2, groups)),
            dma((2, groups)),
            dma((groups, specs - 1)),
            dma((groups, specs - 1)),
            dma,
            dma,
            dma,
            dma,
            dma,
            dma,
            dma,
            pltpu.SemaphoreType.REGULAR,
            pltpu.SemaphoreType.REGULAR,
        ],
        compiler_params=pltpu.CompilerParams(
            collective_id=0, has_side_effects=True, vmem_limit_bytes=54_000_000
        ),
        name="deconvolve",
    )(*turned, pltpu.with_memory_space_constraint(sky_index, pltpu.HBM))
    cleaned, model = pl.pallas_call(
        store_kernel,
        out_shape=(jax.ShapeDtypeStruct(field, f32), jax.ShapeDtypeStruct((EXPO, ROWS), f32)),
        in_specs=[vmem, vmem],
        out_specs=(hbm, hbm),
        scratch_shapes=[pltpu.VMEM((EXPO, ROWS), f32), dma((2,))],
        compiler_params=pltpu.CompilerParams(vmem_limit_bytes=54_000_000),
        name="store",
    )(cleaned, model)
    return (jnp.transpose(cleaned, (0, 2, 1, 3)), model)


def solution(mesh):
    in_specs = (
        P(None, "spec", "wave", None),
        P(None, "spec", "wave", None),
        P(None, "spec", "wave", None),
        P(None, "spec", "wave", None),
        P(None, "spec", "wave", None),
        P("spec", None),
    )
    out_specs = (P(None, "spec", "wave", None), P(None, "wave"))
    return jax.shard_map(local, mesh=mesh, in_specs=in_specs, out_specs=out_specs, check_vma=False)
```

```python
import jax
import jax.numpy as jnp
from jax import lax
from jax.experimental import pallas as pl
from jax.experimental.pallas import tpu as pltpu
from jax.sharding import PartitionSpec as P

F = 500
WIDE = 512
EXPO = 8
PAIR = 2
ROWS = 50
EDGE = 4
REG = 0.05
RIDGE = 1.0
MESH = pl.DeviceIdType.MESH

LINE = 8
CORES = 2
PLANE = 8
GROUP = 4
PARTS = 6
LOAD = 2 * WIDE
TILE = WIDE - 128
SPARE = F - TILE
FAR_FIRST = (4, 3, 5, 2, 6, 1, 7)

f32 = jnp.float32


def absorb(front, weight, outer, inner, pixel):
    a, b, d, ra, rb = front
    w_outer, w_inner, w_pixel = weight * outer, weight * inner, weight * pixel
    outer_square, inner_square = w_outer * outer, w_inner * inner
    own = weight + REG
    a = a + outer_square
    b = b + w_outer
    far = w_outer * inner
    d = d + own
    ra = ra + outer * w_pixel
    rb = rb + w_pixel
    inverse = 1.0 / a
    near_factor, far_factor, start = b * inverse, far * inverse, ra * inverse
    front = (
        d - near_factor * b,
        w_inner - near_factor * far,
        inner_square - far_factor * far,
        rb - b * start,
        inner * w_pixel - far * start,
    )
    return front, (near_factor, far_factor, start), outer_square, inner_square, own


def main_kernel(
    px_hbm, iv_hbm, mk_hbm, lf_hbm, rt_hbm, index_hbm,
    flux, model_ref,
    px, iv, mk, lr, index, near, far, start, prec,
    out_edge, in_edge, sums, boxes, model_v, model_s, load, box_a, part, box_b, piece, slope_ref,
    load_sem, index_sem, edge_send, edge_recv, spec_send, spec_recv, smem_sem,
    a_send, a_recv, b_send, b_recv, c_send, c_recv, known_one, known_two,
):
    me = lax.axis_index("wave")
    count = lax.axis_size("wave")
    spec = lax.axis_index("spec")
    specs = lax.axis_size("spec")
    core = lax.rem(me, CORES)
    col = lax.rem(lax.div(me, CORES), LINE)
    row = lax.div(me, CORES * LINE)
    mem = row * CORES + core

    def plane_peer(d):
        other = lax.rem(mem + d, PLANE)
        return other, (lax.div(other, CORES) * LINE + col) * CORES + lax.rem(other, CORES)

    def line_peer(d):
        return (row * LINE + lax.rem(col + d, LINE)) * CORES + core

    partner = me + 1 - 2 * core
    outside = lax.rem(me + 2 * core - 1 + count, count)

    def send(src, dst, send_sem, recv_sem, where):
        return pltpu.make_async_remote_copy(
            src_ref=src, dst_ref=dst, send_sem=send_sem, recv_sem=recv_sem, device_id=where, device_id_type=MESH
        )

    hbm = (iv_hbm, mk_hbm, lf_hbm, rt_hbm, px_hbm)
    vmem = (iv, mk, lr.at[0], lr.at[1], px)
    spans = (pl.ds((ROWS - EDGE) * core, EDGE), pl.ds((ROWS - EDGE) * (1 - core), EDGE), pl.ds(EDGE, ROWS - 2 * EDGE))
    everything = pl.ds(0, EXPO)
    cuts = [(everything, span) for span in spans[:2]] + [(pl.ds(g * GROUP, GROUP), spans[2]) for g in range(EXPO // GROUP)]
    loads = [
        [pltpu.make_async_copy(h.at[cut], v.at[cut], load_sem.at[i, j]) for j, (h, v) in enumerate(zip(hbm, vmem))]
        for i, cut in enumerate(cuts)
    ]

    barrier = pltpu.get_barrier_semaphore()

    def greet(peers):
        for peer in peers:
            pl.semaphore_signal(barrier, inc=1, device_id=peer, device_id_type=MESH)
        return len(peers)

    for copy in loads[0]:
        copy.start()
    greeted = greet([{"wave": outside}, {"wave": partner}])
    for group in loads[1:3]:
        for copy in group:
            copy.start()
    greeted += greet([{"wave": plane_peer(d)[1]} for d in FAR_FIRST])
    greeted += greet([{"spec": lax.rem(spec + d, specs)} for d in (2, 1, 3)])
    greeted += greet([{"wave": line_peer(1)}, {"wave": line_peer(LINE - 1)}])

    def weight_of(es, n):
        return jnp.where(mk[es, n] == 0, iv[es, n], 0.0)

    sides = ((46 - 43 * core, 1 - 2 * core, core, partner), (3 + 43 * core, 2 * core - 1, 1 - core, outside))

    def reduce_edge(side, g):
        base, step, outer, _ = sides[side]
        es = pl.ds(g * GROUP, GROUP)
        weight, inner = weight_of(es, base), lr[1 - outer, es, base]
        w_inner, w_pixel = weight * inner, weight * px[es, base]
        front = (weight + REG, w_inner, w_inner * inner, w_pixel, inner * w_pixel)
        for i in range(1, EDGE):
            n = base + step * i
            front, _, _, inner_square, _ = absorb(front, weight_of(es, n), lr[outer, es, n], lr[1 - outer, es, n], px[es, n])
        for i, value in enumerate(front + (inner_square,)):
            out_edge[side, g, i] = value

    edges = {}

    def hand_over(side, g):
        copy = send(
            out_edge.at[side, g], in_edge.at[side, g], edge_send.at[side, g], edge_recv.at[side, g],
            {"wave": sides[side][3]},
        )
        copy.start()
        edges[side, g] = copy

    for copy in loads[0]:
        copy.wait()
    reduce_edge(1, 0)
    pl.semaphore_wait(barrier, greeted)
    hand_over(1, 0)
    for copy in loads[1]:
        copy.wait()
    for side, g in ((0, 0), (1, 1), (0, 1)):
        reduce_edge(side, g)
        hand_over(side, g)
    for copy in loads[3]:
        copy.start()
    index_copy = pltpu.make_async_copy(index_hbm, index, index_sem)
    index_copy.start()
    for d in (1, LINE - 1):
        pl.semaphore_signal(known_one, inc=1, device_id={"wave": line_peer(d)}, device_id_type=MESH)
    fibre = lax.broadcasted_iota(jnp.int32, (PAIR, F), 1)
    index_copy.wait()
    second_row = lax.broadcasted_iota(jnp.int32, (PAIR, F), 0) == 1
    is_sky = jnp.zeros((PAIR, F), f32)
    for j in range(index.shape[1]):
        is_sky = is_sky + jnp.where(fibre == jnp.where(second_row, index[1, j], index[0, j]), 1.0, 0.0)
    is_sky = is_sky[None]

    lane8 = lax.broadcasted_iota(jnp.int32, (GROUP * PAIR, 128), 1)
    zero8 = jnp.zeros((GROUP * PAIR, 128), f32)

    def fold(value):
        return jnp.sum(value.reshape(GROUP * PAIR, F), axis=1, keepdims=True)

    first_row, row_step = (ROWS - 1) * (1 - core), 2 * core - 1
    fronts = []
    for g in range(EXPO // GROUP):
        es = pl.ds(g * GROUP, GROUP)
        for copy in loads[2 + g]:
            copy.wait()
        edges[0, g].wait_recv()
        a, b, d, ra, rb, last_square = (in_edge[0, g, i] for i in range(PARTS))

        def forward(k, carry, es=es):
            front, partial, last_square = carry
            n = first_row + row_step * k
            weight = weight_of(es, n)
            front, factors, outer_square, inner_square, own = absorb(
                front, weight, lr[1 - core, es, n], lr[core, es, n], px[es, n]
            )
            prec[es, k] = partial + outer_square
            near[es, k], far[es, k], start[es, k] = factors
            return front, own + last_square, inner_square

        front, partial, _ = lax.fori_loop(
            0, ROWS, forward, ((a, b, d, ra, rb), jnp.zeros_like(a), last_square), unroll=5
        )
        fronts.append((front, partial))

    pl.semaphore_wait(known_one, 2)
    for d in (2, LINE - 2):
        pl.semaphore_signal(known_two, inc=1, device_id={"wave": line_peer(d)}, device_id_type=MESH)
    alone = (me == 0) | (me == count - 1)
    sky_copies = []
    for g in range(EXPO // GROUP):
        es = pl.ds(g * GROUP, GROUP)
        edges[1, g].wait_recv()
        a2, b2, d2, ra2, rb2, next_square = (
            jnp.where(alone, 0.0 if i else REG, in_edge[1, g, i]) for i in range(PARTS)
        )
        (a, b, d, ra, rb), partial = fronts[g]
        prec[es, ROWS] = partial + next_square
        b = b + b2
        inverse = 1.0 / (a + d2)
        factor, base = b * inverse, (ra + rb2) * inverse
        beyond = (rb + ra2 - b * base) / (d + a2 - factor * b)
        edge_flux = base - factor * beyond
        flux[es, first_row + row_step * (ROWS - 1)] = edge_flux

        def backward(i, carry, es=es):
            next_one, next_two = carry
            k = ROWS - 1 - i
            value = start[es, k] - near[es, k] * next_one - far[es, k] * next_two
            flux[es, first_row + row_step * (k - 1)] = value
            return value, next_one

        lax.fori_loop(0, ROWS - 1, backward, (edge_flux, beyond), unroll=49)

        def sky_row(k, carry, es=es):
            top, bottom = carry
            n = first_row + row_step * k
            share = prec[es, k + 1] * is_sky
            scaled = share * flux[es, n]
            return jnp.where(lane8 == n, fold(scaled), top), jnp.where(lane8 == n, fold(share), bottom)

        sums[g, 0], sums[g, 1] = lax.fori_loop(0, ROWS, sky_row, (zero8, zero8), unroll=50)
        sky_copies.append(
            [
                send(
                    sums.at[g], boxes.at[g, specs - 1 - d], spec_send.at[g, d - 1], spec_recv.at[g, specs - 1 - d],
                    {"spec": lax.rem(spec + d, specs)},
                )
                for d in (2, 1, 3)
            ]
        )
        for copy in sky_copies[g]:
            copy.start()

    scale = 2.0 / (count * ROWS - 1)
    base_row = me * ROWS
    lane2 = lax.broadcasted_iota(jnp.int32, (PAIR, 128), 1)
    used = lax.broadcasted_iota(jnp.int32, (GROUP, 128), 1) < ROWS
    zero = jnp.zeros((PAIR, F), f32)
    zero_moment = jnp.zeros((PAIR, 128), f32)
    for g in range(EXPO // GROUP):
        for copy in sky_copies[g]:
            copy.wait_recv()
        held = [sums[g]] + [boxes[g, k] for k in range(specs - 1)]
        total = None
        for s in range(specs):
            place = lax.rem(s - spec + specs, specs)
            term = held[0]
            for k in range(1, specs):
                term = jnp.where(place == k, held[k], term)
            total = term if total is None else total + term
        total = total.reshape(2, GROUP, PAIR, 128).sum(2)
        model = jnp.where(used, total[0], 0.0) / jnp.where(used, total[1], 1.0)
        model_v[g] = model
        to_scalar = pltpu.make_async_copy(model_v.at[g], model_s.at[g], smem_sem)
        to_scalar.start()
        model_ref[g * GROUP : (g + 1) * GROUP] = model
        to_scalar.wait()

        def regress(n, carry, g=g):
            first, second, moment = (list(v) for v in carry)
            place = (base_row + n).astype(f32) * scale - 1.0
            powers = jnp.where(lane2 == SPARE, 1.0, jnp.where(lane2 == SPARE + 1, place, place * place))
            for i in range(GROUP):
                sky = model_s[g, i, n]
                term = flux[g * GROUP + i, n] * sky
                first[i] = first[i] + term
                second[i] = second[i] + term * place
                moment[i] = moment[i] + powers * (sky * sky)
            return tuple(first), tuple(second), tuple(moment)

        first, second, moment = lax.fori_loop(
            0, ROWS, regress, ((zero,) * GROUP, (zero,) * GROUP, (zero_moment,) * GROUP), unroll=10
        )
        for i in range(GROUP):
            e = g * GROUP + i
            load[e, :, 0:F] = first[i]
            load[e, :, WIDE : WIDE + F] = second[i]
            load[e, :, TILE:WIDE] = jnp.where(lane2 < SPARE, load[e, :, TILE:WIDE], moment[i])
        for d in FAR_FIRST:
            other, where = plane_peer(d)

            @pl.when(lax.div(other, GROUP) == g)
            def _(d=d, other=other, where=where):
                send(load.at[other], box_a.at[PLANE - 1 - d], a_send, a_recv, {"wave": where}).start()

    whole_a = send(box_a, box_a, a_send, a_recv, {"wave": partner})
    whole_a.wait_recv()
    pl.semaphore_wait(known_two, 2)
    acc = load[mem]
    for k in range(PLANE - 1):
        acc = acc + box_a[k]
    part[...] = acc
    for d in FAR_FIRST:
        send(part, box_b.at[LINE - 1 - d], b_send, b_recv, {"wave": line_peer(d)}).start()
    whole_b = send(box_b, box_b, b_send, b_recv, {"wave": partner})
    whole_b.wait_recv()
    for k in range(LINE - 1):
        acc = acc + box_b[k]
    first_sum, second_sum, powers_sum = acc[:, :WIDE], acc[:, WIDE:LOAD], acc[:, TILE:WIDE]

    def pick(i):
        return jnp.sum(jnp.where(lane2 == SPARE + i, powers_sum, 0.0), axis=1, keepdims=True)

    upper, cross, lower = pick(0) + RIDGE, pick(1), pick(2) + RIDGE
    inverse = 1.0 / (upper * lower - cross * cross)
    piece[0] = (lower * first_sum - cross * second_sum) * inverse
    piece[1] = (upper * second_sum - cross * first_sum) * inverse
    slope_ref[mem] = piece[...]
    for d in FAR_FIRST:
        send(piece, slope_ref.at[mem], c_send, c_recv, {"wave": plane_peer(d)[1]}).start()
    whole_c = send(slope_ref.at[pl.ds(0, PLANE - 1)], slope_ref.at[pl.ds(0, PLANE - 1)], c_send, c_recv, {"wave": partner})
    whole_c.wait_recv()

    slope_a = [slope_ref[e, 0, :, 0:F] for e in range(EXPO)]
    slope_b = [slope_ref[e, 1, :, 0:F] for e in range(EXPO)]

    def clean(n, carry):
        place = (base_row + n).astype(f32) * scale - 1.0
        for e in range(EXPO):
            fitted = slope_a[e] + slope_b[e] * place
            flux[e, n] = flux[e, n] - fitted * model_s[e // GROUP, e % GROUP, n]
        return carry

    lax.fori_loop(0, ROWS, clean, 0, unroll=10)
    for copy in list(edges.values()) + sky_copies[0] + sky_copies[1]:
        copy.wait_send()
    whole_a.wait_send()
    whole_b.wait_send()
    whole_c.wait_send()


def store_kernel(cleaned, model, cleaned_out, model_out, model_rows, sems):
    main = pltpu.make_async_copy(cleaned, cleaned_out, sems.at[0])
    main.start()
    model_rows[...] = model[:, 0:ROWS]
    small = pltpu.make_async_copy(model_rows, model_out, sems.at[1])
    small.start()
    small.wait()
    main.wait()


def local(pixels, ivar, mask, psf_left, psf_right, sky_index):
    turned = [jnp.transpose(v, (0, 2, 1, 3)) for v in (pixels, ivar, mask, psf_left, psf_right)]
    field = (EXPO, ROWS, PAIR, F)
    specs = lax.axis_size("spec")
    hbm, vmem = pl.BlockSpec(memory_space=pltpu.HBM), pl.BlockSpec(memory_space=pltpu.VMEM)
    dma = pltpu.SemaphoreType.DMA
    groups = EXPO // GROUP
    edge = (2, groups, PARTS, GROUP, PAIR, F)
    cleaned, model = pl.pallas_call(
        main_kernel,
        out_shape=(
            jax.ShapeDtypeStruct(field, f32),
            jax.ShapeDtypeStruct((EXPO, 128), f32),
        ),
        in_specs=[hbm] * 6,
        out_specs=(vmem, vmem),
        scratch_shapes=[
            pltpu.VMEM(field, f32),
            pltpu.VMEM(field, f32),
            pltpu.VMEM(field, jnp.int32),
            pltpu.VMEM((2,) + field, f32),
            pltpu.SMEM(sky_index.shape, jnp.int32),
            pltpu.VMEM(field, f32),
            pltpu.VMEM(field, f32),
            pltpu.VMEM(field, f32),
            pltpu.VMEM((EXPO, ROWS + 1, PAIR, F), f32),
            pltpu.VMEM(edge, f32),
            pltpu.VMEM(edge, f32),
            pltpu.VMEM((groups, 2, GROUP * PAIR, 128), f32),
            pltpu.VMEM((groups, specs - 1, 2, GROUP * PAIR, 128), f32),
            pltpu.VMEM((groups, GROUP, 128), f32),
            pltpu.SMEM((groups, GROUP, 128), f32),
            pltpu.VMEM((EXPO, PAIR, LOAD), f32),
            pltpu.VMEM((PLANE - 1, PAIR, LOAD), f32),
            pltpu.VMEM((PAIR, LOAD), f32),
            pltpu.VMEM((LINE - 1, PAIR, LOAD), f32),
            pltpu.VMEM((2, PAIR, WIDE), f32),
            pltpu.VMEM((EXPO, 2, PAIR, WIDE), f32),
            dma((2 + groups, 5)),
            dma,
            dma((2, groups)),
            dma((2, groups)),
            dma((groups, specs - 1)),
            dma((groups, specs - 1)),
            dma,
            dma,
            dma,
            dma,
            dma,
            dma,
            dma,
            pltpu.SemaphoreType.REGULAR,
            pltpu.SemaphoreType.REGULAR,
        ],
        compiler_params=pltpu.CompilerParams(
            collective_id=0, has_side_effects=True, vmem_limit_bytes=54_000_000
        ),
        name="deconvolve",
    )(*turned, pltpu.with_memory_space_constraint(sky_index, pltpu.HBM))
    cleaned, model = pl.pallas_call(
        store_kernel,
        out_shape=(jax.ShapeDtypeStruct(field, f32), jax.ShapeDtypeStruct((EXPO, ROWS), f32)),
        in_specs=[vmem, vmem],
        out_specs=(hbm, hbm),
        scratch_shapes=[pltpu.VMEM((EXPO, ROWS), f32), dma((2,))],
        compiler_params=pltpu.CompilerParams(vmem_limit_bytes=54_000_000),
        name="store",
    )(cleaned, model)
    return (jnp.transpose(cleaned, (0, 2, 1, 3)), model)


def solution(mesh):
    in_specs = (
        P(None, "spec", "wave", None),
        P(None, "spec", "wave", None),
        P(None, "spec", "wave", None),
        P(None, "spec", "wave", None),
        P(None, "spec", "wave", None),
        P("spec", None),
    )
    out_specs = (P(None, "spec", "wave", None), P(None, "wave"))
    return jax.shard_map(local, mesh=mesh, in_specs=in_specs, out_specs=out_specs, check_vma=False)
```
